32 devices in a mesh: seq: 16 (over z, y, x), head: 2 (over core).
Axes of the slice: x: 2, y: 2, z: 4, core: 2. Of those that a mesh axis runs over, the one named last changes fastest.
Arguments:
- win_query: bfloat16 [4096, 4096], P('seq', 'head'), may hold values from -24 to 24
- win_key: bfloat16 [4096, 4096], P('seq', 'head'), may hold values from -24 to 24
- win_value: bfloat16 [4096, 4096], P('seq', 'head'), may hold values from -24 to 24
- clu_query: bfloat16 [4096, 4096], P('seq', 'head'), may hold values from -24 to 24
- clu_key: bfloat16 [4096, 4096], P('seq', 'head'), may hold values from -24 to 24
- clu_value: bfloat16 [4096, 4096], P('seq', 'head'), may hold values from -24 to 24
- cluster_ids: int32 [32, 4096], P('head', 'seq'), may hold values from 0 to 63, as said below
- win_gain: float32 [4096], P('head'), may hold values from 0.5 to 1.5
- clu_gain: float32 [4096], P('head'), may hold values from 0.5 to 1.5
- win_out_grad: bfloat16 [4096, 4096], P('seq', 'head'), may hold values from -9 to 9
- clu_out_grad: bfloat16 [4096, 4096], P('seq', 'head'), may hold values from -9 to 9
Outputs:
- win_normed: bfloat16 [4096, 4096], P('seq', 'head')
- clu_normed: bfloat16 [4096, 4096], P('seq', 'head')
- win_dq: bfloat16 [4096, 4096], P('seq', 'head')
- win_dk: bfloat16 [4096, 4096], P('seq', 'head')
- win_dv: bfloat16 [4096, 4096], P('seq', 'head')
- clu_dq: bfloat16 [4096, 4096], P('seq', 'head')
- clu_dk: bfloat16 [4096, 4096], P('seq', 'head')
- clu_dv: bfloat16 [4096, 4096], P('seq', 'head')
The draws below stay inside these ranges and needn't reach their ends.
Inputs may be any that keep to these rules, and one draw needn't show every extreme that they name: `cluster_ids`: in every cluster head each cluster holds at most 8 of the tokens of each aligned block of 256 positions, hence at most 128 tokens in all; in every head one cluster holds exactly 8 tokens of every block.
All inputs are finite; a program needn't handle non-finite values.
Results may differ from the reference program's by a relative error of at most 0.035.
Values may be sent and summed in bfloat16 or wider, within the bound.
A program may use at most 192 MiB of HBM per device.

```python
import jax
import jax.numpy as jnp
from jax import lax

HW = 32
HC = 32
DH = 128
WINDOW = 256
SLOTS = 128
TOK_DEV = 256
TOKENS = 4096
CAP = 8
CLUSTERS = 64


def base_field(key, layout):
    values = jax.random.truncated_normal(key, -6.0, 6.0, layout, jnp.float32)
    return values


def cluster_table(key):
    base_key = jax.random.fold_in(key, 11)
    n_blocks = TOKENS // TOK_DEV
    pool_size = CLUSTERS * CAP
    full_cluster = jax.random.randint(jax.random.fold_in(base_key, 1), (HC,), 0, CLUSTERS)
    key_list = jax.random.split(jax.random.fold_in(base_key, 2), HC * n_blocks)
    owners = jnp.repeat(full_cluster, n_blocks)

    def one_block(block_key, chosen):
        first_key = jax.random.fold_in(block_key, 1)
        second_key = jax.random.fold_in(block_key, 2)
        score_int = jax.random.permutation(first_key, pool_size).astype(jnp.int32)
        slot_ids = jnp.arange(pool_size, dtype=jnp.int32)
        score_int = jnp.where(slot_ids // CAP == chosen, -1 - slot_ids % CAP, score_int)
        order_rows = jnp.argsort(score_int, stable=True)[:TOK_DEV]
        return (jax.random.permutation(second_key, order_rows) // CAP).astype(jnp.int32)
    table_ids = jax.vmap(one_block)(key_list, owners)
    return table_ids.reshape(HC, TOKENS)


def window_pairs(key):
    queries = base_field(jax.random.fold_in(key, 31), (TOKENS, HW, DH))
    key_rows = base_field(jax.random.fold_in(key, 32), (TOKENS, HW, DH))
    return (queries.reshape(TOKENS, HW * DH), key_rows.reshape(TOKENS, HW * DH))


def cluster_pairs(key):
    queries = base_field(jax.random.fold_in(key, 21), (TOKENS, HC, DH))
    key_rows = base_field(jax.random.fold_in(key, 22), (TOKENS, HC, DH))
    return (queries.reshape(TOKENS, HC * DH), key_rows.reshape(TOKENS, HC * DH))


def shared_part(key, label, n_heads):
    return base_field(jax.random.fold_in(key, label + 10), (n_heads, DH))


def rising_values(key, label, n_heads):
    head_ramp = 1.0 + 2.0 * jnp.arange(n_heads, dtype=jnp.float32) / (n_heads - 1)
    common = shared_part(key, label, n_heads)
    values = base_field(jax.random.fold_in(key, label), (TOKENS, n_heads, DH)) + 0.15 * common[None]
    values = values * head_ramp[None, :, None]
    return values.reshape(TOKENS, n_heads * DH)


def leaning_grads(key, label, n_heads):
    common = shared_part(key, label, n_heads)
    noise_rows = base_field(jax.random.fold_in(key, label + 20), (TOKENS, n_heads, DH))
    grads = 0.6 * noise_rows + 0.8 * common[None]
    return grads.reshape(TOKENS, n_heads * DH)


def draw_win_query(key, part):
    return window_pairs(key)[0].astype(jnp.bfloat16)


def draw_win_key(key, part):
    return window_pairs(key)[1].astype(jnp.bfloat16)


def draw_win_value(key, part):
    return rising_values(key, 41, HW).astype(jnp.bfloat16)


def draw_clu_query(key, part):
    return cluster_pairs(key)[0].astype(jnp.bfloat16)


def draw_clu_key(key, part):
    return cluster_pairs(key)[1].astype(jnp.bfloat16)


def draw_clu_value(key, part):
    return rising_values(key, 42, HC).astype(jnp.bfloat16)


def draw_cluster_ids(key, part):
    return cluster_table(key)


def draw_win_out_grad(key, part):
    return leaning_grads(key, 41, HW).astype(jnp.bfloat16)


def draw_clu_out_grad(key, part):
    return leaning_grads(key, 42, HC).astype(jnp.bfloat16)


def setup_inputs(seed: int = 0) -> dict:
    streams_of = jax.random.split(jax.random.key(seed), 12)
    return {
        "win_query": draw_win_query(jax.random.fold_in(streams_of[11], 71), 0),
        "win_key": draw_win_key(jax.random.fold_in(streams_of[11], 71), 0),
        "win_value": draw_win_value(jax.random.fold_in(streams_of[11], 71), 0),
        "clu_query": draw_clu_query(jax.random.fold_in(streams_of[11], 71), 0),
        "clu_key": draw_clu_key(jax.random.fold_in(streams_of[11], 71), 0),
        "clu_value": draw_clu_value(jax.random.fold_in(streams_of[11], 71), 0),
        "cluster_ids": draw_cluster_ids(jax.random.fold_in(streams_of[11], 71), 0),
        "win_gain": jnp.clip(1.0 + 0.1 * jax.random.normal(streams_of[7], (HW * DH,), jnp.float32), 0.5, 1.5),
        "clu_gain": jnp.clip(1.0 + 0.1 * jax.random.normal(streams_of[8], (HC * DH,), jnp.float32), 0.5, 1.5),
        "win_out_grad": draw_win_out_grad(jax.random.fold_in(streams_of[11], 71), 0),
        "clu_out_grad": draw_clu_out_grad(jax.random.fold_in(streams_of[11], 71), 0),
    }


EPSILON = 1e-06

def to_bf16_f32(values):
    return lax.optimization_barrier(values.astype(jnp.bfloat16)).astype(jnp.float32)

def softmax_rows(scores, allowed):
    masked = jnp.where(allowed, scores, -jnp.inf)
    top_row = lax.optimization_barrier(jnp.max(masked, axis=-1, keepdims=True))
    summed = lax.optimization_barrier(jnp.sum(jnp.exp(masked - top_row), axis=-1, keepdims=True))
    return jnp.exp(masked - (top_row + jnp.log(summed)))

def window_layout(values):
    blocks = values.astype(jnp.float32).reshape(-1, TOK_DEV, DH)
    before = jnp.concatenate([jnp.zeros_like(blocks[:1]), blocks[:-1]], axis=0)
    return (blocks, jnp.concatenate([before, blocks], axis=1))

def window_mask():
    n_blocks = TOKENS // TOK_DEV
    block_ids = jnp.arange(n_blocks, dtype=jnp.int32)[:, None, None] * TOK_DEV
    query_pos = block_ids + jnp.arange(TOK_DEV, dtype=jnp.int32)[None, :, None]
    key_pos = block_ids - TOK_DEV + jnp.arange(2 * TOK_DEV, dtype=jnp.int32)[None, None, :]
    gap_pos = query_pos - key_pos
    return (gap_pos >= 0) & (gap_pos < WINDOW) & (key_pos >= 0)

def window_core(queries, key_rows, val_rows):
    q_blocks, _ = window_layout(queries)
    _, k_ext = window_layout(key_rows)
    _, v_ext = window_layout(val_rows)
    scores = jnp.einsum('bid,bjd->bij', q_blocks, k_ext) * DH ** (-0.5)
    attn_prob = softmax_rows(scores, window_mask())
    weights = to_bf16_f32(attn_prob)
    return (q_blocks, k_ext, v_ext, attn_prob, weights)

def window_forward(queries, key_rows, val_rows):
    _, _, v_ext, _, weights = window_core(queries, key_rows, val_rows)
    return jnp.einsum('bij,bjd->bid', weights, v_ext).astype(jnp.bfloat16).reshape(TOKENS, DH)

def fold_blocks(part):
    own_part = part[:, TOK_DEV:]
    later = jnp.concatenate([part[1:, :TOK_DEV], jnp.zeros_like(part[:1, :TOK_DEV])], axis=0)
    return (own_part + later).reshape(TOKENS, DH)

def window_backward(queries, key_rows, val_rows, grad_rows, outputs):
    q_blocks, k_ext, v_ext, attn_prob, weights = window_core(queries, key_rows, val_rows)
    g_blocks = grad_rows.astype(jnp.float32).reshape(-1, TOK_DEV, DH)
    row_dot = lax.optimization_barrier(jnp.sum(g_blocks * outputs.astype(jnp.float32).reshape(-1, TOK_DEV, DH), axis=-1, keepdims=True))
    slope_rows = jnp.einsum('bid,bjd->bij', g_blocks, v_ext)
    change = to_bf16_f32(attn_prob * (slope_rows - row_dot))
    factor = DH ** (-0.5)
    grad_q = (jnp.einsum('bij,bjd->bid', change, k_ext) * factor).astype(jnp.bfloat16).reshape(TOKENS, DH)
    key_part = jnp.einsum('bij,bid->bjd', change, q_blocks)
    val_part = jnp.einsum('bij,bid->bjd', weights, g_blocks)
    grad_k = (fold_blocks(key_part) * factor).astype(jnp.bfloat16)
    grad_v = fold_blocks(val_part).astype(jnp.bfloat16)
    return (grad_q, grad_k, grad_v)

def cluster_layout(cluster_row):
    order_rows = jnp.argsort(cluster_row, stable=True).astype(jnp.int32)
    counts = jax.ops.segment_sum(jnp.ones((TOKENS,), jnp.int32), cluster_row, num_segments=CLUSTERS)
    starts = (jnp.cumsum(counts) - counts).astype(jnp.int32)
    sorted_ids = cluster_row[order_rows]
    rank_in = jnp.arange(TOKENS, dtype=jnp.int32) - starts[sorted_ids]
    slot_of = (sorted_ids * SLOTS + rank_in).astype(jnp.int32)
    slot_table = jnp.full((CLUSTERS * SLOTS,), TOKENS, jnp.int32).at[slot_of].set(order_rows)
    token_slot = jnp.zeros((TOKENS,), jnp.int32).at[order_rows].set(slot_of)
    return (slot_table, token_slot)

def padded(values, slot_table):
    valid_rows = slot_table < TOKENS
    picked = jnp.take(values.astype(jnp.float32), jnp.minimum(slot_table, TOKENS - 1), axis=0)
    picked = jnp.where(valid_rows[:, None], picked, 0.0)
    return (picked.reshape(CLUSTERS, SLOTS, DH), valid_rows.reshape(CLUSTERS, SLOTS))

def cluster_core(queries, key_rows, val_rows, cluster_row):
    slot_table, token_slot = cluster_layout(cluster_row)
    q_pad, valid_rows = padded(queries, slot_table)
    k_pad, _ = padded(key_rows, slot_table)
    v_pad, _ = padded(val_rows, slot_table)
    scores = jnp.einsum('cid,cjd->cij', q_pad, k_pad) * DH ** (-0.5)
    row_pos = lax.broadcasted_iota(jnp.int32, (SLOTS, SLOTS), 0)
    col_pos = lax.broadcasted_iota(jnp.int32, (SLOTS, SLOTS), 1)
    allowed = valid_rows[:, None, :] & (col_pos <= row_pos)[None] | (col_pos == row_pos)[None]
    attn_prob = softmax_rows(scores, allowed)
    weights = to_bf16_f32(attn_prob)
    out_pad = jnp.einsum('cij,cjd->cid', weights, v_pad).astype(jnp.bfloat16)
    return (slot_table, token_slot, q_pad, k_pad, v_pad, attn_prob, weights, out_pad)

def cluster_forward(queries, key_rows, val_rows, cluster_row):
    parts = cluster_core(queries, key_rows, val_rows, cluster_row)
    return parts[7].reshape(-1, DH)[parts[1]]

def cluster_backward(queries, key_rows, val_rows, cluster_row, grad_rows):
    slot_table, token_slot, q_pad, k_pad, v_pad, attn_prob, weights, out_pad = cluster_core(queries, key_rows, val_rows, cluster_row)
    g_pad, _ = padded(grad_rows, slot_table)
    row_dot = lax.optimization_barrier(jnp.sum(g_pad * out_pad.astype(jnp.float32), axis=-1, keepdims=True))
    slope_rows = jnp.einsum('cid,cjd->cij', g_pad, v_pad)
    change = to_bf16_f32(attn_prob * (slope_rows - row_dot))
    factor = DH ** (-0.5)
    grad_q = (jnp.einsum('cij,cjd->cid', change, k_pad) * factor).astype(jnp.bfloat16)
    grad_k = (jnp.einsum('cij,cid->cjd', change, q_pad) * factor).astype(jnp.bfloat16)
    grad_v = jnp.einsum('cij,cid->cjd', weights, g_pad).astype(jnp.bfloat16)
    return (grad_q.reshape(-1, DH)[token_slot], grad_k.reshape(-1, DH)[token_slot], grad_v.reshape(-1, DH)[token_slot])

def by_head(values, n_heads):
    return values.reshape(TOKENS, n_heads, DH).transpose(1, 0, 2)

def by_token(values, n_heads):
    return values.transpose(1, 0, 2).reshape(TOKENS, n_heads * DH)

def reference(win_query, win_key, win_value, clu_query, clu_key, clu_value, cluster_ids, win_gain, clu_gain, win_out_grad, clu_out_grad):
    q_win, k_win, v_win = (by_head(win_query, HW), by_head(win_key, HW), by_head(win_value, HW))
    q_clu, k_clu, v_clu = (by_head(clu_query, HC), by_head(clu_key, HC), by_head(clu_value, HC))
    attn_win = lax.map(lambda packed: window_forward(*packed), (q_win, k_win, v_win))
    attn_clu = lax.map(lambda packed: cluster_forward(*packed), (q_clu, k_clu, v_clu, cluster_ids))
    flat_win = by_token(attn_win, HW).astype(jnp.float32)
    flat_clu = by_token(attn_clu, HC).astype(jnp.float32)
    feat_width = (HW + HC) * DH
    sq_total = lax.optimization_barrier(jnp.sum(flat_win * flat_win, axis=1)) + lax.optimization_barrier(jnp.sum(flat_clu * flat_clu, axis=1))
    inv_rms = 1.0 / jnp.sqrt(sq_total / feat_width + EPSILON)
    win_normed = (flat_win * inv_rms[:, None] * win_gain).astype(jnp.bfloat16)
    clu_normed = (flat_clu * inv_rms[:, None] * clu_gain).astype(jnp.bfloat16)
    grad_win = win_out_grad.astype(jnp.float32) * win_gain
    grad_clu = clu_out_grad.astype(jnp.float32) * clu_gain
    dot_total = lax.optimization_barrier(jnp.sum(grad_win * flat_win, axis=1)) + lax.optimization_barrier(jnp.sum(grad_clu * flat_clu, axis=1))
    coef_rows = inv_rms ** 3 * dot_total / feat_width
    dout_win = (inv_rms[:, None] * grad_win - coef_rows[:, None] * flat_win).astype(jnp.bfloat16)
    dout_clu = (inv_rms[:, None] * grad_clu - coef_rows[:, None] * flat_clu).astype(jnp.bfloat16)
    win_grads = lax.map(lambda packed: window_backward(*packed), (q_win, k_win, v_win, by_head(dout_win, HW), attn_win))
    clu_grads = lax.map(lambda packed: cluster_backward(*packed), (q_clu, k_clu, v_clu, cluster_ids, by_head(dout_clu, HC)))
    return (win_normed, clu_normed, by_token(win_grads[0], HW), by_token(win_grads[1], HW), by_token(win_grads[2], HW), by_token(clu_grads[0], HC), by_token(clu_grads[1], HC), by_token(clu_grads[2], HC))
```

```python
import functools

import jax
import jax.numpy as jnp
from jax import lax
from jax.experimental import pallas as pl
from jax.experimental.pallas import tpu as pltpu
from jax.sharding import PartitionSpec as P

HW = 32
HC = 32
DH = 128
WINDOW = 256
SLOTS = 128
CHUNKS = 2

EPSILON = 1e-06
F32 = jnp.float32
BF16 = jnp.bfloat16


def from_behind(block, axis, distance):
    devices = range(lax.axis_size(axis))
    route = [(i - distance, i) for i in devices if i - distance in devices]
    return lax.ppermute(block, axis, route)


def nt(a, b):
    return lax.dot_general(a, b, (((1,), (1,)), ((), ())), preferred_element_type=F32)


def tn(a, b):
    return lax.dot_general(a, b, (((0,), (0,)), ((), ())), preferred_element_type=F32)


def nn(a, b):
    return jnp.dot(a, b, preferred_element_type=F32)


def one_hot(slot_ref, pool):
    n = slot_ref.shape[-1]
    hit = lax.broadcasted_iota(jnp.int32, (pool, n), 0) == slot_ref[0]
    return jnp.where(hit, 1.0, 0.0).astype(BF16)


def normalized(scores, allowed):
    masked = jnp.where(allowed, scores, -jnp.inf)
    grown = jnp.exp(masked - jnp.max(masked, axis=-1, keepdims=True))
    return grown * (1.0 / jnp.sum(grown, axis=-1, keepdims=True))


def call(kernel, grid, in_specs, out_specs, out_shape, flops, size, **more):
    return pl.pallas_call(
        kernel,
        grid=grid,
        in_specs=in_specs,
        out_specs=out_specs,
        out_shape=out_shape,
        cost_estimate=pl.CostEstimate(flops=flops, bytes_accessed=size, transcendentals=0),
        compiler_params=pltpu.CompilerParams(vmem_limit_bytes=48 << 20),
        **more,
    )


def dispatch_kernel(*refs):
    slot_ref, value_refs, out_ref = refs[0], refs[1:-1], refs[-1]
    picked = one_hot(slot_ref, out_ref.shape[0])
    for i, ref in enumerate(value_refs):
        out_ref[:, i * DH : (i + 1) * DH] = nn(picked, ref[...]).astype(BF16)


def dispatch(slot_at, values, first, count, pool):
    n = slot_at.shape[-1]
    wide = len(values) * DH
    return call(
        dispatch_kernel,
        (count,),
        [pl.BlockSpec((1, 1, n), lambda h: (h + first, 0, 0))]
        + [pl.BlockSpec((n, DH), lambda h: (0, h + first)) for _ in values],
        pl.BlockSpec((pool, wide), lambda h: (0, h)),
        jax.ShapeDtypeStruct((pool, count * wide), BF16),
        2 * count * pool * n * wide,
        2 * count * (pool + n) * wide,
    )(slot_at, *values)


def collect_kernel(n_out, *refs):
    slot_ref, rows_ref, out_refs = refs[0], refs[1], refs[-n_out:]
    picked = one_hot(slot_ref, rows_ref.shape[0])
    merged = tn(picked, rows_ref[...]).astype(BF16)
    for i, ref in enumerate(out_refs):
        ref[...] = merged[:, i * DH : (i + 1) * DH]


def collect(slot_at, rows, first, count, n_out, earlier):
    n = slot_at.shape[-1]
    pool = rows.shape[0]
    heads = slot_at.shape[0]
    wide = n_out * DH
    return call(
        functools.partial(collect_kernel, n_out),
        (count,),
        [
            pl.BlockSpec((1, 1, n), lambda h: (h + first, 0, 0)),
            pl.BlockSpec((pool, wide), lambda h: (0, h)),
        ]
        + [pl.BlockSpec(memory_space=pl.ANY) for _ in earlier],
        [pl.BlockSpec((n, DH), lambda h: (0, h + first))] * n_out,
        [jax.ShapeDtypeStruct((n, heads * DH), BF16)] * n_out,
        2 * count * pool * n * wide,
        2 * count * (pool + n) * wide,
        input_output_aliases={2 + i: i for i in range(len(earlier))},
    )(slot_at, rows, *earlier)


class Rows:
    def __init__(self, sources, owned, cap):
        self.sources, self.owned, self.cap = sources, owned, cap
        self.aligned = cap % 8 == 0

    def selector(self, c):
        members = self.sources * self.cap
        layout = (members, members * self.owned)
        member = lax.broadcasted_iota(jnp.int32, layout, 0)
        row = lax.broadcasted_iota(jnp.int32, layout, 1)
        want = member // self.cap * (self.cap * self.owned) + c * self.cap + member % self.cap
        return jnp.where(row == want, 1.0, 0.0).astype(BF16)

    def split(self, rows):
        members = self.sources * self.cap
        if not self.aligned:
            return [nn(self.selector(c), rows).astype(BF16) for c in range(self.owned)]
        wide = rows.shape[1]
        four = rows.astype(F32).reshape(self.sources, self.owned, self.cap, wide)
        return [four[:, c].reshape(members, wide).astype(BF16) for c in range(self.owned)]

    def join(self, parts):
        wide = parts[0].shape[1]
        pool = self.sources * self.cap * self.owned
        if not self.aligned:
            total = jnp.zeros((pool, wide), F32)
            for c, part in enumerate(parts):
                total = total + tn(self.selector(c), part.astype(BF16))
            return total.astype(BF16)
        shaped = [p.reshape(self.sources, 1, self.cap, wide) for p in parts]
        return jnp.concatenate(shaped, axis=1).reshape(pool, wide).astype(BF16)


def cluster_allowed(live_ref, c, members):
    row = lax.broadcasted_iota(jnp.int32, (members, members), 0)
    col = lax.broadcasted_iota(jnp.int32, (members, members), 1)
    live = jnp.broadcast_to(live_ref[0, c : c + 1, :], (members, members)) > 0.5
    return (live & (col <= row)) | (col == row)


def owner_fwd_kernel(rows, factor, live_ref, qkv_ref, out_ref):
    members = rows.sources * rows.cap
    parts = []
    for c, qkv in enumerate(rows.split(qkv_ref[...])):
        q, k, v = qkv[:, :DH], qkv[:, DH : 2 * DH], qkv[:, 2 * DH :]
        prob = normalized(nt(q, k) * factor, cluster_allowed(live_ref, c, members))
        parts.append(nn(prob.astype(BF16), v))
    out_ref[...] = rows.join(parts)


def owner_bwd_kernel(rows, factor, live_ref, qkv_ref, attn_ref, grad_ref, out_ref):
    members = rows.sources * rows.cap
    attn_parts = rows.split(attn_ref[...])
    grad_parts = rows.split(grad_ref[...])
    parts = []
    for c, qkv in enumerate(rows.split(qkv_ref[...])):
        q, k, v = qkv[:, :DH], qkv[:, DH : 2 * DH], qkv[:, 2 * DH :]
        grad = grad_parts[c]
        row_dot = jnp.sum(grad.astype(F32) * attn_parts[c].astype(F32), axis=-1, keepdims=True)
        prob = normalized(nt(q, k) * factor, cluster_allowed(live_ref, c, members))
        change = (prob * (nt(grad, v) - row_dot)).astype(BF16)
        dq = nn(change, k) * factor
        dk = tn(change, q) * factor
        dv = tn(prob.astype(BF16), grad)
        parts.append(jnp.concatenate([dq, dk, dv], axis=1))
    out_ref[...] = rows.join(parts)


def owner_call(kernel, rows, factor, live, first, arrays, n_out):
    pool = arrays[0].shape[0]
    count = arrays[0].shape[1] // (3 * DH)
    members = rows.sources * rows.cap
    wides = [a.shape[1] // count for a in arrays]
    return call(
        functools.partial(kernel, rows, factor),
        (count,),
        [pl.BlockSpec((1, rows.owned, members), lambda h: (h + first, 0, 0))]
        + [pl.BlockSpec((pool, w), lambda h: (0, h)) for w in wides],
        pl.BlockSpec((pool, n_out * DH), lambda h: (0, h)),
        jax.ShapeDtypeStruct((pool, count * n_out * DH), BF16),
        12 * count * pool * members * DH,
        2 * count * pool * (sum(wides) + n_out * DH),
    )(live, *arrays)


def window_prob(factor, q, keys):
    n = q.shape[0]
    row = lax.broadcasted_iota(jnp.int32, (n, n + WINDOW), 0)
    col = lax.broadcasted_iota(jnp.int32, (n, n + WINDOW), 1)
    gap = row + WINDOW - col
    lowest = jnp.where(lax.axis_index("seq") > 0, 0, WINDOW)
    allowed = (gap >= 0) & (gap < WINDOW) & (col >= lowest)
    return normalized(nt(q, keys) * factor, allowed)


def window_fwd_kernel(factor, q_ref, kp_ref, k_ref, vp_ref, v_ref, out_ref):
    keys = jnp.concatenate([kp_ref[0], k_ref[...]], axis=0)
    vals = jnp.concatenate([vp_ref[0], v_ref[...]], axis=0)
    prob = window_prob(factor, q_ref[...], keys)
    out_ref[...] = nn(prob.astype(BF16), vals).astype(BF16)


def window_bwd_kernel(
    factor, q_ref, kp_ref, k_ref, vp_ref, v_ref, attn_ref, grad_ref, dq_ref, dk_ref, dv_ref, rim_ref
):
    q, grad = q_ref[...], grad_ref[...]
    keys = jnp.concatenate([kp_ref[0], k_ref[...]], axis=0)
    vals = jnp.concatenate([vp_ref[0], v_ref[...]], axis=0)
    prob = window_prob(factor, q, keys)
    row_dot = jnp.sum(grad.astype(F32) * attn_ref[...].astype(F32), axis=-1, keepdims=True)
    change = (prob * (nt(grad, vals) - row_dot)).astype(BF16)
    dq_ref[...] = (nn(change, keys) * factor).astype(BF16)
    dk = tn(change, q)
    dv = tn(prob.astype(BF16), grad)
    rim_ref[0] = dk[:WINDOW].astype(BF16)
    rim_ref[1] = dv[:WINDOW].astype(BF16)
    dk_ref[...] = dk[WINDOW:]
    dv_ref[...] = dv[WINDOW:]


def window_specs(n):
    here = pl.BlockSpec((n, DH), lambda h: (0, h))
    key = pl.BlockSpec((1, n, DH), lambda h: (0, 0, h))
    val = pl.BlockSpec((1, n, DH), lambda h: (1, 0, h))
    return here, key, val


def window_fwd(factor, query, key, value, before):
    n, wide = query.shape
    here, rim_key, rim_val = window_specs(n)
    return call(
        functools.partial(window_fwd_kernel, factor),
        (wide // DH,),
        [here, rim_key, here, rim_val, here],
        here,
        jax.ShapeDtypeStruct((n, wide), BF16),
        4 * n * 2 * n * wide,
        12 * n * wide,
    )(query, before, key, before, value)


def window_bwd(factor, query, key, value, before, attn, grad):
    n, wide = query.shape
    here, rim_key, rim_val = window_specs(n)
    return call(
        functools.partial(window_bwd_kernel, factor),
        (wide // DH,),
        [here, rim_key, here, rim_val, here, here, here],
        [here, here, here, pl.BlockSpec((2, n, DH), lambda h: (0, 0, h))],
        [
            jax.ShapeDtypeStruct((n, wide), BF16),
            jax.ShapeDtypeStruct((n, wide), F32),
            jax.ShapeDtypeStruct((n, wide), F32),
            jax.ShapeDtypeStruct((2, n, wide), BF16),
        ],
        10 * n * 2 * n * wide,
        28 * n * wide,
    )(query, before, key, before, value, attn, grad)


def body(
    win_query,
    win_key,
    win_value,
    clu_query,
    clu_key,
    clu_value,
    cluster_ids,
    win_gain,
    clu_gain,
    win_out_grad,
    clu_out_grad,
):
    n_rows = win_query.shape[0]
    factor = DH ** (-0.5)
    feat_width = (HW + HC) * DH
    sources = lax.axis_size("seq")
    n_cap = SLOTS // sources
    owned_count = 2 * n_rows // SLOTS
    pool_size = 2 * n_rows
    clu_heads = clu_query.shape[1] // DH
    rows = Rows(sources, owned_count, n_cap)

    def exchange(values):
        shaped = values.reshape(sources, pool_size // sources, values.shape[1])
        moved = lax.all_to_all(shaped, "seq", split_axis=0, concat_axis=0, tiled=True)
        return moved.reshape(values.shape)

    row_ids = lax.broadcasted_iota(jnp.int32, (n_rows, n_rows), 0)
    col_ids = lax.broadcasted_iota(jnp.int32, (n_rows, n_rows), 1)
    same_cluster = (cluster_ids[:, :, None] == cluster_ids[:, None, :]) & (col_ids < row_ids)
    rank_in = jnp.sum(same_cluster.astype(jnp.int32), axis=-1)
    slot_at = (cluster_ids * n_cap + rank_in)[:, None, :]

    n_clusters = sources * owned_count
    every = lax.broadcasted_iota(jnp.int32, (n_clusters, clu_heads, n_rows), 0)
    counts = jnp.sum((cluster_ids[None] == every).astype(F32), axis=-1)
    counts = counts.reshape(sources, owned_count, clu_heads)
    counts = lax.all_to_all(counts, "seq", split_axis=0, concat_axis=0, tiled=True)
    slot_pos = lax.broadcasted_iota(F32, (clu_heads, owned_count, sources, n_cap), 3)
    live = (slot_pos < counts.transpose(2, 1, 0)[..., None]).astype(F32)
    live = live.reshape(clu_heads, owned_count, sources * n_cap)

    chunks = CHUNKS if clu_heads % CHUNKS == 0 else 1
    per = clu_heads // chunks
    starts = [i * per for i in range(chunks)]

    held = [
        exchange(dispatch(slot_at, [clu_query, clu_key, clu_value], first, per, pool_size))
        for first in starts
    ]
    before = from_behind(jnp.stack([win_key, win_value]), "seq", 1)
    attn_win = window_fwd(factor, win_query, win_key, win_value, before)

    attn_held = [
        owner_call(owner_fwd_kernel, rows, factor, live, first, [qkv], 1)
        for first, qkv in zip(starts, held)
    ]
    attn_back = [exchange(part) for part in attn_held]
    attn_clu = ()
    for first, part in zip(starts, attn_back):
        attn_clu = collect(slot_at, part, first, per, 1, attn_clu)
    attn_clu = attn_clu[0]

    flat_win = attn_win.astype(F32)
    flat_clu = attn_clu.astype(F32)
    grad_win = win_out_grad.astype(F32) * win_gain
    grad_clu = clu_out_grad.astype(F32) * clu_gain
    totals = jnp.stack(
        [
            jnp.sum(flat_win * flat_win, axis=1) + jnp.sum(flat_clu * flat_clu, axis=1),
            jnp.sum(grad_win * flat_win, axis=1) + jnp.sum(grad_clu * flat_clu, axis=1),
        ]
    )
    totals = lax.psum(totals, "head")
    sq_total, dot_total = totals[0], totals[1]
    inv_rms = 1.0 / jnp.sqrt(sq_total / feat_width + EPSILON)
    coef_rows = inv_rms**3 * dot_total / feat_width
    dout_clu = (inv_rms[:, None] * grad_clu - coef_rows[:, None] * flat_clu).astype(BF16)
    dout_win = (inv_rms[:, None] * grad_win - coef_rows[:, None] * flat_win).astype(BF16)
    win_normed = (flat_win * inv_rms[:, None] * win_gain).astype(BF16)
    clu_normed = (flat_clu * inv_rms[:, None] * clu_gain).astype(BF16)

    grad_held = [
        exchange(dispatch(slot_at, [dout_clu], first, per, pool_size)) for first in starts
    ]
    win_dq, key_own, val_own, rim = window_bwd(
        factor, win_query, win_key, win_value, before, attn_win, dout_win
    )
    after_rim = from_behind(rim, "seq", -1)

    clu_grads = ()
    sent = [
        owner_call(owner_bwd_kernel, rows, factor, live, first, [qkv, part, grad], 3)
        for first, qkv, part, grad in zip(starts, held, attn_held, grad_held)
    ]
    home = [exchange(part) for part in sent]
    win_dk = ((key_own + after_rim[0]) * factor).astype(BF16)
    win_dv = (val_own + after_rim[1]).astype(BF16)
    for first, part in zip(starts, home):
        clu_grads = collect(slot_at, part, first, per, 3, clu_grads)
    return (win_normed, clu_normed, win_dq, win_dk, win_dv, *clu_grads)


BIG = 1e30


def hits_of(slot, pool):
    n = slot.shape[-1]
    hit = lax.broadcasted_iota(jnp.int32, (pool, n), 0) == slot
    return jnp.where(hit, 1.0, 0.0).astype(BF16)


def sort_block(slot_ref, values, b, cap, pool, into_ref):
    wide = values.shape[1]
    rows = nn(hits_of(slot_ref[b], pool), values)
    at = pl.ds(pl.multiple_of(b * cap, cap), cap)
    into_ref[:, at, :] = rows.reshape(pool // cap, cap, wide)


def unsort_block(slot_ref, from_ref, b, cap, pool):
    at = pl.ds(pl.multiple_of(b * cap, cap), cap)
    rows = from_ref[:, at, :]
    rows = rows.reshape(pool, rows.shape[2]).astype(BF16)
    return tn(hits_of(slot_ref[b], pool), rows).astype(BF16)


def cluster_prob(factor, rows, members):
    lane = lax.broadcasted_iota(jnp.int32, (members, DH), 1)
    pick = jnp.where(lane == 0, BIG, 0.0).astype(BF16)
    q = jnp.concatenate([rows[:, :DH].astype(BF16), pick], axis=1)
    k = jnp.concatenate(
        [rows[:, DH : 2 * DH].astype(BF16), (rows[:, 3 * DH :] - 1.0).astype(BF16)], axis=1
    )
    row = lax.broadcasted_iota(jnp.int32, (members, members), 0)
    col = lax.broadcasted_iota(jnp.int32, (members, members), 1)
    return normalized(nt(q, k) * factor, col <= row)


def with_ones(values):
    return jnp.concatenate([values, jnp.ones((values.shape[0], DH), BF16)], axis=1)


def head_fwd_kernel(factor, cap, group, slot_ref, qkv_ref, out_ref, held, outs):
    blocks = qkv_ref.shape[0]
    clusters, members = held.shape[0], held.shape[1]
    pool = clusters * cap

    @pl.loop(0, blocks)
    def _(b):
        sort_block(slot_ref, with_ones(qkv_ref[b]), b, cap, pool, held)

    @pl.loop(0, clusters // group)
    def _(g):
        for i in range(group):
            c = g * group + i
            rows = held[c]
            prob = cluster_prob(factor, rows, members)
            outs[c] = nn(prob.astype(BF16), rows[:, 2 * DH : 3 * DH].astype(BF16))

    @pl.loop(0, blocks)
    def _(b):
        out_ref[b] = unsort_block(slot_ref, outs, b, cap, pool)


def head_bwd_kernel(
    factor, cap, group, slot_ref, qkv_ref, attn_ref, grad_ref, out_ref, held, given
):
    blocks = qkv_ref.shape[0]
    clusters, members = held.shape[0], held.shape[1]
    pool = clusters * cap

    @pl.loop(0, blocks)
    def _(b):
        sort_block(slot_ref, with_ones(qkv_ref[b]), b, cap, pool, held)
        both = jnp.concatenate([grad_ref[b], attn_ref[b]], axis=1)
        sort_block(slot_ref, both, b, cap, pool, given)

    @pl.loop(0, clusters // group)
    def _(g):
        for i in range(group):
            c = g * group + i
            rows = held[c]
            q, k, v = (rows[:, j * DH : (j + 1) * DH].astype(BF16) for j in range(3))
            prob = cluster_prob(factor, rows, members)
            both = given[c]
            row_dot = jnp.sum(both[:, :DH] * both[:, DH:], axis=-1, keepdims=True)
            grad = both[:, :DH].astype(BF16)
            change = (prob * (nt(grad, v) - row_dot)).astype(BF16)
            held[c, :, :DH] = nn(change, k) * factor
            held[c, :, DH : 2 * DH] = tn(change, q) * factor
            held[c, :, 2 * DH : 3 * DH] = tn(prob.astype(BF16), grad)

    @pl.loop(0, blocks)
    def _(b):
        at = pl.ds(pl.multiple_of(b * cap, cap), cap)
        rows = held[:, at, : 3 * DH].reshape(pool, 3 * DH).astype(BF16)
        out_ref[b] = tn(hits_of(slot_ref[b], pool), rows).astype(BF16)


def head_call(kernel, factor, cap, clusters, arrays, n_out, second):
    blocks, n = arrays[0].shape[0], arrays[0].shape[2]
    members = blocks * cap
    vmem = pl.BlockSpec(memory_space=pltpu.VMEM)
    return pl.pallas_call(
        functools.partial(kernel, factor, cap, 4 if clusters % 4 == 0 else 1),
        in_specs=[vmem] * len(arrays),
        out_specs=vmem,
        out_shape=jax.ShapeDtypeStruct((blocks, n, n_out * DH), BF16),
        scratch_shapes=[
            pltpu.VMEM((clusters, members, 4 * DH), F32),
            pltpu.VMEM((clusters, members, second * DH), F32),
        ],
        cost_estimate=pl.CostEstimate(
            flops=20 * clusters * members * members * DH,
            bytes_accessed=8 * blocks * n * DH * 2,
            transcendentals=0,
        ),
        compiler_params=pltpu.CompilerParams(vmem_limit_bytes=48 << 20),
    )(*arrays)


def pack_kernel(*refs):
    out_ref = refs[-1]
    for i, ref in enumerate(refs[:-1]):
        out_ref[0, :, i * DH : (i + 1) * DH] = ref[...]


def pack(values):
    n, wide = values[0].shape
    heads, count = wide // DH, len(values)
    return call(
        pack_kernel,
        (heads,),
        [pl.BlockSpec((n, DH), lambda h: (0, h))] * count,
        pl.BlockSpec((1, n, count * DH), lambda h: (h, 0, 0)),
        jax.ShapeDtypeStruct((heads, n, count * DH), BF16),
        0,
        4 * count * n * wide,
    )(*values)


def unpack_kernel(*refs):
    for i, ref in enumerate(refs[1:]):
        ref[...] = refs[0][0, :, i * DH : (i + 1) * DH]


def unpack(values):
    heads, n, wide = values.shape
    count = wide // DH
    return call(
        unpack_kernel,
        (heads,),
        [pl.BlockSpec((1, n, wide), lambda h: (h, 0, 0))],
        [pl.BlockSpec((n, DH), lambda h: (0, h))] * count,
        [jax.ShapeDtypeStruct((n, heads * DH), BF16)] * count,
        0,
        4 * heads * n * wide,
    )(values)


def whole_heads_body(
    win_query,
    win_key,
    win_value,
    clu_query,
    clu_key,
    clu_value,
    cluster_ids,
    win_gain,
    clu_gain,
    win_out_grad,
    clu_out_grad,
):
    n_rows = win_query.shape[0]
    factor = DH ** (-0.5)
    feat_width = (HW + HC) * DH
    sources = lax.axis_size("seq")
    n_cap = SLOTS // sources
    clusters = sources * (2 * n_rows // SLOTS)

    def exchange(values):
        return lax.all_to_all(values, "seq", split_axis=0, concat_axis=0, tiled=True)

    row_ids = lax.broadcasted_iota(jnp.int32, (n_rows, n_rows), 0)
    col_ids = lax.broadcasted_iota(jnp.int32, (n_rows, n_rows), 1)
    same_cluster = (cluster_ids[:, :, None] == cluster_ids[:, None, :]) & (col_ids < row_ids)
    rank_in = jnp.sum(same_cluster.astype(jnp.int32), axis=-1)
    slot_at = exchange((cluster_ids * n_cap + rank_in)[:, None, :])

    qkv = exchange(pack([clu_query, clu_key, clu_value]))
    before = from_behind(jnp.stack([win_key, win_value]), "seq", 1)
    attn_win = window_fwd(factor, win_query, win_key, win_value, before)
    attn_head = head_call(head_fwd_kernel, factor, n_cap, clusters, [slot_at, qkv], 1, 1)
    (attn_clu,) = unpack(exchange(attn_head))

    flat_win = attn_win.astype(F32)
    flat_clu = attn_clu.astype(F32)
    grad_win = win_out_grad.astype(F32) * win_gain
    grad_clu = clu_out_grad.astype(F32) * clu_gain
    totals = jnp.stack(
        [
            jnp.sum(flat_win * flat_win, axis=1) + jnp.sum(flat_clu * flat_clu, axis=1),
            jnp.sum(grad_win * flat_win, axis=1) + jnp.sum(grad_clu * flat_clu, axis=1),
        ]
    )
    totals = lax.psum(totals, "head")
    sq_total, dot_total = totals[0], totals[1]
    inv_rms = 1.0 / jnp.sqrt(sq_total / feat_width + EPSILON)
    coef_rows = inv_rms**3 * dot_total / feat_width
    dout_clu = (inv_rms[:, None] * grad_clu - coef_rows[:, None] * flat_clu).astype(BF16)
    dout_win = (inv_rms[:, None] * grad_win - coef_rows[:, None] * flat_win).astype(BF16)
    win_normed = (flat_win * inv_rms[:, None] * win_gain).astype(BF16)
    clu_normed = (flat_clu * inv_rms[:, None] * clu_gain).astype(BF16)

    grad_head = exchange(pack([dout_clu]))
    win_dq, key_own, val_own, rim = window_bwd(
        factor, win_query, win_key, win_value, before, attn_win, dout_win
    )
    after_rim = from_behind(rim, "seq", -1)
    grads = head_call(
        head_bwd_kernel, factor, n_cap, clusters, [slot_at, qkv, attn_head, grad_head], 3, 2
    )
    home = exchange(grads)
    win_dk = ((key_own + after_rim[0]) * factor).astype(BF16)
    win_dv = (val_own + after_rim[1]).astype(BF16)
    return (win_normed, clu_normed, win_dq, win_dk, win_dv, *unpack(home))


def solution(mesh):
    sources, split = mesh.shape["seq"], mesh.shape["head"]
    whole_heads = HC // split == sources and SLOTS // sources % 8 == 0
    return jax.shard_map(
        whole_heads_body if whole_heads else body,
        mesh=mesh,
        in_specs=(P("seq", "head"),) * 6
        + (P("head", "seq"), P("head"), P("head"))
        + (P("seq", "head"),) * 2,
        out_specs=(P("seq", "head"),) * 8,
        check_vma=False,
    )
```

```python
import functools

import jax
import jax.numpy as jnp
from jax import lax
from jax.experimental import pallas as pl
from jax.experimental.pallas import tpu as pltpu
from jax.sharding import PartitionSpec as P

HW = 32
HC = 32
DH = 128
WINDOW = 256
SLOTS = 128
CHUNKS = 2

EPSILON = 1e-06
F32 = jnp.float32
BF16 = jnp.bfloat16


def from_behind(block, axis, distance):
    devices = range(lax.axis_size(axis))
    route = [(i - distance, i) for i in devices if i - distance in devices]
    return lax.ppermute(block, axis, route)


def nt(a, b):
    return lax.dot_general(a, b, (((1,), (1,)), ((), ())), preferred_element_type=F32)


def tn(a, b):
    return lax.dot_general(a, b, (((0,), (0,)), ((), ())), preferred_element_type=F32)


def nn(a, b):
    return jnp.dot(a, b, preferred_element_type=F32)


def one_hot(slot_ref, pool):
    n = slot_ref.shape[-1]
    hit = lax.broadcasted_iota(jnp.int32, (pool, n), 0) == slot_ref[0]
    return jnp.where(hit, 1.0, 0.0).astype(BF16)


def normalized(scores, allowed):
    masked = jnp.where(allowed, scores, -jnp.inf)
    grown = jnp.exp(masked - jnp.max(masked, axis=-1, keepdims=True))
    return grown * (1.0 / jnp.sum(grown, axis=-1, keepdims=True))


def call(kernel, grid, in_specs, out_specs, out_shape, flops, size, **more):
    return pl.pallas_call(
        kernel,
        grid=grid,
        in_specs=in_specs,
        out_specs=out_specs,
        out_shape=out_shape,
        cost_estimate=pl.CostEstimate(flops=flops, bytes_accessed=size, transcendentals=0),
        compiler_params=pltpu.CompilerParams(vmem_limit_bytes=48 << 20),
        **more,
    )


def dispatch_kernel(*refs):
    slot_ref, value_refs, out_ref = refs[0], refs[1:-1], refs[-1]
    picked = one_hot(slot_ref, out_ref.shape[0])
    for i, ref in enumerate(value_refs):
        out_ref[:, i * DH : (i + 1) * DH] = nn(picked, ref[...]).astype(BF16)


def dispatch(slot_at, values, first, count, pool):
    n = slot_at.shape[-1]
    wide = len(values) * DH
    return call(
        dispatch_kernel,
        (count,),
        [pl.BlockSpec((1, 1, n), lambda h: (h + first, 0, 0))]
        + [pl.BlockSpec((n, DH), lambda h: (0, h + first)) for _ in values],
        pl.BlockSpec((pool, wide), lambda h: (0, h)),
        jax.ShapeDtypeStruct((pool, count * wide), BF16),
        2 * count * pool * n * wide,
        2 * count * (pool + n) * wide,
    )(slot_at, *values)


def collect_kernel(n_out, *refs):
    slot_ref, rows_ref, out_refs = refs[0], refs[1], refs[-n_out:]
    picked = one_hot(slot_ref, rows_ref.shape[0])
    merged = tn(picked, rows_ref[...]).astype(BF16)
    for i, ref in enumerate(out_refs):
        ref[...] = merged[:, i * DH : (i + 1) * DH]


def collect(slot_at, rows, first, count, n_out, earlier):
    n = slot_at.shape[-1]
    pool = rows.shape[0]
    heads = slot_at.shape[0]
    wide = n_out * DH
    return call(
        functools.partial(collect_kernel, n_out),
        (count,),
        [
            pl.BlockSpec((1, 1, n), lambda h: (h + first, 0, 0)),
            pl.BlockSpec((pool, wide), lambda h: (0, h)),
        ]
        + [pl.BlockSpec(memory_space=pl.ANY) for _ in earlier],
        [pl.BlockSpec((n, DH), lambda h: (0, h + first))] * n_out,
        [jax.ShapeDtypeStruct((n, heads * DH), BF16)] * n_out,
        2 * count * pool * n * wide,
        2 * count * (pool + n) * wide,
        input_output_aliases={2 + i: i for i in range(len(earlier))},
    )(slot_at, rows, *earlier)


class Rows:
    def __init__(self, sources, owned, cap):
        self.sources, self.owned, self.cap = sources, owned, cap
        self.aligned = cap % 8 == 0

    def selector(self, c):
        members = self.sources * self.cap
        layout = (members, members * self.owned)
        member = lax.broadcasted_iota(jnp.int32, layout, 0)
        row = lax.broadcasted_iota(jnp.int32, layout, 1)
        want = member // self.cap * (self.cap * self.owned) + c * self.cap + member % self.cap
        return jnp.where(row == want, 1.0, 0.0).astype(BF16)

    def split(self, rows):
        members = self.sources * self.cap
        if not self.aligned:
            return [nn(self.selector(c), rows).astype(BF16) for c in range(self.owned)]
        wide = rows.shape[1]
        four = rows.astype(F32).reshape(self.sources, self.owned, self.cap, wide)
        return [four[:, c].reshape(members, wide).astype(BF16) for c in range(self.owned)]

    def join(self, parts):
        wide = parts[0].shape[1]
        pool = self.sources * self.cap * self.owned
        if not self.aligned:
            total = jnp.zeros((pool, wide), F32)
            for c, part in enumerate(parts):
                total = total + tn(self.selector(c), part.astype(BF16))
            return total.astype(BF16)
        shaped = [p.reshape(self.sources, 1, self.cap, wide) for p in parts]
        return jnp.concatenate(shaped, axis=1).reshape(pool, wide).astype(BF16)


def cluster_allowed(live_ref, c, members):
    row = lax.broadcasted_iota(jnp.int32, (members, members), 0)
    col = lax.broadcasted_iota(jnp.int32, (members, members), 1)
    live = jnp.broadcast_to(live_ref[0, c : c + 1, :], (members, members)) > 0.5
    return (live & (col <= row)) | (col == row)


def owner_fwd_kernel(rows, factor, live_ref, qkv_ref, out_ref):
    members = rows.sources * rows.cap
    parts = []
    for c, qkv in enumerate(rows.split(qkv_ref[...])):
        q, k, v = qkv[:, :DH], qkv[:, DH : 2 * DH], qkv[:, 2 * DH :]
        prob = normalized(nt(q, k) * factor, cluster_allowed(live_ref, c, members))
        parts.append(nn(prob.astype(BF16), v))
    out_ref[...] = rows.join(parts)


def owner_bwd_kernel(rows, factor, live_ref, qkv_ref, attn_ref, grad_ref, out_ref):
    members = rows.sources * rows.cap
    attn_parts = rows.split(attn_ref[...])
    grad_parts = rows.split(grad_ref[...])
    parts = []
    for c, qkv in enumerate(rows.split(qkv_ref[...])):
        q, k, v = qkv[:, :DH], qkv[:, DH : 2 * DH], qkv[:, 2 * DH :]
        grad = grad_parts[c]
        row_dot = jnp.sum(grad.astype(F32) * attn_parts[c].astype(F32), axis=-1, keepdims=True)
        prob = normalized(nt(q, k) * factor, cluster_allowed(live_ref, c, members))
        change = (prob * (nt(grad, v) - row_dot)).astype(BF16)
        dq = nn(change, k) * factor
        dk = tn(change, q) * factor
        dv = tn(prob.astype(BF16), grad)
        parts.append(jnp.concatenate([dq, dk, dv], axis=1))
    out_ref[...] = rows.join(parts)


def owner_call(kernel, rows, factor, live, first, arrays, n_out):
    pool = arrays[0].shape[0]
    count = arrays[0].shape[1] // (3 * DH)
    members = rows.sources * rows.cap
    wides = [a.shape[1] // count for a in arrays]
    return call(
        functools.partial(kernel, rows, factor),
        (count,),
        [pl.BlockSpec((1, rows.owned, members), lambda h: (h + first, 0, 0))]
        + [pl.BlockSpec((pool, w), lambda h: (0, h)) for w in wides],
        pl.BlockSpec((pool, n_out * DH), lambda h: (0, h)),
        jax.ShapeDtypeStruct((pool, count * n_out * DH), BF16),
        12 * count * pool * members * DH,
        2 * count * pool * (sum(wides) + n_out * DH),
    )(live, *arrays)


def window_prob(factor, q, keys):
    n = q.shape[0]
    row = lax.broadcasted_iota(jnp.int32, (n, n + WINDOW), 0)
    col = lax.broadcasted_iota(jnp.int32, (n, n + WINDOW), 1)
    gap = row + WINDOW - col
    lowest = jnp.where(lax.axis_index("seq") > 0, 0, WINDOW)
    allowed = (gap >= 0) & (gap < WINDOW) & (col >= lowest)
    return normalized(nt(q, keys) * factor, allowed)


def window_fwd_kernel(factor, q_ref, kp_ref, k_ref, vp_ref, v_ref, out_ref):
    keys = jnp.concatenate([kp_ref[0], k_ref[...]], axis=0)
    vals = jnp.concatenate([vp_ref[0], v_ref[...]], axis=0)
    prob = window_prob(factor, q_ref[...], keys)
    out_ref[...] = nn(prob.astype(BF16), vals).astype(BF16)


def window_bwd_kernel(
    factor, q_ref, kp_ref, k_ref, vp_ref, v_ref, attn_ref, grad_ref, dq_ref, dk_ref, dv_ref, rim_ref
):
    q, grad = q_ref[...], grad_ref[...]
    keys = jnp.concatenate([kp_ref[0], k_ref[...]], axis=0)
    vals = jnp.concatenate([vp_ref[0], v_ref[...]], axis=0)
    prob = window_prob(factor, q, keys)
    row_dot = jnp.sum(grad.astype(F32) * attn_ref[...].astype(F32), axis=-1, keepdims=True)
    change = (prob * (nt(grad, vals) - row_dot)).astype(BF16)
    dq_ref[...] = (nn(change, keys) * factor).astype(BF16)
    dk = tn(change, q)
    dv = tn(prob.astype(BF16), grad)
    rim_ref[0] = dk[:WINDOW].astype(BF16)
    rim_ref[1] = dv[:WINDOW].astype(BF16)
    dk_ref[...] = dk[WINDOW:]
    dv_ref[...] = dv[WINDOW:]


def window_specs(n):
    here = pl.BlockSpec((n, DH), lambda h: (0, h))
    key = pl.BlockSpec((1, n, DH), lambda h: (0, 0, h))
    val = pl.BlockSpec((1, n, DH), lambda h: (1, 0, h))
    return here, key, val


def window_fwd(factor, query, key, value, before):
    n, wide = query.shape
    here, rim_key, rim_val = window_specs(n)
    return call(
        functools.partial(window_fwd_kernel, factor),
        (wide // DH,),
        [here, rim_key, here, rim_val, here],
        here,
        jax.ShapeDtypeStruct((n, wide), BF16),
        4 * n * 2 * n * wide,
        12 * n * wide,
    )(query, before, key, before, value)


def window_bwd(factor, query, key, value, before, attn, grad):
    n, wide = query.shape
    here, rim_key, rim_val = window_specs(n)
    return call(
        functools.partial(window_bwd_kernel, factor),
        (wide // DH,),
        [here, rim_key, here, rim_val, here, here, here],
        [here, here, here, pl.BlockSpec((2, n, DH), lambda h: (0, 0, h))],
        [
            jax.ShapeDtypeStruct((n, wide), BF16),
            jax.ShapeDtypeStruct((n, wide), F32),
            jax.ShapeDtypeStruct((n, wide), F32),
            jax.ShapeDtypeStruct((2, n, wide), BF16),
        ],
        10 * n * 2 * n * wide,
        28 * n * wide,
    )(query, before, key, before, value, attn, grad)


def body(
    win_query,
    win_key,
    win_value,
    clu_query,
    clu_key,
    clu_value,
    cluster_ids,
    win_gain,
    clu_gain,
    win_out_grad,
    clu_out_grad,
):
    n_rows = win_query.shape[0]
    factor = DH ** (-0.5)
    feat_width = (HW + HC) * DH
    sources = lax.axis_size("seq")
    n_cap = SLOTS // sources
    owned_count = 2 * n_rows // SLOTS
    pool_size = 2 * n_rows
    clu_heads = clu_query.shape[1] // DH
    rows = Rows(sources, owned_count, n_cap)

    def exchange(values):
        shaped = values.reshape(sources, pool_size // sources, values.shape[1])
        moved = lax.all_to_all(shaped, "seq", split_axis=0, concat_axis=0, tiled=True)
        return moved.reshape(values.shape)

    row_ids = lax.broadcasted_iota(jnp.int32, (n_rows, n_rows), 0)
    col_ids = lax.broadcasted_iota(jnp.int32, (n_rows, n_rows), 1)
    same_cluster = (cluster_ids[:, :, None] == cluster_ids[:, None, :]) & (col_ids < row_ids)
    rank_in = jnp.sum(same_cluster.astype(jnp.int32), axis=-1)
    slot_at = (cluster_ids * n_cap + rank_in)[:, None, :]

    n_clusters = sources * owned_count
    every = lax.broadcasted_iota(jnp.int32, (n_clusters, clu_heads, n_rows), 0)
    counts = jnp.sum((cluster_ids[None] == every).astype(F32), axis=-1)
    counts = counts.reshape(sources, owned_count, clu_heads)
    counts = lax.all_to_all(counts, "seq", split_axis=0, concat_axis=0, tiled=True)
    slot_pos = lax.broadcasted_iota(F32, (clu_heads, owned_count, sources, n_cap), 3)
    live = (slot_pos < counts.transpose(2, 1, 0)[..., None]).astype(F32)
    live = live.reshape(clu_heads, owned_count, sources * n_cap)

    chunks = CHUNKS if clu_heads % CHUNKS == 0 else 1
    per = clu_heads // chunks
    starts = [i * per for i in range(chunks)]

    held = [
        exchange(dispatch(slot_at, [clu_query, clu_key, clu_value], first, per, pool_size))
        for first in starts
    ]
    before = from_behind(jnp.stack([win_key, win_value]), "seq", 1)
    attn_win = window_fwd(factor, win_query, win_key, win_value, before)

    attn_held = [
        owner_call(owner_fwd_kernel, rows, factor, live, first, [qkv], 1)
        for first, qkv in zip(starts, held)
    ]
    attn_back = [exchange(part) for part in attn_held]
    attn_clu = ()
    for first, part in zip(starts, attn_back):
        attn_clu = collect(slot_at, part, first, per, 1, attn_clu)
    attn_clu = attn_clu[0]

    flat_win = attn_win.astype(F32)
    flat_clu = attn_clu.astype(F32)
    grad_win = win_out_grad.astype(F32) * win_gain
    grad_clu = clu_out_grad.astype(F32) * clu_gain
    totals = jnp.stack(
        [
            jnp.sum(flat_win * flat_win, axis=1) + jnp.sum(flat_clu * flat_clu, axis=1),
            jnp.sum(grad_win * flat_win, axis=1) + jnp.sum(grad_clu * flat_clu, axis=1),
        ]
    )
    totals = lax.psum(totals, "head")
    sq_total, dot_total = totals[0], totals[1]
    inv_rms = 1.0 / jnp.sqrt(sq_total / feat_width + EPSILON)
    coef_rows = inv_rms**3 * dot_total / feat_width
    dout_clu = (inv_rms[:, None] * grad_clu - coef_rows[:, None] * flat_clu).astype(BF16)
    dout_win = (inv_rms[:, None] * grad_win - coef_rows[:, None] * flat_win).astype(BF16)
    win_normed = (flat_win * inv_rms[:, None] * win_gain).astype(BF16)
    clu_normed = (flat_clu * inv_rms[:, None] * clu_gain).astype(BF16)

    grad_held = [
        exchange(dispatch(slot_at, [dout_clu], first, per, pool_size)) for first in starts
    ]
    win_dq, key_own, val_own, rim = window_bwd(
        factor, win_query, win_key, win_value, before, attn_win, dout_win
    )
    after_rim = from_behind(rim, "seq", -1)

    clu_grads = ()
    sent = [
        owner_call(owner_bwd_kernel, rows, factor, live, first, [qkv, part, grad], 3)
        for first, qkv, part, grad in zip(starts, held, attn_held, grad_held)
    ]
    home = [exchange(part) for part in sent]
    win_dk = ((key_own + after_rim[0]) * factor).astype(BF16)
    win_dv = (val_own + after_rim[1]).astype(BF16)
    for first, part in zip(starts, home):
        clu_grads = collect(slot_at, part, first, per, 3, clu_grads)
    return (win_normed, clu_normed, win_dq, win_dk, win_dv, *clu_grads)


BIG = 1e30
MESH = pl.DeviceIdType.MESH
LOG2E = 1.4426950408889634


def hits_of(slot, pool):
    n = slot.shape[-1]
    hit = lax.broadcasted_iota(jnp.int32, (pool, n), 0) == slot
    return jnp.where(hit, 1.0, 0.0).astype(BF16)


def hits_by_token(slot, pool):
    n = slot.shape[-1]
    column = jnp.broadcast_to(slot.astype(F32), (8, n)).T[:, :1].astype(jnp.int32)
    hit = lax.broadcasted_iota(jnp.int32, (n, pool), 1) == column
    return jnp.where(hit, 1.0, 0.0).astype(BF16)


def stat_rows(attn, gained):
    wide = attn.shape[1]
    both = jnp.concatenate([attn * attn, gained * attn], axis=1)
    row = lax.broadcasted_iota(jnp.int32, (8, 2 * wide), 0)
    col = lax.broadcasted_iota(jnp.int32, (8, 2 * wide), 1)
    pick = jnp.where(col // wide == row, 1.0, 0.0).astype(BF16)
    high = both.astype(BF16)
    low = (both - high.astype(F32)).astype(BF16)
    return nt(pick, high) + nt(pick, low)


def head_cols(h):
    return pl.ds(pl.multiple_of(h * DH, DH), DH)


def layer_kernel(
    factor,
    cap,
    group,
    wq,
    wk,
    wv,
    cq,
    ck,
    cv,
    ids,
    w_gain,
    c_gain,
    wg,
    cg,
    win_normed,
    clu_normed,
    win_dq,
    win_dk,
    win_dv,
    clu_dq,
    clu_dk,
    clu_dv,
    taken,
    ids_in,
    slots,
    wq_v,
    wk_v,
    wv_v,
    wg_v,
    rim,
    rim_back,
    attn_win,
    attn_home,
    attn_own,
    held,
    outs,
    probs,
    dk_own,
    dv_own,
    part_out,
    part_in,
    pair,
    stat_own,
    stats,
    send_sem,
    recv_sem,
    rim_send,
    rim_recv,
    pair_sem,
    local_sem,
):
    me, core = lax.axis_index("seq"), lax.axis_index("head")
    n_seq = lax.axis_size("seq")
    n = wq.shape[0]
    heads = wq.shape[1] // DH
    clusters, members = held.shape[0], held.shape[1]
    pool = clusters * cap
    feat_width = (HW + HC) * DH
    Q, K, V, G, IDS, ATTN, PART, STAT, DQ, DK, DV = range(11)

    def peer(d):
        return lax.rem(me + d, n_seq)

    def send(kind, src, dst, to):
        return pltpu.make_async_remote_copy(
            src_ref=src,
            dst_ref=dst,
            send_sem=send_sem.at[kind, to],
            recv_sem=recv_sem.at[kind, me],
            device_id=(to, core),
            device_id_type=MESH,
        )

    def keep(kind, src, dst):
        return pltpu.make_async_copy(src, dst, recv_sem.at[kind, me])

    def got(kind, dst, source):
        pltpu.make_async_copy(dst, dst, recv_sem.at[kind, source]).wait()

    def sent(kind, src, to):
        pltpu.make_async_copy(src, src, send_sem.at[kind, to]).wait()

    def deliver(kind, src, dst, to):
        @pl.when(to != me)
        def _():
            send(kind, src, dst, to).start()

        @pl.when(to == me)
        def _():
            keep(kind, src, dst).start()

    loads = [
        pltpu.make_async_copy(src, dst, local_sem.at[i])
        for i, (src, dst) in enumerate([(wq, wq_v), (wk, wk_v), (wv, wv_v), (wg, wg_v)])
    ]

    barrier = pltpu.get_barrier_semaphore()

    @pl.loop(1, n_seq)
    def _(d):
        pl.semaphore_signal(barrier, inc=1, device_id=(peer(d), core), device_id_type=MESH)

    pl.semaphore_signal(barrier, inc=1, device_id=(me, 1 - core), device_id_type=MESH)
    pl.semaphore_wait(barrier, n_seq)

    def rim_copy(i, src):
        return pltpu.make_async_remote_copy(
            src_ref=src,
            dst_ref=rim.at[i],
            send_sem=rim_send.at[i],
            recv_sem=rim_recv.at[i],
            device_id=(me + 1, core),
            device_id_type=MESH,
        )

    @pl.when(me < n_seq - 1)
    def _():
        rim_copy(0, wk).start()
        rim_copy(1, wv).start()

    arrays = [(Q, cq), (K, ck), (V, cv), (G, cg)]

    def into(kind, source):
        return taken.at[source, :, kind * DH : (kind + 1) * DH]

    @pl.loop(1, n_seq)
    def _(d):
        to = peer(d)
        send(IDS, ids.at[to], ids_in.at[me], to).start()
        for kind, src in arrays[:3]:
            send(kind, src.at[:, head_cols(to)], into(kind, me), to).start()

    keep(IDS, ids.at[me], ids_in.at[me]).start()
    for kind, src in arrays:
        keep(kind, src.at[:, head_cols(me)], into(kind, me)).start()
    for load in loads:
        load.start()

    @pl.loop(1, n_seq)
    def _(d):
        to = peer(d)
        send(G, cg.at[:, head_cols(to)], into(G, me), to).start()

    earlier = lax.broadcasted_iota(jnp.int32, (n, n), 0) < lax.broadcasted_iota(
        jnp.int32, (n, n), 1
    )
    earlier = jnp.where(earlier, 1.0, 0.0).astype(BF16)

    @pl.loop(0, n_seq)
    def _(b):
        got(IDS, ids_in.at[b], b)
        of_block = ids_in[b]
        member = hits_of(of_block, clusters)
        rank = jnp.sum(member.astype(F32) * nn(member, earlier), axis=0, keepdims=True)
        slots[b] = of_block * cap + rank.astype(jnp.int32)

    for load in loads:
        load.wait()

    @pl.when(me > 0)
    def _():
        for i in range(2):
            pltpu.make_async_copy(rim.at[i], rim.at[i], rim_recv.at[i]).wait()

    @pl.when(me == 0)
    def _():
        rim[...] = jnp.zeros_like(rim)

    pair[0] = jnp.zeros((8, n), F32)

    @pl.loop(0, heads)
    def _(h):
        cols = head_cols(h)
        keys = jnp.concatenate([rim[0, :, cols], wk_v[:, cols]], axis=0)
        vals = jnp.concatenate([rim[1, :, cols], wv_v[:, cols]], axis=0)
        prob = window_prob(factor, wq_v[:, cols], keys)
        attn = nn(prob.astype(BF16), vals).astype(BF16)
        attn_win[:, cols] = attn
        gained = wg_v[:, cols].astype(F32) * w_gain[:, cols]
        pair[0] += stat_rows(attn.astype(F32), gained)

    @pl.loop(0, n_seq)
    def _(b):
        for kind in (Q, K, V):
            got(kind, into(kind, b), b)
        at = pl.ds(pl.multiple_of(b * cap, cap), cap)
        values = jnp.concatenate([taken[b, :, : 3 * DH], jnp.ones((n, DH), BF16)], axis=1)
        rows = nn(hits_of(slots[b], pool), values)
        held[:, at, :] = rows.reshape(clusters, cap, 4 * DH)

    row = lax.broadcasted_iota(jnp.int32, (members, members), 0)
    col = lax.broadcasted_iota(jnp.int32, (members, members), 1)
    lane = lax.broadcasted_iota(jnp.int32, (members, DH), 1)
    pick = jnp.where(lane == 0, BIG, 0.0).astype(BF16)

    @pl.loop(0, clusters // group)
    def _(g):
        each = [g * group + i for i in range(group)]
        scores = []
        for c in each:
            q = jnp.concatenate([held[c, :, :DH].astype(BF16), pick], axis=1)
            live = (held[c, :, 3 * DH :] - 1.0).astype(BF16)
            k = jnp.concatenate([held[c, :, DH : 2 * DH].astype(BF16), live], axis=1)
            scores.append(jnp.where(col <= row, nt(q, k), -jnp.inf))
        grown = []
        for s in scores:
            top = jnp.max(s, axis=-1, keepdims=True)
            grown.append(jnp.exp2((s - top) * (factor * LOG2E)))
        weights = []
        for c, e in zip(each, grown):
            prob = e * (1.0 / jnp.sum(e, axis=-1, keepdims=True))
            probs[c] = prob
            weights.append(prob.astype(BF16))
        for c, w in zip(each, weights):
            outs[c] = nn(w, held[c, :, 2 * DH : 3 * DH].astype(BF16)).astype(BF16).astype(F32)

    gain = c_gain[:, head_cols(me)]

    @pl.loop(0, n_seq)
    def _(d):
        b = peer(d + 1)
        at = pl.ds(pl.multiple_of(b * cap, cap), cap)
        rows = outs[:, at, :].reshape(pool, DH).astype(BF16)
        attn = nn(hits_by_token(slots[b], pool), rows)
        attn_own[b] = attn.astype(BF16)
        got(G, into(G, b), b)
        gained = taken[b, :, 3 * DH :].astype(F32) * gain
        part_out[b] = stat_rows(attn, gained)
        deliver(PART, part_out.at[b], part_in.at[me], b)
        deliver(ATTN, attn_own.at[b], attn_home.at[:, head_cols(me)], b)

    @pl.loop(0, n_seq)
    def _(b):
        got(PART, part_in.at[b], b)
        pair[0] += part_in[b]

    swap = pltpu.make_async_remote_copy(
        src_ref=pair.at[0],
        dst_ref=pair.at[1],
        send_sem=pair_sem.at[0],
        recv_sem=pair_sem.at[1],
        device_id=(me, 1 - core),
        device_id_type=MESH,
    )
    swap.start()
    swap.wait()
    totals = pair[0] + pair[1]
    inv = 1.0 / jnp.sqrt(totals[0:1] / feat_width + EPSILON)
    coef = inv * inv * inv * totals[1:2] / feat_width
    index = lax.broadcasted_iota(jnp.int32, (8, n), 0)
    stat_own[...] = jnp.where(index == 0, inv, coef)

    @pl.loop(0, n_seq)
    def _(d):
        deliver(STAT, stat_own, stats.at[me], peer(d + 1))

    @pl.loop(0, n_seq)
    def _(b):
        got(STAT, stats.at[b], b)
        by_token = stats[b].T
        gained = taken[b, :, 3 * DH :].astype(F32) * gain
        dout = by_token[:, 0:1] * gained - by_token[:, 1:2] * attn_own[b].astype(F32)
        rows = nn(hits_of(slots[b], pool), dout.astype(BF16))
        at = pl.ds(pl.multiple_of(b * cap, cap), cap)
        held[:, at, 3 * DH :] = rows.reshape(clusters, cap, DH)

    @pl.loop(0, clusters // group)
    def _(g):
        each = [g * group + i for i in range(group)]
        slopes = []
        for c in each:
            grad = held[c, :, 3 * DH :]
            v = held[c, :, 2 * DH : 3 * DH].astype(BF16)
            row_dot = jnp.sum(grad * outs[c], axis=-1, keepdims=True)
            slopes.append(nt(grad.astype(BF16), v) - row_dot)
        changes = [(probs[c] * s).astype(BF16) for c, s in zip(each, slopes)]
        for c, change in zip(each, changes):
            q, k = held[c, :, :DH].astype(BF16), held[c, :, DH : 2 * DH].astype(BF16)
            grad = held[c, :, 3 * DH :].astype(BF16)
            held[c, :, :DH] = nn(change, k) * factor
            held[c, :, DH : 2 * DH] = tn(change, q) * factor
            held[c, :, 2 * DH : 3 * DH] = tn(probs[c].astype(BF16), grad)

    homes = [(DQ, clu_dq), (DK, clu_dk), (DV, clu_dv)]

    @pl.loop(0, n_seq)
    def _(d):
        b = peer(d + 1)
        at = pl.ds(pl.multiple_of(b * cap, cap), cap)
        rows = held[:, at, : 3 * DH].reshape(pool, 3 * DH).astype(BF16)
        taken[b, :, : 3 * DH] = nn(hits_by_token(slots[b], pool), rows).astype(BF16)
        for i, (kind, home) in enumerate(homes):
            deliver(kind, into(i, b), home.at[:, head_cols(me)], b)

    @pl.loop(0, n_seq)
    def _(b):
        got(ATTN, attn_home.at[:, head_cols(b)], b)

    @pl.when(me < n_seq - 1)
    def _():
        rim_copy(0, wk).wait_send()
        rim_copy(1, wv).wait_send()

    def back_copy(i):
        cols = slice(i * (heads // 4) * DH, (i + 1) * (heads // 4) * DH)
        return pltpu.make_async_remote_copy(
            src_ref=rim.at[:, :, cols],
            dst_ref=rim_back.at[:, :, cols],
            send_sem=rim_send.at[2 + i],
            recv_sem=rim_recv.at[2 + i],
            device_id=(me - 1, core),
            device_id_type=MESH,
        )

    by_token = stat_own[...].T
    inv_col, coef_col = by_token[:, 0:1], by_token[:, 1:2]
    for i in range(4):

        @pl.loop(i * (heads // 4), (i + 1) * (heads // 4))
        def _(h):
            cols = head_cols(h)
            q = wq_v[:, cols]
            keys = jnp.concatenate([rim[0, :, cols], wk_v[:, cols]], axis=0)
            vals = jnp.concatenate([rim[1, :, cols], wv_v[:, cols]], axis=0)
            attn = attn_win[:, cols].astype(F32)
            gained = wg_v[:, cols].astype(F32) * w_gain[:, cols]
            grad = (inv_col * gained - coef_col * attn).astype(BF16)
            prob = window_prob(factor, q, keys)
            row_dot = jnp.sum(grad.astype(F32) * attn, axis=-1, keepdims=True)
            change = (prob * (nt(grad, vals) - row_dot)).astype(BF16)
            wq_v[:, cols] = (nn(change, keys) * factor).astype(BF16)
            dk = tn(change, q)
            dv = tn(prob.astype(BF16), grad)
            rim[0, :, cols] = dk[:WINDOW].astype(BF16)
            rim[1, :, cols] = dv[:WINDOW].astype(BF16)
            dk_own[:, cols] = dk[WINDOW:]
            dv_own[:, cols] = dv[WINDOW:]
            attn_win[:, cols] = (attn * inv_col * w_gain[:, cols]).astype(BF16)
            clu = attn_home[:, cols].astype(F32)
            attn_home[:, cols] = (clu * inv_col * c_gain[:, cols]).astype(BF16)

        @pl.when(me > 0)
        def _():
            back_copy(i).start()

    stores = [
        pltpu.make_async_copy(src, dst, local_sem.at[4 + i])
        for i, (src, dst) in enumerate(
            [
                (attn_win, win_normed),
                (attn_home, clu_normed),
                (wq_v, win_dq),
                (wk_v, win_dk),
                (wv_v, win_dv),
            ]
        )
    ]
    for store in stores[:3]:
        store.start()

    @pl.when(me < n_seq - 1)
    def _():
        for i in range(4):
            cols = slice(i * (heads // 4) * DH, (i + 1) * (heads // 4) * DH)
            view = rim_back.at[:, :, cols]
            pltpu.make_async_copy(view, view, rim_recv.at[2 + i]).wait()

    @pl.when(me == n_seq - 1)
    def _():
        rim_back[...] = jnp.zeros_like(rim_back)

    @pl.loop(0, heads)
    def _(h):
        cols = head_cols(h)
        wk_v[:, cols] = ((dk_own[:, cols] + rim_back[0, :, cols].astype(F32)) * factor).astype(BF16)
        wv_v[:, cols] = (dv_own[:, cols] + rim_back[1, :, cols].astype(F32)).astype(BF16)

    for store in stores[3:]:
        store.start()

    @pl.when(me > 0)
    def _():
        for i in range(4):
            back_copy(i).wait_send()

    @pl.loop(1, n_seq)
    def _(d):
        to = peer(d)
        for kind, src in arrays:
            sent(kind, src.at[:, head_cols(to)], to)
        sent(IDS, ids.at[to], to)
        sent(PART, part_out.at[to], to)
        sent(ATTN, attn_own.at[to], to)
        sent(STAT, stat_own, to)
        for i, (kind, home) in enumerate(homes):
            sent(kind, into(i, to), to)

    @pl.loop(0, n_seq)
    def _(b):
        for kind, home in homes:
            got(kind, home.at[:, head_cols(b)], b)

    for store in stores:
        store.wait()


def layer(*arrays):
    win_query, cluster_ids = arrays[0], arrays[6]
    n, wide = win_query.shape
    sources = lax.axis_size("seq")
    cap = SLOTS // sources
    clusters = sources * (2 * n // SLOTS)
    members = sources * cap
    heads = wide // DH
    given = list(arrays)
    given[6] = cluster_ids[:, None, :]
    given[7], given[8] = arrays[7][None, :], arrays[8][None, :]
    anywhere = pl.BlockSpec(memory_space=pl.ANY)
    vmem = pl.BlockSpec(memory_space=pltpu.VMEM)
    group = 16 if clusters % 16 == 0 else clusters
    return pl.pallas_call(
        functools.partial(layer_kernel, DH ** (-0.5), cap, group),
        in_specs=[anywhere] * 6 + [vmem] * 3 + [anywhere] * 2,
        out_specs=[anywhere] * 8,
        out_shape=[jax.ShapeDtypeStruct((n, wide), BF16)] * 8,
        scratch_shapes=[
            pltpu.VMEM((sources, n, 4 * DH), BF16),
            pltpu.VMEM((sources, 1, n), jnp.int32),
            pltpu.VMEM((sources, 1, n), jnp.int32),
        ]
        + [pltpu.VMEM((n, wide), BF16)] * 4
        + [pltpu.VMEM((2, n, wide), BF16)] * 2
        + [pltpu.VMEM((n, wide), BF16)] * 2
        + [
            pltpu.VMEM((sources, n, DH), BF16),
            pltpu.VMEM((clusters, members, 4 * DH), F32),
            pltpu.VMEM((clusters, members, DH), F32),
            pltpu.VMEM((clusters, members, members), F32),
            pltpu.VMEM((n, wide), F32),
            pltpu.VMEM((n, wide), F32),
            pltpu.VMEM((sources, 8, n), F32),
            pltpu.VMEM((sources, 8, n), F32),
            pltpu.VMEM((2, 8, n), F32),
            pltpu.VMEM((8, n), F32),
            pltpu.VMEM((sources, 8, n), F32),
            pltpu.SemaphoreType.DMA((11, sources)),
            pltpu.SemaphoreType.DMA((11, sources)),
            pltpu.SemaphoreType.DMA((6,)),
            pltpu.SemaphoreType.DMA((6,)),
            pltpu.SemaphoreType.DMA((2,)),
            pltpu.SemaphoreType.DMA((9,)),
        ],
        cost_estimate=pl.CostEstimate(
            flops=14 * n * 2 * n * wide, bytes_accessed=16 * n * wide * 2, transcendentals=0
        ),
        compiler_params=pltpu.CompilerParams(
            vmem_limit_bytes=56 << 20, collective_id=0, has_side_effects=True
        ),
    )(*given)


def solution(mesh):
    sources, split = mesh.shape["seq"], mesh.shape["head"]
    whole_heads = HC // split == sources and SLOTS // sources % 8 == 0 and split == 2
    return jax.shard_map(
        layer if whole_heads else body,
        mesh=mesh,
        in_specs=(P("seq", "head"),) * 6
        + (P("head", "seq"), P("head"), P("head"))
        + (P("seq", "head"),) * 2,
        out_specs=(P("seq", "head"),) * 8,
        check_vma=False,
    )
```

```python
import functools

import jax
import jax.numpy as jnp
from jax import lax
from jax.experimental import pallas as pl
from jax.experimental.pallas import tpu as pltpu
from jax.sharding import PartitionSpec as P

HW = 32
HC = 32
DH = 128
WINDOW = 256
SLOTS = 128
CHUNKS = 2

EPSILON = 1e-06
F32 = jnp.float32
BF16 = jnp.bfloat16


def from_behind(block, axis, distance):
    devices = range(lax.axis_size(axis))
    route = [(i - distance, i) for i in devices if i - distance in devices]
    return lax.ppermute(block, axis, route)


def nt(a, b):
    return lax.dot_general(a, b, (((1,), (1,)), ((), ())), preferred_element_type=F32)


def tn(a, b):
    return lax.dot_general(a, b, (((0,), (0,)), ((), ())), preferred_element_type=F32)


def nn(a, b):
    return jnp.dot(a, b, preferred_element_type=F32)


def one_hot(slot_ref, pool):
    n = slot_ref.shape[-1]
    hit = lax.broadcasted_iota(jnp.int32, (pool, n), 0) == slot_ref[0]
    return jnp.where(hit, 1.0, 0.0).astype(BF16)


def normalized(scores, allowed):
    masked = jnp.where(allowed, scores, -jnp.inf)
    grown = jnp.exp(masked - jnp.max(masked, axis=-1, keepdims=True))
    return grown * (1.0 / jnp.sum(grown, axis=-1, keepdims=True))


def call(kernel, grid, in_specs, out_specs, out_shape, flops, size, **more):
    return pl.pallas_call(
        kernel,
        grid=grid,
        in_specs=in_specs,
        out_specs=out_specs,
        out_shape=out_shape,
        cost_estimate=pl.CostEstimate(flops=flops, bytes_accessed=size, transcendentals=0),
        compiler_params=pltpu.CompilerParams(vmem_limit_bytes=48 << 20),
        **more,
    )


def dispatch_kernel(*refs):
    slot_ref, value_refs, out_ref = refs[0], refs[1:-1], refs[-1]
    picked = one_hot(slot_ref, out_ref.shape[0])
    for i, ref in enumerate(value_refs):
        out_ref[:, i * DH : (i + 1) * DH] = nn(picked, ref[...]).astype(BF16)


def dispatch(slot_at, values, first, count, pool):
    n = slot_at.shape[-1]
    wide = len(values) * DH
    return call(
        dispatch_kernel,
        (count,),
        [pl.BlockSpec((1, 1, n), lambda h: (h + first, 0, 0))]
        + [pl.BlockSpec((n, DH), lambda h: (0, h + first)) for _ in values],
        pl.BlockSpec((pool, wide), lambda h: (0, h)),
        jax.ShapeDtypeStruct((pool, count * wide), BF16),
        2 * count * pool * n * wide,
        2 * count * (pool + n) * wide,
    )(slot_at, *values)


def collect_kernel(n_out, *refs):
    slot_ref, rows_ref, out_refs = refs[0], refs[1], refs[-n_out:]
    picked = one_hot(slot_ref, rows_ref.shape[0])
    merged = tn(picked, rows_ref[...]).astype(BF16)
    for i, ref in enumerate(out_refs):
        ref[...] = merged[:, i * DH : (i + 1) * DH]


def collect(slot_at, rows, first, count, n_out, earlier):
    n = slot_at.shape[-1]
    pool = rows.shape[0]
    heads = slot_at.shape[0]
    wide = n_out * DH
    return call(
        functools.partial(collect_kernel, n_out),
        (count,),
        [
            pl.BlockSpec((1, 1, n), lambda h: (h + first, 0, 0)),
            pl.BlockSpec((pool, wide), lambda h: (0, h)),
        ]
        + [pl.BlockSpec(memory_space=pl.ANY) for _ in earlier],
        [pl.BlockSpec((n, DH), lambda h: (0, h + first))] * n_out,
        [jax.ShapeDtypeStruct((n, heads * DH), BF16)] * n_out,
        2 * count * pool * n * wide,
        2 * count * (pool + n) * wide,
        input_output_aliases={2 + i: i for i in range(len(earlier))},
    )(slot_at, rows, *earlier)


class Rows:
    def __init__(self, sources, owned, cap):
        self.sources, self.owned, self.cap = sources, owned, cap
        self.aligned = cap % 8 == 0

    def selector(self, c):
        members = self.sources * self.cap
        layout = (members, members * self.owned)
        member = lax.broadcasted_iota(jnp.int32, layout, 0)
        row = lax.broadcasted_iota(jnp.int32, layout, 1)
        want = member // self.cap * (self.cap * self.owned) + c * self.cap + member % self.cap
        return jnp.where(row == want, 1.0, 0.0).astype(BF16)

    def split(self, rows):
        members = self.sources * self.cap
        if not self.aligned:
            return [nn(self.selector(c), rows).astype(BF16) for c in range(self.owned)]
        wide = rows.shape[1]
        four = rows.astype(F32).reshape(self.sources, self.owned, self.cap, wide)
        return [four[:, c].reshape(members, wide).astype(BF16) for c in range(self.owned)]

    def join(self, parts):
        wide = parts[0].shape[1]
        pool = self.sources * self.cap * self.owned
        if not self.aligned:
            total = jnp.zeros((pool, wide), F32)
            for c, part in enumerate(parts):
                total = total + tn(self.selector(c), part.astype(BF16))
            return total.astype(BF16)
        shaped = [p.reshape(self.sources, 1, self.cap, wide) for p in parts]
        return jnp.concatenate(shaped, axis=1).reshape(pool, wide).astype(BF16)


def cluster_allowed(live_ref, c, members):
    row = lax.broadcasted_iota(jnp.int32, (members, members), 0)
    col = lax.broadcasted_iota(jnp.int32, (members, members), 1)
    live = jnp.broadcast_to(live_ref[0, c : c + 1, :], (members, members)) > 0.5
    return (live & (col <= row)) | (col == row)


def owner_fwd_kernel(rows, factor, live_ref, qkv_ref, out_ref):
    members = rows.sources * rows.cap
    parts = []
    for c, qkv in enumerate(rows.split(qkv_ref[...])):
        q, k, v = qkv[:, :DH], qkv[:, DH : 2 * DH], qkv[:, 2 * DH :]
        prob = normalized(nt(q, k) * factor, cluster_allowed(live_ref, c, members))
        parts.append(nn(prob.astype(BF16), v))
    out_ref[...] = rows.join(parts)


def owner_bwd_kernel(rows, factor, live_ref, qkv_ref, attn_ref, grad_ref, out_ref):
    members = rows.sources * rows.cap
    attn_parts = rows.split(attn_ref[...])
    grad_parts = rows.split(grad_ref[...])
    parts = []
    for c, qkv in enumerate(rows.split(qkv_ref[...])):
        q, k, v = qkv[:, :DH], qkv[:, DH : 2 * DH], qkv[:, 2 * DH :]
        grad = grad_parts[c]
        row_dot = jnp.sum(grad.astype(F32) * attn_parts[c].astype(F32), axis=-1, keepdims=True)
        prob = normalized(nt(q, k) * factor, cluster_allowed(live_ref, c, members))
        change = (prob * (nt(grad, v) - row_dot)).astype(BF16)
        dq = nn(change, k) * factor
        dk = tn(change, q) * factor
        dv = tn(prob.astype(BF16), grad)
        parts.append(jnp.concatenate([dq, dk, dv], axis=1))
    out_ref[...] = rows.join(parts)


def owner_call(kernel, rows, factor, live, first, arrays, n_out):
    pool = arrays[0].shape[0]
    count = arrays[0].shape[1] // (3 * DH)
    members = rows.sources * rows.cap
    wides = [a.shape[1] // count for a in arrays]
    return call(
        functools.partial(kernel, rows, factor),
        (count,),
        [pl.BlockSpec((1, rows.owned, members), lambda h: (h + first, 0, 0))]
        + [pl.BlockSpec((pool, w), lambda h: (0, h)) for w in wides],
        pl.BlockSpec((pool, n_out * DH), lambda h: (0, h)),
        jax.ShapeDtypeStruct((pool, count * n_out * DH), BF16),
        12 * count * pool * members * DH,
        2 * count * pool * (sum(wides) + n_out * DH),
    )(live, *arrays)


def window_prob(factor, q, keys):
    n = q.shape[0]
    row = lax.broadcasted_iota(jnp.int32, (n, n + WINDOW), 0)
    col = lax.broadcasted_iota(jnp.int32, (n, n + WINDOW), 1)
    gap = row + WINDOW - col
    lowest = jnp.where(lax.axis_index("seq") > 0, 0, WINDOW)
    allowed = (gap >= 0) & (gap < WINDOW) & (col >= lowest)
    return normalized(nt(q, keys) * factor, allowed)


def window_fwd_kernel(factor, q_ref, kp_ref, k_ref, vp_ref, v_ref, out_ref):
    keys = jnp.concatenate([kp_ref[0], k_ref[...]], axis=0)
    vals = jnp.concatenate([vp_ref[0], v_ref[...]], axis=0)
    prob = window_prob(factor, q_ref[...], keys)
    out_ref[...] = nn(prob.astype(BF16), vals).astype(BF16)


def window_bwd_kernel(
    factor, q_ref, kp_ref, k_ref, vp_ref, v_ref, attn_ref, grad_ref, dq_ref, dk_ref, dv_ref, rim_ref
):
    q, grad = q_ref[...], grad_ref[...]
    keys = jnp.concatenate([kp_ref[0], k_ref[...]], axis=0)
    vals = jnp.concatenate([vp_ref[0], v_ref[...]], axis=0)
    prob = window_prob(factor, q, keys)
    row_dot = jnp.sum(grad.astype(F32) * attn_ref[...].astype(F32), axis=-1, keepdims=True)
    change = (prob * (nt(grad, vals) - row_dot)).astype(BF16)
    dq_ref[...] = (nn(change, keys) * factor).astype(BF16)
    dk = tn(change, q)
    dv = tn(prob.astype(BF16), grad)
    rim_ref[0] = dk[:WINDOW].astype(BF16)
    rim_ref[1] = dv[:WINDOW].astype(BF16)
    dk_ref[...] = dk[WINDOW:]
    dv_ref[...] = dv[WINDOW:]


def window_specs(n):
    here = pl.BlockSpec((n, DH), lambda h: (0, h))
    key = pl.BlockSpec((1, n, DH), lambda h: (0, 0, h))
    val = pl.BlockSpec((1, n, DH), lambda h: (1, 0, h))
    return here, key, val


def window_fwd(factor, query, key, value, before):
    n, wide = query.shape
    here, rim_key, rim_val = window_specs(n)
    return call(
        functools.partial(window_fwd_kernel, factor),
        (wide // DH,),
        [here, rim_key, here, rim_val, here],
        here,
        jax.ShapeDtypeStruct((n, wide), BF16),
        4 * n * 2 * n * wide,
        12 * n * wide,
    )(query, before, key, before, value)


def window_bwd(factor, query, key, value, before, attn, grad):
    n, wide = query.shape
    here, rim_key, rim_val = window_specs(n)
    return call(
        functools.partial(window_bwd_kernel, factor),
        (wide // DH,),
        [here, rim_key, here, rim_val, here, here, here],
        [here, here, here, pl.BlockSpec((2, n, DH), lambda h: (0, 0, h))],
        [
            jax.ShapeDtypeStruct((n, wide), BF16),
            jax.ShapeDtypeStruct((n, wide), F32),
            jax.ShapeDtypeStruct((n, wide), F32),
            jax.ShapeDtypeStruct((2, n, wide), BF16),
        ],
        10 * n * 2 * n * wide,
        28 * n * wide,
    )(query, before, key, before, value, attn, grad)


def body(
    win_query,
    win_key,
    win_value,
    clu_query,
    clu_key,
    clu_value,
    cluster_ids,
    win_gain,
    clu_gain,
    win_out_grad,
    clu_out_grad,
):
    n_rows = win_query.shape[0]
    factor = DH ** (-0.5)
    feat_width = (HW + HC) * DH
    sources = lax.axis_size("seq")
    n_cap = SLOTS // sources
    owned_count = 2 * n_rows // SLOTS
    pool_size = 2 * n_rows
    clu_heads = clu_query.shape[1] // DH
    rows = Rows(sources, owned_count, n_cap)

    def exchange(values):
        shaped = values.reshape(sources, pool_size // sources, values.shape[1])
        moved = lax.all_to_all(shaped, "seq", split_axis=0, concat_axis=0, tiled=True)
        return moved.reshape(values.shape)

    row_ids = lax.broadcasted_iota(jnp.int32, (n_rows, n_rows), 0)
    col_ids = lax.broadcasted_iota(jnp.int32, (n_rows, n_rows), 1)
    same_cluster = (cluster_ids[:, :, None] == cluster_ids[:, None, :]) & (col_ids < row_ids)
    rank_in = jnp.sum(same_cluster.astype(jnp.int32), axis=-1)
    slot_at = (cluster_ids * n_cap + rank_in)[:, None, :]

    n_clusters = sources * owned_count
    every = lax.broadcasted_iota(jnp.int32, (n_clusters, clu_heads, n_rows), 0)
    counts = jnp.sum((cluster_ids[None] == every).astype(F32), axis=-1)
    counts = counts.reshape(sources, owned_count, clu_heads)
    counts = lax.all_to_all(counts, "seq", split_axis=0, concat_axis=0, tiled=True)
    slot_pos = lax.broadcasted_iota(F32, (clu_heads, owned_count, sources, n_cap), 3)
    live = (slot_pos < counts.transpose(2, 1, 0)[..., None]).astype(F32)
    live = live.reshape(clu_heads, owned_count, sources * n_cap)

    chunks = CHUNKS if clu_heads % CHUNKS == 0 else 1
    per = clu_heads // chunks
    starts = [i * per for i in range(chunks)]

    held = [
        exchange(dispatch(slot_at, [clu_query, clu_key, clu_value], first, per, pool_size))
        for first in starts
    ]
    before = from_behind(jnp.stack([win_key, win_value]), "seq", 1)
    attn_win = window_fwd(factor, win_query, win_key, win_value, before)

    attn_held = [
        owner_call(owner_fwd_kernel, rows, factor, live, first, [qkv], 1)
        for first, qkv in zip(starts, held)
    ]
    attn_back = [exchange(part) for part in attn_held]
    attn_clu = ()
    for first, part in zip(starts, attn_back):
        attn_clu = collect(slot_at, part, first, per, 1, attn_clu)
    attn_clu = attn_clu[0]

    flat_win = attn_win.astype(F32)
    flat_clu = attn_clu.astype(F32)
    grad_win = win_out_grad.astype(F32) * win_gain
    grad_clu = clu_out_grad.astype(F32) * clu_gain
    totals = jnp.stack(
        [
            jnp.sum(flat_win * flat_win, axis=1) + jnp.sum(flat_clu * flat_clu, axis=1),
            jnp.sum(grad_win * flat_win, axis=1) + jnp.sum(grad_clu * flat_clu, axis=1),
        ]
    )
    totals = lax.psum(totals, "head")
    sq_total, dot_total = totals[0], totals[1]
    inv_rms = 1.0 / jnp.sqrt(sq_total / feat_width + EPSILON)
    coef_rows = inv_rms**3 * dot_total / feat_width
    dout_clu = (inv_rms[:, None] * grad_clu - coef_rows[:, None] * flat_clu).astype(BF16)
    dout_win = (inv_rms[:, None] * grad_win - coef_rows[:, None] * flat_win).astype(BF16)
    win_normed = (flat_win * inv_rms[:, None] * win_gain).astype(BF16)
    clu_normed = (flat_clu * inv_rms[:, None] * clu_gain).astype(BF16)

    grad_held = [
        exchange(dispatch(slot_at, [dout_clu], first, per, pool_size)) for first in starts
    ]
    win_dq, key_own, val_own, rim = window_bwd(
        factor, win_query, win_key, win_value, before, attn_win, dout_win
    )
    after_rim = from_behind(rim, "seq", -1)

    clu_grads = ()
    sent = [
        owner_call(owner_bwd_kernel, rows, factor, live, first, [qkv, part, grad], 3)
        for first, qkv, part, grad in zip(starts, held, attn_held, grad_held)
    ]
    home = [exchange(part) for part in sent]
    win_dk = ((key_own + after_rim[0]) * factor).astype(BF16)
    win_dv = (val_own + after_rim[1]).astype(BF16)
    for first, part in zip(starts, home):
        clu_grads = collect(slot_at, part, first, per, 3, clu_grads)
    return (win_normed, clu_normed, win_dq, win_dk, win_dv, *clu_grads)


BIG = 1e30
MESH = pl.DeviceIdType.MESH
LOG2E = 1.4426950408889634


def hits_of(slot, pool):
    n = slot.shape[-1]
    hit = lax.broadcasted_iota(jnp.int32, (pool, n), 0) == slot
    return jnp.where(hit, 1.0, 0.0).astype(BF16)


def hits_by_token(slot, pool):
    n = slot.shape[-1]
    column = jnp.broadcast_to(slot.astype(F32), (8, n)).T[:, :1].astype(jnp.int32)
    hit = lax.broadcasted_iota(jnp.int32, (n, pool), 1) == column
    return jnp.where(hit, 1.0, 0.0).astype(BF16)


def stat_rows(attn, gained):
    wide = attn.shape[1]
    both = jnp.concatenate([attn * attn, gained * attn], axis=1)
    row = lax.broadcasted_iota(jnp.int32, (8, 2 * wide), 0)
    col = lax.broadcasted_iota(jnp.int32, (8, 2 * wide), 1)
    pick = jnp.where(col // wide == row, 1.0, 0.0).astype(BF16)
    high = both.astype(BF16)
    low = (both - high.astype(F32)).astype(BF16)
    return nt(pick, high) + nt(pick, low)


def head_cols(h):
    return pl.ds(pl.multiple_of(h * DH, DH), DH)


def columns(first, count):
    return pl.ds(pl.multiple_of(first * DH, DH), count * DH)


def at_lanes(shape, values):
    lane = lax.broadcasted_iota(jnp.int32, shape, 1)
    total = jnp.zeros(shape, F32)
    for i, value in enumerate(values):
        total = jnp.where(lane == i, value, total)
    return total


def in_parts(x, count):
    parts = []
    for _ in range(count - 1):
        parts.append(x.astype(BF16).astype(F32))
        x = x - parts[-1]
    return parts + [x]


def layer_kernel(
    factor,
    cap,
    group,
    plane,
    wq,
    wk,
    wv,
    cq,
    ck,
    cv,
    ids,
    w_gain,
    c_gain,
    wg,
    cg,
    win_normed,
    clu_normed,
    win_dq,
    win_dk,
    win_dv,
    clu_dq,
    clu_dk,
    clu_dv,
    taken,
    ids_in,
    slots,
    wq_v,
    wk_v,
    wv_v,
    wg_v,
    rim,
    rim_back,
    relay,
    relay_back,
    attn_win,
    attn_home,
    attn_own,
    x_in,
    d_in,
    x_out,
    d_out,
    rows16,
    xq16,
    work,
    acc,
    probs,
    probs_x,
    lse_own,
    lse_out,
    lse_in,
    dot_out,
    dot_in,
    shares,
    part_out,
    part_in,
    pair,
    stat_own,
    stats,
    send_sem,
    recv_sem,
    rim_send,
    rim_recv,
    relay_sem,
    pair_sem,
    local_sem,
):
    me, core = lax.axis_index("seq"), lax.axis_index("head")
    n_seq = lax.axis_size("seq")
    near = n_seq // 2
    half, t = me // near, lax.rem(me, near)
    base = half * near
    early, late = half == 0, half == 1
    n = wq.shape[0]
    heads = wq.shape[1] // DH
    each = heads // near
    pairs = rows16.shape[0] // each
    members = rows16.shape[1]
    part = members // 2
    clusters = 2 * pairs
    pool = clusters * cap
    feat_width = (HW + HC) * DH
    (Q, K, V, G, IDS, IDSX, QX, OX, LX, PART, ATTN, STAT, DX, RX, DQX, DQ, DK, DV) = range(18)

    def peer(d):
        return lax.rem(t + d, near)

    def remote(kind, src, dst, mine, theirs, to):
        return pltpu.make_async_remote_copy(
            src_ref=src,
            dst_ref=dst,
            send_sem=send_sem.at[kind, mine],
            recv_sem=recv_sem.at[kind, theirs],
            device_id=(to, core),
            device_id_type=MESH,
        )

    def got(kind, dst, index):
        pltpu.make_async_copy(dst, dst, recv_sem.at[kind, index]).wait()

    def sent(kind, src, index):
        pltpu.make_async_copy(src, src, send_sem.at[kind, index]).wait()

    def deliver(kind, src, dst, b, mine, theirs):
        @pl.when(b != t)
        def _():
            remote(kind, src, dst, mine, theirs, base + b).start()

        @pl.when(b == t)
        def _():
            pltpu.make_async_copy(src, dst, recv_sem.at[kind, theirs]).start()

    loads = [
        pltpu.make_async_copy(src, dst, local_sem.at[i])
        for i, (src, dst) in enumerate([(wq, wq_v), (wk, wk_v), (wv, wv_v), (wg, wg_v)])
    ]

    barrier = pltpu.get_barrier_semaphore()

    @pl.loop(1, n_seq)
    def _(d):
        to = lax.rem(me + d, n_seq)
        pl.semaphore_signal(barrier, inc=1, device_id=(to, core), device_id_type=MESH)

    pl.semaphore_signal(barrier, inc=1, device_id=(me, 1 - core), device_id_type=MESH)
    pl.semaphore_wait(barrier, n_seq)

    spot, level = lax.rem(me, plane), me // plane
    quarter = heads // 4 * DH
    span = [slice(j * quarter, (j + 1) * quarter) for j in range(4)]
    crosses = (spot == plane - 1) & (me < n_seq - 1)
    straight = (spot != plane - 1) & (me < n_seq - 1)
    relays = (spot != plane - 1) & (me < n_seq - plane)

    def rim_copy(i, j, src, dst, sem, to):
        return pltpu.make_async_remote_copy(
            src_ref=src,
            dst_ref=dst,
            send_sem=rim_send.at[i, j],
            recv_sem=sem,
            device_id=(to, core),
            device_id_type=MESH,
        )

    def rim_first(i, j, by_relay):
        src = (wk, wv)[i].at[:, span[j]]
        if by_relay:
            return rim_copy(i, j, src, relay.at[i], relay_sem.at[i], level * plane + j)
        return rim_copy(i, j, src, rim.at[i, :, span[j]], rim_recv.at[i, j], me + 1)

    @pl.when(crosses)
    def _():
        for j in range(4):
            for i in range(2):
                rim_first(i, j, j < plane - 1).start()

    @pl.when(straight)
    def _():
        for j in range(4):
            for i in range(2):
                rim_first(i, j, False).start()

    arrays = [(Q, cq), (K, ck), (V, cv), (G, cg)]

    def into(kind, source):
        return taken.at[source, :, kind * each * DH : (kind + 1) * each * DH]

    def of_head(kind, hh):
        return slice((kind * each + hh) * DH, (kind * each + hh + 1) * DH)

    @pl.when(late)
    def _():
        @pl.loop(0, near)
        def _(d):
            to = peer(d)
            view = ids.at[pl.ds(to * each, each)]
            remote(IDSX, view, ids_in.at[near + t], to, t, to).start()
            src = cq.at[:, columns(to * each, 1)]
            remote(QX, src, x_in.at[t, :, :DH], to, t, to).start()

    @pl.loop(1, near)
    def _(d):
        to = peer(d)
        remote(IDS, ids.at[pl.ds(to * each, each)], ids_in.at[t], to, t, base + to).start()
        for kind, src in arrays[:3]:
            view = src.at[:, columns(to * each, each)]
            remote(kind, view, into(kind, t), to, t, base + to).start()

    pltpu.make_async_copy(
        ids.at[pl.ds(t * each, each)], ids_in.at[t], recv_sem.at[IDS, t]
    ).start()
    for kind, src in arrays:
        view = src.at[:, columns(t * each, each)]
        pltpu.make_async_copy(view, into(kind, t), recv_sem.at[kind, t]).start()
    for load in loads:
        load.start()

    @pl.when(late)
    def _():
        for hh in range(1, each):

            @pl.loop(0, near)
            def _(d):
                to = peer(d)
                src = cq.at[:, columns(to * each + hh, 1)]
                dst = x_in.at[t, :, hh * DH : (hh + 1) * DH]
                remote(QX, src, dst, hh * near + to, hh * near + t, to).start()

    @pl.loop(1, near)
    def _(d):
        to = peer(d)
        view = cg.at[:, columns(to * each, each)]
        remote(G, view, into(G, t), to, t, base + to).start()

    earlier = lax.broadcasted_iota(jnp.int32, (n, n), 0) < lax.broadcasted_iota(
        jnp.int32, (n, n), 1
    )
    earlier = jnp.where(earlier, 1.0, 0.0).astype(BF16)

    def place(b):
        for hh in range(each):
            of_block = ids_in[b, hh]
            member = hits_of(of_block, clusters)
            rank = jnp.sum(member.astype(F32) * nn(member, earlier), axis=0, keepdims=True)
            slots[b, hh] = of_block * cap + rank.astype(jnp.int32)

    @pl.loop(0, near)
    def _(b):
        got(IDS, ids_in.at[b], b)
        place(b)

    @pl.when(early)
    def _():
        @pl.loop(0, near)
        def _(b):
            got(IDSX, ids_in.at[near + b], b)
            place(near + b)

    def pass_on(i, j):
        return pltpu.make_async_remote_copy(
            src_ref=relay.at[i],
            dst_ref=rim.at[i, :, span[j]],
            send_sem=relay_sem.at[4 + i],
            recv_sem=rim_recv.at[i, j],
            device_id=((level + 1) * plane, core),
            device_id_type=MESH,
        )

    for j in range(plane - 1):

        @pl.when(relays & (spot == j))
        def _():
            for i in range(2):
                pltpu.make_async_copy(relay.at[i], relay.at[i], relay_sem.at[i]).wait()
                pass_on(i, j).start()

    def block_rows(b):
        return pl.ds(pl.multiple_of(b * cap, cap), cap)

    def sort_into(ref, hh, b, lanes, rows):
        shaped = rows.reshape(pairs, 2, cap, rows.shape[1])
        ref[hh * pairs : (hh + 1) * pairs, :, block_rows(b), lanes] = shaped

    def sorted_rows(ref, hh, b, lanes):
        rows = ref[hh * pairs : (hh + 1) * pairs, :, block_rows(b), lanes]
        return rows.reshape(pool, rows.shape[3]).astype(BF16)

    def whole(ref, p, lanes):
        return ref[p, :, :, lanes].reshape(members, lanes.stop - lanes.start)

    one, two = slice(0, DH), slice(0, 2 * DH)

    @pl.loop(0, near)
    def _(b):
        for kind in (Q, K, V):
            got(kind, into(kind, b), b)
        for hh in range(each):
            values = jnp.concatenate(
                [taken[b, :, of_head(kind, hh)] for kind in (Q, K, V)]
                + [jnp.ones((n, DH), BF16)],
                axis=1,
            )
            rows = nn(hits_of(slots[b, hh], pool), values)
            sort_into(acc, hh, b, slice(0, 3 * DH), rows[:, : 3 * DH])
            sort_into(work, hh, b, one, rows[:, 3 * DH :])

    row = lax.broadcasted_iota(jnp.int32, (members, members), 0)
    col = lax.broadcasted_iota(jnp.int32, (members, members), 1)
    same = (row // part) == (col // part)
    lane = lax.broadcasted_iota(jnp.int32, (members, DH), 1)
    pick = jnp.where(lane == 0, BIG, 0.0).astype(BF16)
    scale = factor * LOG2E

    def attend(group_of, queries, keys, values, allowed, prob_ref):
        scores = [
            jnp.where(allowed, nt(jnp.concatenate([q, pick], axis=1), k), -jnp.inf)
            for q, k in zip(queries, keys)
        ]
        tops = [jnp.max(s, axis=-1, keepdims=True) for s in scores]
        grown = [jnp.exp2((s - top) * scale) for s, top in zip(scores, tops)]
        sums = [jnp.sum(e, axis=-1, keepdims=True) for e in grown]
        weights = [(e * (1.0 / total)).astype(BF16) for e, total in zip(grown, sums)]
        for p, w, v, top, total in zip(group_of, weights, values, tops, sums):
            prob_ref[p] = w
            lse = top * scale + jnp.log(total) * LOG2E
            out = jnp.concatenate([nn(w, v), at_lanes((members, DH), in_parts(lse, 3))], axis=1)
            work[p] = out.reshape(2, part, 2 * DH)

    @pl.loop(0, rows16.shape[0] // group)
    def _(g):
        group_of = [g * group + i for i in range(group)]
        queries, keys, values = [], [], []
        for p in group_of:
            q, k, v = (
                whole(acc, p, slice(i * DH, (i + 1) * DH)).astype(BF16) for i in range(3)
            )
            live = (whole(work, p, one) - 1.0).astype(BF16)
            rows16[p, :, :DH] = q
            rows16[p, :, DH : 2 * DH] = k
            rows16[p, :, 2 * DH : 3 * DH] = live
            rows16[p, :, 3 * DH :] = v
            queries.append(q)
            keys.append(jnp.concatenate([k, live], axis=1))
            values.append(v)
        attend(group_of, queries, keys, values, same & (col <= row), probs)

    def by_tokens(hh, b, slot_index):
        rows = sorted_rows(work, hh, b, two)
        return nn(hits_by_token(slots[slot_index, hh], pool), rows)

    @pl.loop(0, near)
    def _(b):
        for hh in range(each):
            back = by_tokens(hh, b, b)
            attn_own[b, :, hh * DH : (hh + 1) * DH] = back[:, :DH].astype(BF16)
            lse_own[hh * near + b] = back[:, DH:].T[:8]

    @pl.when(early)
    def _():
        for hh in range(each):

            @pl.loop(0, near)
            def _(b):
                view = x_in.at[b, :, hh * DH : (hh + 1) * DH]
                got(QX, view, hh * near + b)
                rows = nn(hits_of(slots[near + b, hh], pool), view[...])
                sort_into(work, hh, b, one, rows)

            @pl.loop(0, pairs // group)
            def _(g):
                group_of = [hh * pairs + g * group + i for i in range(group)]
                queries = [whole(work, p, one).astype(BF16) for p in group_of]
                for p, q in zip(group_of, queries):
                    xq16[p] = q
                keys = [rows16[p, :, DH : 3 * DH] for p in group_of]
                values = [rows16[p, :, 3 * DH :] for p in group_of]
                attend(group_of, queries, keys, values, same, probs_x)

            @pl.loop(0, near)
            def _(b):
                back = by_tokens(hh, b, near + b)
                at = hh * near + b
                view = x_out.at[b, :, hh * DH : (hh + 1) * DH]
                view[...] = back[:, :DH].astype(BF16)
                lse_out[at] = back[:, DH:].T[:8]
                dst = x_in.at[b, :, hh * DH : (hh + 1) * DH]
                remote(OX, view, dst, at, at, me + near).start()
                remote(LX, lse_out.at[at], lse_in.at[at], at, at, me + near).start()

    for load in loads:
        load.wait()

    @pl.when(me > 0)
    def _():
        for j in range(4):
            for i in range(2):
                view = rim.at[i, :, span[j]]
                pltpu.make_async_copy(view, view, rim_recv.at[i, j]).wait()

    @pl.when(me == 0)
    def _():
        rim[...] = jnp.zeros_like(rim)

    pair[0] = jnp.zeros((8, n), F32)

    @pl.loop(0, heads)
    def _(h):
        cols = columns(h, 1)
        keys = jnp.concatenate([rim[0, :, cols], wk_v[:, cols]], axis=0)
        vals = jnp.concatenate([rim[1, :, cols], wv_v[:, cols]], axis=0)
        prob = window_prob(factor, wq_v[:, cols], keys)
        attn = nn(prob.astype(BF16), vals).astype(BF16)
        attn_win[:, cols] = attn
        gained = wg_v[:, cols].astype(F32) * w_gain[:, cols]
        pair[0] += stat_rows(attn.astype(F32), gained)

    which = lax.broadcasted_iota(jnp.int32, (8, n), 0)

    def gained_of(b, hh):
        gain = c_gain[:, columns(t * each + hh, 1)]
        return taken[b, :, of_head(G, hh)].astype(F32) * gain

    def finish(b, merge):
        total = jnp.zeros((8, n), F32)
        for hh in range(each):
            at = hh * near + b
            lanes = slice(hh * DH, (hh + 1) * DH)
            if merge:
                got(OX, x_in.at[b, :, lanes], at)
                got(LX, lse_in.at[at], at)
                mine = jnp.sum(lse_own[at][0:3], axis=0, keepdims=True)
                other = jnp.sum(lse_in[at][0:3], axis=0, keepdims=True)
                top = jnp.maximum(mine, other)
                mine, other = jnp.exp2(mine - top), jnp.exp2(other - top)
                share = jnp.where(which == 0, mine, other) / (mine + other)
                shares[at] = share
                by_token = share.T
                attn = by_token[:, 0:1] * attn_own[b, :, lanes].astype(F32)
                attn = attn + by_token[:, 1:2] * x_in[b, :, lanes].astype(F32)
                attn_own[b, :, lanes] = attn.astype(BF16)
            else:
                shares[at] = jnp.where(which == 0, 1.0, 0.0)
        got(G, into(G, b), b)
        for hh in range(each):
            attn = attn_own[b, :, hh * DH : (hh + 1) * DH].astype(F32)
            total = total + stat_rows(attn, gained_of(b, hh))
        part_out[b] = total
        deliver(PART, part_out.at[b], part_in.at[t], b, b, t)
        deliver(ATTN, attn_own.at[b], attn_home.at[:, columns(t * each, each)], b, b, t)

    for this_half, merge in ((early, False), (late, True)):

        @pl.when(this_half)
        def _():
            @pl.loop(0, near)
            def _(d):
                finish(peer(d + 1), merge)

    @pl.loop(0, near)
    def _(b):
        got(PART, part_in.at[b], b)
        pair[0] += part_in[b]

    swap = pltpu.make_async_remote_copy(
        src_ref=pair.at[0],
        dst_ref=pair.at[1],
        send_sem=pair_sem.at[0],
        recv_sem=pair_sem.at[1],
        device_id=(me, 1 - core),
        device_id_type=MESH,
    )
    swap.start()
    swap.wait()
    totals = pair[0] + pair[1]
    inv = 1.0 / jnp.sqrt(totals[0:1] / feat_width + EPSILON)
    coef = inv * inv * inv * totals[1:2] / feat_width
    stat_own[...] = jnp.where(which == 0, inv, coef)

    @pl.loop(0, near)
    def _(d):
        b = peer(d + 1)
        deliver(STAT, stat_own, stats.at[t], b, b, t)

    for hh in range(each):
        lanes = slice(hh * DH, (hh + 1) * DH)

        @pl.loop(0, near)
        def _(d):
            b = peer(d + 1)
            at = hh * near + b
            if hh == 0:
                got(STAT, stats.at[b], b)
            by_token = stats[b].T
            share = shares[at].T
            attn = attn_own[b, :, lanes].astype(F32)
            dout = by_token[:, 0:1] * gained_of(b, hh) - by_token[:, 1:2] * attn
            dout = dout.astype(BF16).astype(F32)
            row_dot = jnp.sum(dout * attn, axis=-1, keepdims=True)

            @pl.when(late)
            def _():
                view = d_out.at[b, :, lanes]
                view[...] = (share[:, 1:2] * dout).astype(BF16)
                dot_out[at] = at_lanes((n, DH), in_parts(share[:, 1:2] * row_dot, 2)).T[:8]
                remote(DX, view, d_in.at[b, :, lanes], at, at, me - near).start()
                remote(RX, dot_out.at[at], dot_in.at[at], at, at, me - near).start()

            dots = at_lanes((n, DH), in_parts(share[:, 0:1] * row_dot, 2)).astype(BF16)
            both = jnp.concatenate([(share[:, 0:1] * dout).astype(BF16), dots], axis=1)
            sort_into(work, hh, b, two, nn(hits_of(slots[b, hh], pool), both))

    minus = jnp.where(lane < 2, -1.0, 0.0).astype(BF16)

    def changes_of(group_of, prob_ref):
        slopes = []
        for p in group_of:
            v = jnp.concatenate([rows16[p, :, 3 * DH :], minus], axis=1)
            slopes.append(nt(whole(work, p, two).astype(BF16), v))
        return [(prob_ref[p].astype(F32) * s).astype(BF16) for p, s in zip(group_of, slopes)]

    def split_rows(x):
        return x.reshape(2, part, DH)

    second, third = slice(DH, 2 * DH), slice(2 * DH, 3 * DH)

    @pl.loop(0, rows16.shape[0] // group)
    def _(g):
        group_of = [g * group + i for i in range(group)]
        for p, change in zip(group_of, changes_of(group_of, probs)):
            grad = whole(work, p, one).astype(BF16)
            acc[p, :, :, one] = split_rows(nn(change, rows16[p, :, DH : 2 * DH]) * factor)
            acc[p, :, :, second] = split_rows(tn(change, rows16[p, :, :DH]))
            acc[p, :, :, third] = split_rows(tn(probs[p], grad))

    homes = [(DQ, clu_dq), (DK, clu_dk), (DV, clu_dv)]

    def home_of(i, hh, owner):
        return homes[i][1].at[:, columns(owner * each + hh, 1)]

    def give(i, hh, b):
        at = hh * near + b
        view = taken.at[b, :, of_head(i, hh)]
        deliver(homes[i][0], view, home_of(i, hh, t), b, at, hh * near + t)

    def keys_home(hh, b, hits):
        rows = sorted_rows(acc, hh, b, slice(DH, 3 * DH))
        back = nn(hits, rows)
        taken[b, :, of_head(1, hh)] = (back[:, :DH] * factor).astype(BF16)
        taken[b, :, of_head(2, hh)] = back[:, DH:].astype(BF16)
        give(1, hh, b)
        give(2, hh, b)

    for hh in range(each):

        @pl.loop(0, near)
        def _(d):
            b = peer(d + 1)
            hits = hits_by_token(slots[b, hh], pool)
            taken[b, :, of_head(0, hh)] = nn(hits, sorted_rows(acc, hh, b, one)).astype(BF16)

            @pl.when(early)
            def _():
                give(0, hh, b)

            @pl.when(late)
            def _():
                keys_home(hh, b, hits)

    @pl.loop(0, near)
    def _(b):
        got(ATTN, attn_home.at[:, columns(b * each, each)], b)

    for j in range(plane - 1):

        @pl.when(relays & (spot == j))
        def _():
            for i in range(2):
                pass_on(i, j).wait_send()

    @pl.when(crosses)
    def _():
        for j in range(4):
            for i in range(2):
                rim_first(i, j, j < plane - 1).wait_send()

    @pl.when(straight)
    def _():
        for j in range(4):
            for i in range(2):
                rim_first(i, j, False).wait_send()

    back_crosses = (spot == 0) & (me > 0)
    back_straight = spot != 0
    back_relays = (spot != 0) & (me >= plane)

    def back_copy(j, src, dst, sem, to):
        return pltpu.make_async_remote_copy(
            src_ref=src,
            dst_ref=dst,
            send_sem=rim_send.at[2, j],
            recv_sem=sem,
            device_id=(to, core),
            device_id_type=MESH,
        )

    def back_first(j, by_relay):
        src = rim.at[:, :, span[j]]
        if by_relay:
            return back_copy(j, src, relay_back, relay_sem.at[2], level * plane + j)
        return back_copy(j, src, rim_back.at[:, :, span[j]], rim_recv.at[2, j], me - 1)

    by_token = stat_own[...].T
    inv_col, coef_col = by_token[:, 0:1], by_token[:, 1:2]
    for j in (1, 2, 3, 0):

        @pl.loop(j * (heads // 4), (j + 1) * (heads // 4))
        def _(h):
            cols = columns(h, 1)
            q = wq_v[:, cols]
            keys = jnp.concatenate([rim[0, :, cols], wk_v[:, cols]], axis=0)
            vals = jnp.concatenate([rim[1, :, cols], wv_v[:, cols]], axis=0)
            attn = attn_win[:, cols].astype(F32)
            gained = wg_v[:, cols].astype(F32) * w_gain[:, cols]
            grad = (inv_col * gained - coef_col * attn).astype(BF16)
            prob = window_prob(factor, q, keys)
            row_dot = jnp.sum(grad.astype(F32) * attn, axis=-1, keepdims=True)
            change = (prob * (nt(grad, vals) - row_dot)).astype(BF16)
            wq_v[:, cols] = (nn(change, keys) * factor).astype(BF16)
            dk = tn(change, q)
            dv = tn(prob.astype(BF16), grad)
            rim[0, :, cols] = dk[:WINDOW].astype(BF16)
            rim[1, :, cols] = dv[:WINDOW].astype(BF16)
            wk_v[:, cols] = dk[WINDOW:].astype(BF16)
            wv_v[:, cols] = dv[WINDOW:].astype(BF16)
            attn_win[:, cols] = (attn * inv_col * w_gain[:, cols]).astype(BF16)
            clu = attn_home[:, cols].astype(F32)
            attn_home[:, cols] = (clu * inv_col * c_gain[:, cols]).astype(BF16)

        @pl.when(back_crosses)
        def _():
            back_first(j, 0 < j < plane).start()

        @pl.when(back_straight)
        def _():
            back_first(j, False).start()

    stores = [
        pltpu.make_async_copy(src, dst, local_sem.at[4 + i])
        for i, (src, dst) in enumerate(
            [
                (attn_win, win_normed),
                (attn_home, clu_normed),
                (wq_v, win_dq),
                (wk_v, win_dk),
                (wv_v, win_dv),
            ]
        )
    ]
    for store in stores[:3]:
        store.start()

    def pass_back(j):
        dst = rim_back.at[:, :, span[j]]
        return pltpu.make_async_remote_copy(
            src_ref=relay_back,
            dst_ref=dst,
            send_sem=relay_sem.at[3],
            recv_sem=rim_recv.at[2, j],
            device_id=(level * plane - 1, core),
            device_id_type=MESH,
        )

    for j in range(1, plane):

        @pl.when(back_relays & (spot == j))
        def _():
            pltpu.make_async_copy(relay_back, relay_back, relay_sem.at[2]).wait()
            pass_back(j).start()

    @pl.when(early)
    def _():
        for hh in range(each):
            lanes = slice(hh * DH, (hh + 1) * DH)

            @pl.loop(0, near)
            def _(d):
                b = peer(d + 1)
                at = hh * near + b
                got(DX, d_in.at[b, :, lanes], at)
                got(RX, dot_in.at[at], at)
                dots = jnp.concatenate(
                    [dot_in[at].T, jnp.zeros((n, DH - 8), F32)], axis=1
                ).astype(BF16)
                both = jnp.concatenate([d_in[b, :, lanes], dots], axis=1)
                sort_into(work, hh, b, two, nn(hits_of(slots[near + b, hh], pool), both))

            @pl.loop(0, pairs // group)
            def _(g):
                group_of = [hh * pairs + g * group + i for i in range(group)]
                for p, change in zip(group_of, changes_of(group_of, probs_x)):
                    grad = whole(work, p, one).astype(BF16)
                    acc[p, :, :, second] += split_rows(tn(change, xq16[p]))
                    acc[p, :, :, third] += split_rows(tn(probs_x[p], grad))
                    dq = nn(change, rows16[p, :, DH : 2 * DH]) * factor
                    work[p, :, :, one] = split_rows(dq)

            @pl.loop(0, near)
            def _(d):
                b = peer(d + 1)
                at = hh * near + b
                hits = hits_by_token(slots[near + b, hh], pool)
                view = x_out.at[b, :, lanes]
                sent(OX, view, at)
                view[...] = nn(hits, sorted_rows(work, hh, b, one)).astype(BF16)
                remote(DQX, view, d_in.at[b, :, lanes], at, at, me + near).start()

            @pl.loop(0, near)
            def _(d):
                b = peer(d + 1)
                keys_home(hh, b, hits_by_token(slots[b, hh], pool))

    @pl.when(late)
    def _():
        for hh in range(each):
            lanes = slice(hh * DH, (hh + 1) * DH)

            @pl.loop(0, near)
            def _(d):
                b = peer(d + 1)
                got(DQX, d_in.at[b, :, lanes], hh * near + b)
                more = d_in[b, :, lanes].astype(F32)
                view = taken.at[b, :, of_head(0, hh)]
                view[...] = (view[...].astype(F32) + more).astype(BF16)
                give(0, hh, b)

    @pl.when(me < n_seq - 1)
    def _():
        for j in range(4):
            view = rim_back.at[:, :, span[j]]
            pltpu.make_async_copy(view, view, rim_recv.at[2, j]).wait()

    @pl.when(me == n_seq - 1)
    def _():
        rim_back[...] = jnp.zeros_like(rim_back)

    @pl.loop(0, heads)
    def _(h):
        cols = columns(h, 1)
        dk = wk_v[:, cols].astype(F32) + rim_back[0, :, cols].astype(F32)
        wk_v[:, cols] = (dk * factor).astype(BF16)
        dv = wv_v[:, cols].astype(F32) + rim_back[1, :, cols].astype(F32)
        wv_v[:, cols] = dv.astype(BF16)

    for store in stores[3:]:
        store.start()

    for j in range(4):

        @pl.when(back_crosses)
        def _():
            back_first(j, 0 < j < plane).wait_send()

        @pl.when(back_straight)
        def _():
            back_first(j, False).wait_send()

    for j in range(1, plane):

        @pl.when(back_relays & (spot == j))
        def _():
            pass_back(j).wait_send()

    @pl.loop(1, near)
    def _(d):
        to = peer(d)
        for kind, src in arrays:
            sent(kind, src.at[:, columns(to * each, each)], to)
        sent(IDS, ids.at[pl.ds(to * each, each)], to)
        sent(PART, part_out.at[to], to)
        sent(ATTN, attn_own.at[to], to)
        sent(STAT, stat_own, to)
        for hh in range(each):
            for i, (kind, home) in enumerate(homes):
                sent(kind, taken.at[to, :, of_head(i, hh)], hh * near + to)

    @pl.loop(0, near)
    def _(b):
        for hh in range(each):
            for i, (kind, home) in enumerate(homes):
                got(kind, home_of(i, hh, b), hh * near + b)

    @pl.when(late)
    def _():
        @pl.loop(0, near)
        def _(b):
            sent(IDSX, ids.at[pl.ds(b * each, each)], b)
            for hh in range(each):
                at = hh * near + b
                sent(QX, cq.at[:, columns(b * each + hh, 1)], at)
                sent(DX, d_out.at[b, :, hh * DH : (hh + 1) * DH], at)
                sent(RX, dot_out.at[at], at)

    @pl.when(early)
    def _():
        @pl.loop(0, near)
        def _(b):
            for hh in range(each):
                at = hh * near + b
                sent(LX, lse_out.at[at], at)
                sent(DQX, x_out.at[b, :, hh * DH : (hh + 1) * DH], at)

    for store in stores:
        store.wait()


def layer(*arrays):
    win_query, cluster_ids = arrays[0], arrays[6]
    n, wide = win_query.shape
    sources = lax.axis_size("seq")
    near = sources // 2
    cap = SLOTS // sources
    clusters = sources * (2 * n // SLOTS)
    part = near * cap
    heads = wide // DH
    each = heads // near
    pairs = each * clusters // 2
    given = list(arrays)
    given[6] = cluster_ids[:, None, :]
    given[7], given[8] = arrays[7][None, :], arrays[8][None, :]
    anywhere = pl.BlockSpec(memory_space=pl.ANY)
    vmem = pl.BlockSpec(memory_space=pltpu.VMEM)
    group = next(g for g in (16, 8, 4, 2, 1) if clusters // 2 % g == 0)
    rows_of = pltpu.VMEM((each * near, 8, n), F32)
    return pl.pallas_call(
        functools.partial(layer_kernel, DH ** (-0.5), cap, group, 4),
        in_specs=[anywhere] * 6 + [vmem] * 3 + [anywhere] * 2,
        out_specs=[anywhere] * 8,
        out_shape=[jax.ShapeDtypeStruct((n, wide), BF16)] * 8,
        scratch_shapes=[
            pltpu.VMEM((near, n, 4 * each * DH), BF16),
            pltpu.VMEM((sources, each, 1, n), jnp.int32),
            pltpu.VMEM((sources, each, 1, n), jnp.int32),
        ]
        + [pltpu.VMEM((n, wide), BF16)] * 4
        + [pltpu.VMEM((2, n, wide), BF16)] * 2
        + [pltpu.VMEM((2, n, wide // 4), BF16)] * 2
        + [pltpu.VMEM((n, wide), BF16)] * 2
        + [pltpu.VMEM((near, n, each * DH), BF16)] * 5
        + [
            pltpu.VMEM((pairs, 2 * part, 4 * DH), BF16),
            pltpu.VMEM((pairs, 2 * part, DH), BF16),
            pltpu.VMEM((pairs, 2, part, 2 * DH), F32),
            pltpu.VMEM((pairs, 2, part, 3 * DH), F32),
            pltpu.VMEM((pairs, 2 * part, 2 * part), BF16),
            pltpu.VMEM((pairs, 2 * part, 2 * part), BF16),
        ]
        + [rows_of] * 6
        + [
            pltpu.VMEM((near, 8, n), F32),
            pltpu.VMEM((near, 8, n), F32),
            pltpu.VMEM((2, 8, n), F32),
            pltpu.VMEM((8, n), F32),
            pltpu.VMEM((near, 8, n), F32),
            pltpu.SemaphoreType.DMA((18, sources)),
            pltpu.SemaphoreType.DMA((18, sources)),
            pltpu.SemaphoreType.DMA((3, 4)),
            pltpu.SemaphoreType.DMA((3, 4)),
            pltpu.SemaphoreType.DMA((6,)),
            pltpu.SemaphoreType.DMA((2,)),
            pltpu.SemaphoreType.DMA((9,)),
        ],
        cost_estimate=pl.CostEstimate(
            flops=14 * n * 2 * n * wide, bytes_accessed=16 * n * wide * 2, transcendentals=0
        ),
        compiler_params=pltpu.CompilerParams(
            vmem_limit_bytes=60 << 20, collective_id=0, has_side_effects=True
        ),
    )(*given)


def solution(mesh):
    sources, split = mesh.shape["seq"], mesh.shape["head"]
    whole_heads = HC // split == sources and SLOTS // sources % 8 == 0 and split == 2 and sources % 4 == 0
    return jax.shard_map(
        layer if whole_heads else body,
        mesh=mesh,
        in_specs=(P("seq", "head"),) * 6
        + (P("head", "seq"), P("head"), P("head"))
        + (P("seq", "head"),) * 2,
        out_specs=(P("seq", "head"),) * 8,
        check_vma=False,
    )
```

```python
import functools

import jax
import jax.numpy as jnp
from jax import lax
from jax.experimental import pallas as pl
from jax.experimental.pallas import tpu as pltpu
from jax.sharding import PartitionSpec as P

HW = 32
HC = 32
DH = 128
WINDOW = 256
SLOTS = 128
CHUNKS = 2

EPSILON = 1e-06
F32 = jnp.float32
BF16 = jnp.bfloat16


def from_behind(block, axis, distance):
    devices = range(lax.axis_size(axis))
    route = [(i - distance, i) for i in devices if i - distance in devices]
    return lax.ppermute(block, axis, route)


def nt(a, b):
    return lax.dot_general(a, b, (((1,), (1,)), ((), ())), preferred_element_type=F32)


def tn(a, b):
    return lax.dot_general(a, b, (((0,), (0,)), ((), ())), preferred_element_type=F32)


def nn(a, b):
    return jnp.dot(a, b, preferred_element_type=F32)


def one_hot(slot_ref, pool):
    n = slot_ref.shape[-1]
    hit = lax.broadcasted_iota(jnp.int32, (pool, n), 0) == slot_ref[0]
    return jnp.where(hit, 1.0, 0.0).astype(BF16)


def normalized(scores, allowed):
    masked = jnp.where(allowed, scores, -jnp.inf)
    grown = jnp.exp(masked - jnp.max(masked, axis=-1, keepdims=True))
    return grown * (1.0 / jnp.sum(grown, axis=-1, keepdims=True))


def call(kernel, grid, in_specs, out_specs, out_shape, flops, size, **more):
    return pl.pallas_call(
        kernel,
        grid=grid,
        in_specs=in_specs,
        out_specs=out_specs,
        out_shape=out_shape,
        cost_estimate=pl.CostEstimate(flops=flops, bytes_accessed=size, transcendentals=0),
        compiler_params=pltpu.CompilerParams(vmem_limit_bytes=48 << 20),
        **more,
    )


def dispatch_kernel(*refs):
    slot_ref, value_refs, out_ref = refs[0], refs[1:-1], refs[-1]
    picked = one_hot(slot_ref, out_ref.shape[0])
    for i, ref in enumerate(value_refs):
        out_ref[:, i * DH : (i + 1) * DH] = nn(picked, ref[...]).astype(BF16)


def dispatch(slot_at, values, first, count, pool):
    n = slot_at.shape[-1]
    wide = len(values) * DH
    return call(
        dispatch_kernel,
        (count,),
        [pl.BlockSpec((1, 1, n), lambda h: (h + first, 0, 0))]
        + [pl.BlockSpec((n, DH), lambda h: (0, h + first)) for _ in values],
        pl.BlockSpec((pool, wide), lambda h: (0, h)),
        jax.ShapeDtypeStruct((pool, count * wide), BF16),
        2 * count * pool * n * wide,
        2 * count * (pool + n) * wide,
    )(slot_at, *values)


def collect_kernel(n_out, *refs):
    slot_ref, rows_ref, out_refs = refs[0], refs[1], refs[-n_out:]
    picked = one_hot(slot_ref, rows_ref.shape[0])
    merged = tn(picked, rows_ref[...]).astype(BF16)
    for i, ref in enumerate(out_refs):
        ref[...] = merged[:, i * DH : (i + 1) * DH]


def collect(slot_at, rows, first, count, n_out, earlier):
    n = slot_at.shape[-1]
    pool = rows.shape[0]
    heads = slot_at.shape[0]
    wide = n_out * DH
    return call(
        functools.partial(collect_kernel, n_out),
        (count,),
        [
            pl.BlockSpec((1, 1, n), lambda h: (h + first, 0, 0)),
            pl.BlockSpec((pool, wide), lambda h: (0, h)),
        ]
        + [pl.BlockSpec(memory_space=pl.ANY) for _ in earlier],
        [pl.BlockSpec((n, DH), lambda h: (0, h + first))] * n_out,
        [jax.ShapeDtypeStruct((n, heads * DH), BF16)] * n_out,
        2 * count * pool * n * wide,
        2 * count * (pool + n) * wide,
        input_output_aliases={2 + i: i for i in range(len(earlier))},
    )(slot_at, rows, *earlier)


class Rows:
    def __init__(self, sources, owned, cap):
        self.sources, self.owned, self.cap = sources, owned, cap
        self.aligned = cap % 8 == 0

    def selector(self, c):
        members = self.sources * self.cap
        layout = (members, members * self.owned)
        member = lax.broadcasted_iota(jnp.int32, layout, 0)
        row = lax.broadcasted_iota(jnp.int32, layout, 1)
        want = member // self.cap * (self.cap * self.owned) + c * self.cap + member % self.cap
        return jnp.where(row == want, 1.0, 0.0).astype(BF16)

    def split(self, rows):
        members = self.sources * self.cap
        if not self.aligned:
            return [nn(self.selector(c), rows).astype(BF16) for c in range(self.owned)]
        wide = rows.shape[1]
        four = rows.astype(F32).reshape(self.sources, self.owned, self.cap, wide)
        return [four[:, c].reshape(members, wide).astype(BF16) for c in range(self.owned)]

    def join(self, parts):
        wide = parts[0].shape[1]
        pool = self.sources * self.cap * self.owned
        if not self.aligned:
            total = jnp.zeros((pool, wide), F32)
            for c, part in enumerate(parts):
                total = total + tn(self.selector(c), part.astype(BF16))
            return total.astype(BF16)
        shaped = [p.reshape(self.sources, 1, self.cap, wide) for p in parts]
        return jnp.concatenate(shaped, axis=1).reshape(pool, wide).astype(BF16)


def cluster_allowed(live_ref, c, members):
    row = lax.broadcasted_iota(jnp.int32, (members, members), 0)
    col = lax.broadcasted_iota(jnp.int32, (members, members), 1)
    live = jnp.broadcast_to(live_ref[0, c : c + 1, :], (members, members)) > 0.5
    return (live & (col <= row)) | (col == row)


def owner_fwd_kernel(rows, factor, live_ref, qkv_ref, out_ref):
    members = rows.sources * rows.cap
    parts = []
    for c, qkv in enumerate(rows.split(qkv_ref[...])):
        q, k, v = qkv[:, :DH], qkv[:, DH : 2 * DH], qkv[:, 2 * DH :]
        prob = normalized(nt(q, k) * factor, cluster_allowed(live_ref, c, members))
        parts.append(nn(prob.astype(BF16), v))
    out_ref[...] = rows.join(parts)


def owner_bwd_kernel(rows, factor, live_ref, qkv_ref, attn_ref, grad_ref, out_ref):
    members = rows.sources * rows.cap
    attn_parts = rows.split(attn_ref[...])
    grad_parts = rows.split(grad_ref[...])
    parts = []
    for c, qkv in enumerate(rows.split(qkv_ref[...])):
        q, k, v = qkv[:, :DH], qkv[:, DH : 2 * DH], qkv[:, 2 * DH :]
        grad = grad_parts[c]
        row_dot = jnp.sum(grad.astype(F32) * attn_parts[c].astype(F32), axis=-1, keepdims=True)
        prob = normalized(nt(q, k) * factor, cluster_allowed(live_ref, c, members))
        change = (prob * (nt(grad, v) - row_dot)).astype(BF16)
        dq = nn(change, k) * factor
        dk = tn(change, q) * factor
        dv = tn(prob.astype(BF16), grad)
        parts.append(jnp.concatenate([dq, dk, dv], axis=1))
    out_ref[...] = rows.join(parts)


def owner_call(kernel, rows, factor, live, first, arrays, n_out):
    pool = arrays[0].shape[0]
    count = arrays[0].shape[1] // (3 * DH)
    members = rows.sources * rows.cap
    wides = [a.shape[1] // count for a in arrays]
    return call(
        functools.partial(kernel, rows, factor),
        (count,),
        [pl.BlockSpec((1, rows.owned, members), lambda h: (h + first, 0, 0))]
        + [pl.BlockSpec((pool, w), lambda h: (0, h)) for w in wides],
        pl.BlockSpec((pool, n_out * DH), lambda h: (0, h)),
        jax.ShapeDtypeStruct((pool, count * n_out * DH), BF16),
        12 * count * pool * members * DH,
        2 * count * pool * (sum(wides) + n_out * DH),
    )(live, *arrays)


def window_prob(factor, q, keys):
    n = q.shape[0]
    row = lax.broadcasted_iota(jnp.int32, (n, n + WINDOW), 0)
    col = lax.broadcasted_iota(jnp.int32, (n, n + WINDOW), 1)
    gap = row + WINDOW - col
    lowest = jnp.where(lax.axis_index("seq") > 0, 0, WINDOW)
    allowed = (gap >= 0) & (gap < WINDOW) & (col >= lowest)
    return normalized(nt(q, keys) * factor, allowed)


def window_fwd_kernel(factor, q_ref, kp_ref, k_ref, vp_ref, v_ref, out_ref):
    keys = jnp.concatenate([kp_ref[0], k_ref[...]], axis=0)
    vals = jnp.concatenate([vp_ref[0], v_ref[...]], axis=0)
    prob = window_prob(factor, q_ref[...], keys)
    out_ref[...] = nn(prob.astype(BF16), vals).astype(BF16)


def window_bwd_kernel(
    factor, q_ref, kp_ref, k_ref, vp_ref, v_ref, attn_ref, grad_ref, dq_ref, dk_ref, dv_ref, rim_ref
):
    q, grad = q_ref[...], grad_ref[...]
    keys = jnp.concatenate([kp_ref[0], k_ref[...]], axis=0)
    vals = jnp.concatenate([vp_ref[0], v_ref[...]], axis=0)
    prob = window_prob(factor, q, keys)
    row_dot = jnp.sum(grad.astype(F32) * attn_ref[...].astype(F32), axis=-1, keepdims=True)
    change = (prob * (nt(grad, vals) - row_dot)).astype(BF16)
    dq_ref[...] = (nn(change, keys) * factor).astype(BF16)
    dk = tn(change, q)
    dv = tn(prob.astype(BF16), grad)
    rim_ref[0] = dk[:WINDOW].astype(BF16)
    rim_ref[1] = dv[:WINDOW].astype(BF16)
    dk_ref[...] = dk[WINDOW:]
    dv_ref[...] = dv[WINDOW:]


def window_specs(n):
    here = pl.BlockSpec((n, DH), lambda h: (0, h))
    key = pl.BlockSpec((1, n, DH), lambda h: (0, 0, h))
    val = pl.BlockSpec((1, n, DH), lambda h: (1, 0, h))
    return here, key, val


def window_fwd(factor, query, key, value, before):
    n, wide = query.shape
    here, rim_key, rim_val = window_specs(n)
    return call(
        functools.partial(window_fwd_kernel, factor),
        (wide // DH,),
        [here, rim_key, here, rim_val, here],
        here,
        jax.ShapeDtypeStruct((n, wide), BF16),
        4 * n * 2 * n * wide,
        12 * n * wide,
    )(query, before, key, before, value)


def window_bwd(factor, query, key, value, before, attn, grad):
    n, wide = query.shape
    here, rim_key, rim_val = window_specs(n)
    return call(
        functools.partial(window_bwd_kernel, factor),
        (wide // DH,),
        [here, rim_key, here, rim_val, here, here, here],
        [here, here, here, pl.BlockSpec((2, n, DH), lambda h: (0, 0, h))],
        [
            jax.ShapeDtypeStruct((n, wide), BF16),
            jax.ShapeDtypeStruct((n, wide), F32),
            jax.ShapeDtypeStruct((n, wide), F32),
            jax.ShapeDtypeStruct((2, n, wide), BF16),
        ],
        10 * n * 2 * n * wide,
        28 * n * wide,
    )(query, before, key, before, value, attn, grad)


def body(
    win_query,
    win_key,
    win_value,
    clu_query,
    clu_key,
    clu_value,
    cluster_ids,
    win_gain,
    clu_gain,
    win_out_grad,
    clu_out_grad,
):
    n_rows = win_query.shape[0]
    factor = DH ** (-0.5)
    feat_width = (HW + HC) * DH
    sources = lax.axis_size("seq")
    n_cap = SLOTS // sources
    owned_count = 2 * n_rows // SLOTS
    pool_size = 2 * n_rows
    clu_heads = clu_query.shape[1] // DH
    rows = Rows(sources, owned_count, n_cap)

    def exchange(values):
        shaped = values.reshape(sources, pool_size // sources, values.shape[1])
        moved = lax.all_to_all(shaped, "seq", split_axis=0, concat_axis=0, tiled=True)
        return moved.reshape(values.shape)

    row_ids = lax.broadcasted_iota(jnp.int32, (n_rows, n_rows), 0)
    col_ids = lax.broadcasted_iota(jnp.int32, (n_rows, n_rows), 1)
    same_cluster = (cluster_ids[:, :, None] == cluster_ids[:, None, :]) & (col_ids < row_ids)
    rank_in = jnp.sum(same_cluster.astype(jnp.int32), axis=-1)
    slot_at = (cluster_ids * n_cap + rank_in)[:, None, :]

    n_clusters = sources * owned_count
    every = lax.broadcasted_iota(jnp.int32, (n_clusters, clu_heads, n_rows), 0)
    counts = jnp.sum((cluster_ids[None] == every).astype(F32), axis=-1)
    counts = counts.reshape(sources, owned_count, clu_heads)
    counts = lax.all_to_all(counts, "seq", split_axis=0, concat_axis=0, tiled=True)
    slot_pos = lax.broadcasted_iota(F32, (clu_heads, owned_count, sources, n_cap), 3)
    live = (slot_pos < counts.transpose(2, 1, 0)[..., None]).astype(F32)
    live = live.reshape(clu_heads, owned_count, sources * n_cap)

    chunks = CHUNKS if clu_heads % CHUNKS == 0 else 1
    per = clu_heads // chunks
    starts = [i * per for i in range(chunks)]

    held = [
        exchange(dispatch(slot_at, [clu_query, clu_key, clu_value], first, per, pool_size))
        for first in starts
    ]
    before = from_behind(jnp.stack([win_key, win_value]), "seq", 1)
    attn_win = window_fwd(factor, win_query, win_key, win_value, before)

    attn_held = [
        owner_call(owner_fwd_kernel, rows, factor, live, first, [qkv], 1)
        for first, qkv in zip(starts, held)
    ]
    attn_back = [exchange(part) for part in attn_held]
    attn_clu = ()
    for first, part in zip(starts, attn_back):
        attn_clu = collect(slot_at, part, first, per, 1, attn_clu)
    attn_clu = attn_clu[0]

    flat_win = attn_win.astype(F32)
    flat_clu = attn_clu.astype(F32)
    grad_win = win_out_grad.astype(F32) * win_gain
    grad_clu = clu_out_grad.astype(F32) * clu_gain
    totals = jnp.stack(
        [
            jnp.sum(flat_win * flat_win, axis=1) + jnp.sum(flat_clu * flat_clu, axis=1),
            jnp.sum(grad_win * flat_win, axis=1) + jnp.sum(grad_clu * flat_clu, axis=1),
        ]
    )
    totals = lax.psum(totals, "head")
    sq_total, dot_total = totals[0], totals[1]
    inv_rms = 1.0 / jnp.sqrt(sq_total / feat_width + EPSILON)
    coef_rows = inv_rms**3 * dot_total / feat_width
    dout_clu = (inv_rms[:, None] * grad_clu - coef_rows[:, None] * flat_clu).astype(BF16)
    dout_win = (inv_rms[:, None] * grad_win - coef_rows[:, None] * flat_win).astype(BF16)
    win_normed = (flat_win * inv_rms[:, None] * win_gain).astype(BF16)
    clu_normed = (flat_clu * inv_rms[:, None] * clu_gain).astype(BF16)

    grad_held = [
        exchange(dispatch(slot_at, [dout_clu], first, per, pool_size)) for first in starts
    ]
    win_dq, key_own, val_own, rim = window_bwd(
        factor, win_query, win_key, win_value, before, attn_win, dout_win
    )
    after_rim = from_behind(rim, "seq", -1)

    clu_grads = ()
    sent = [
        owner_call(owner_bwd_kernel, rows, factor, live, first, [qkv, part, grad], 3)
        for first, qkv, part, grad in zip(starts, held, attn_held, grad_held)
    ]
    home = [exchange(part) for part in sent]
    win_dk = ((key_own + after_rim[0]) * factor).astype(BF16)
    win_dv = (val_own + after_rim[1]).astype(BF16)
    for first, part in zip(starts, home):
        clu_grads = collect(slot_at, part, first, per, 3, clu_grads)
    return (win_normed, clu_normed, win_dq, win_dk, win_dv, *clu_grads)


BIG = 1e30
MESH = pl.DeviceIdType.MESH
LOG2E = 1.4426950408889634


def hits_of(slot, pool):
    n = slot.shape[-1]
    hit = lax.broadcasted_iota(jnp.int32, (pool, n), 0) == slot
    return jnp.where(hit, 1.0, 0.0).astype(BF16)


def hits_by_token(slot, pool):
    n = slot.shape[-1]
    column = jnp.broadcast_to(slot.astype(F32), (8, n)).T[:, :1].astype(jnp.int32)
    hit = lax.broadcasted_iota(jnp.int32, (n, pool), 1) == column
    return jnp.where(hit, 1.0, 0.0).astype(BF16)


def stat_rows(attn, gained):
    wide = attn.shape[1]
    both = jnp.concatenate([attn * attn, gained * attn], axis=1)
    row = lax.broadcasted_iota(jnp.int32, (8, 2 * wide), 0)
    col = lax.broadcasted_iota(jnp.int32, (8, 2 * wide), 1)
    pick = jnp.where(col // wide == row, 1.0, 0.0).astype(BF16)
    high = both.astype(BF16)
    low = (both - high.astype(F32)).astype(BF16)
    return nt(pick, high) + nt(pick, low)


def head_cols(h):
    return pl.ds(pl.multiple_of(h * DH, DH), DH)


def columns(first, count):
    return pl.ds(pl.multiple_of(first * DH, DH), count * DH)


def at_lanes(shape, values):
    lane = lax.broadcasted_iota(jnp.int32, shape, 1)
    total = jnp.zeros(shape, F32)
    for i, value in enumerate(values):
        total = jnp.where(lane == i, value, total)
    return total


def in_parts(x, count):
    parts = []
    for _ in range(count - 1):
        parts.append(x.astype(BF16).astype(F32))
        x = x - parts[-1]
    return parts + [x]


def layer_kernel(
    factor,
    cap,
    group,
    plane,
    wq,
    wk,
    wv,
    cq,
    ck,
    cv,
    ids,
    w_gain,
    c_gain,
    wg,
    cg,
    win_normed,
    clu_normed,
    win_dq,
    win_dk,
    win_dv,
    clu_dq,
    clu_dk,
    clu_dv,
    taken,
    ids_in,
    slots,
    wq_v,
    wk_v,
    wv_v,
    wg_v,
    rim,
    rim_back,
    relay,
    relay_back,
    attn_win,
    attn_home,
    attn_own,
    x_in,
    d_in,
    x_out,
    d_out,
    rows16,
    xq16,
    work,
    acc,
    probs,
    probs_x,
    lse_own,
    lse_out,
    lse_in,
    dot_out,
    dot_in,
    shares,
    part_out,
    part_in,
    pair,
    stat_own,
    stats,
    send_sem,
    recv_sem,
    rim_send,
    rim_recv,
    relay_sem,
    pair_sem,
    local_sem,
):
    me, core = lax.axis_index("seq"), lax.axis_index("head")
    n_seq = lax.axis_size("seq")
    near = n_seq // 2
    half, t = me // near, lax.rem(me, near)
    base = half * near
    early, late = half == 0, half == 1
    n = wq.shape[0]
    heads = wq.shape[1] // DH
    each = heads // near
    pairs = rows16.shape[0] // each
    members = rows16.shape[1]
    part = members // 2
    clusters = 2 * pairs
    pool = clusters * cap
    feat_width = (HW + HC) * DH
    (Q, K, V, G, IDS, IDSX, QX, OX, LX, PART, ATTN, STAT, DX, RX, DQX, DQ, DK, DV) = range(18)

    def peer(d):
        return lax.rem(t + d, near)

    def remote(kind, src, dst, mine, theirs, to):
        return pltpu.make_async_remote_copy(
            src_ref=src,
            dst_ref=dst,
            send_sem=send_sem.at[kind, mine],
            recv_sem=recv_sem.at[kind, theirs],
            device_id=(to, core),
            device_id_type=MESH,
        )

    def got(kind, dst, index):
        pltpu.make_async_copy(dst, dst, recv_sem.at[kind, index]).wait()

    def sent(kind, src, index):
        pltpu.make_async_copy(src, src, send_sem.at[kind, index]).wait()

    def deliver(kind, src, dst, b, mine, theirs):
        @pl.when(b != t)
        def _():
            remote(kind, src, dst, mine, theirs, base + b).start()

        @pl.when(b == t)
        def _():
            pltpu.make_async_copy(src, dst, recv_sem.at[kind, theirs]).start()

    loads = [
        pltpu.make_async_copy(src, dst, local_sem.at[i])
        for i, (src, dst) in enumerate([(wq, wq_v), (wk, wk_v), (wv, wv_v), (wg, wg_v)])
    ]

    barrier = pltpu.get_barrier_semaphore()

    @pl.loop(1, n_seq)
    def _(d):
        to = lax.rem(me + d, n_seq)
        pl.semaphore_signal(barrier, inc=1, device_id=(to, core), device_id_type=MESH)

    pl.semaphore_signal(barrier, inc=1, device_id=(me, 1 - core), device_id_type=MESH)
    pl.semaphore_wait(barrier, n_seq)

    @pl.loop(0, near)
    def _(d):
        to = peer(d)
        view = ids.at[pl.ds(to * each, each)]
        deliver(IDS, view, ids_in.at[t], to, to, t)

        @pl.when(late)
        def _():
            remote(IDSX, view, ids_in.at[near + t], to, t, to).start()

    spot, level = lax.rem(me, plane), me // plane
    quarter = heads // 4 * DH
    span = [slice(j * quarter, (j + 1) * quarter) for j in range(4)]
    crosses = (spot == plane - 1) & (me < n_seq - 1)
    straight = (spot != plane - 1) & (me < n_seq - 1)
    relays = (spot != plane - 1) & (me < n_seq - plane)

    def rim_copy(i, j, src, dst, sem, to):
        return pltpu.make_async_remote_copy(
            src_ref=src,
            dst_ref=dst,
            send_sem=rim_send.at[i, j],
            recv_sem=sem,
            device_id=(to, core),
            device_id_type=MESH,
        )

    def rim_first(i, j, by_relay):
        src = (wk, wv)[i].at[:, span[j]]
        if by_relay:
            return rim_copy(i, j, src, relay.at[i], relay_sem.at[i], level * plane + j)
        return rim_copy(i, j, src, rim.at[i, :, span[j]], rim_recv.at[i, j], me + 1)

    arrays = [(Q, cq), (K, ck), (V, cv), (G, cg)]

    def into(kind, source):
        return taken.at[source, :, kind * each * DH : (kind + 1) * each * DH]

    def of_head(kind, hh):
        return slice((kind * each + hh) * DH, (kind * each + hh + 1) * DH)

    def exchange(some):
        @pl.loop(1, near)
        def _(d):
            to = peer(d)
            for kind, src in some:
                view = src.at[:, columns(to * each, each)]
                remote(kind, view, into(kind, t), to, t, base + to).start()

    exchange(arrays[:1])

    exchange(arrays[1:3])

    @pl.when(crosses)
    def _():
        for j in range(4):
            for i in range(2):
                rim_first(i, j, j < plane - 1).start()

    for kind, src in arrays:
        view = src.at[:, columns(t * each, each)]
        pltpu.make_async_copy(view, into(kind, t), recv_sem.at[kind, t]).start()
    for load in loads:
        load.start()

    @pl.when(late)
    def _():
        for hh in range(each):

            @pl.loop(0, near)
            def _(b):
                if hh == 0:
                    got(Q, into(Q, b), b)
                view = taken.at[b, :, of_head(Q, hh)]
                dst = x_in.at[b, :, hh * DH : (hh + 1) * DH]
                remote(QX, view, dst, hh * near + b, hh * near + b, me - near).start()

    earlier = lax.broadcasted_iota(jnp.int32, (n, n), 0) < lax.broadcasted_iota(
        jnp.int32, (n, n), 1
    )
    earlier = jnp.where(earlier, 1.0, 0.0).astype(BF16)

    def place(b):
        for hh in range(each):
            of_block = ids_in[b, hh]
            member = hits_of(of_block, clusters)
            rank = jnp.sum(member.astype(F32) * nn(member, earlier), axis=0, keepdims=True)
            slots[b, hh] = of_block * cap + rank.astype(jnp.int32)

    @pl.loop(0, near)
    def _(b):
        got(IDS, ids_in.at[b], b)
        place(b)

    @pl.when(early)
    def _():
        @pl.loop(0, near)
        def _(b):
            got(IDSX, ids_in.at[near + b], b)
            place(near + b)

    def pass_on(i, j):
        return pltpu.make_async_remote_copy(
            src_ref=relay.at[i],
            dst_ref=rim.at[i, :, span[j]],
            send_sem=relay_sem.at[4 + i],
            recv_sem=rim_recv.at[i, j],
            device_id=((level + 1) * plane, core),
            device_id_type=MESH,
        )

    def block_rows(b):
        return pl.ds(pl.multiple_of(b * cap, cap), cap)

    def sort_into(ref, hh, b, lanes, rows):
        shaped = rows.reshape(pairs, 2, cap, rows.shape[1])
        ref[hh * pairs : (hh + 1) * pairs, :, block_rows(b), lanes] = shaped

    def sorted_rows(ref, hh, b, lanes):
        rows = ref[hh * pairs : (hh + 1) * pairs, :, block_rows(b), lanes]
        return rows.reshape(pool, rows.shape[3]).astype(BF16)

    def whole(ref, p, lanes):
        return ref[p, :, :, lanes].reshape(members, lanes.stop - lanes.start)

    one, two = slice(0, DH), slice(0, 2 * DH)

    @pl.loop(0, near)
    def _(b):
        for kind in (K, V):
            got(kind, into(kind, b), b)

    @pl.when(early)
    def _():
        @pl.loop(0, near)
        def _(b):
            got(Q, into(Q, b), b)

    @pl.when(straight)
    def _():
        for j in range(4):
            for i in range(2):
                rim_first(i, j, False).start()

    exchange(arrays[3:])

    @pl.loop(0, near, unroll=4)
    def _(b):
        for hh in range(each):
            values = jnp.concatenate(
                [taken[b, :, of_head(kind, hh)] for kind in (Q, K, V)]
                + [jnp.ones((n, DH), BF16)],
                axis=1,
            )
            rows = nn(hits_of(slots[b, hh], pool), values)
            sort_into(acc, hh, b, slice(0, 3 * DH), rows[:, : 3 * DH])
            sort_into(work, hh, b, one, rows[:, 3 * DH :])

    row = lax.broadcasted_iota(jnp.int32, (members, members), 0)
    col = lax.broadcasted_iota(jnp.int32, (members, members), 1)
    same = (row // part) == (col // part)
    lane = lax.broadcasted_iota(jnp.int32, (members, DH), 1)
    pick = jnp.where(lane == 0, BIG, 0.0).astype(BF16)
    scale = factor * LOG2E

    def attend(group_of, queries, keys, values, allowed, prob_ref):
        scores = [
            jnp.where(allowed, nt(jnp.concatenate([q, pick], axis=1), k), -jnp.inf)
            for q, k in zip(queries, keys)
        ]
        tops = [jnp.max(s, axis=-1, keepdims=True) for s in scores]
        grown = [jnp.exp2((s - top) * scale) for s, top in zip(scores, tops)]
        sums = [jnp.sum(e, axis=-1, keepdims=True) for e in grown]
        weights = [(e * (1.0 / total)).astype(BF16) for e, total in zip(grown, sums)]
        for p, w, v, top, total in zip(group_of, weights, values, tops, sums):
            prob_ref[p] = w
            lse = top * scale + jnp.log(total) * LOG2E
            out = jnp.concatenate([nn(w, v), at_lanes((members, DH), in_parts(lse, 3))], axis=1)
            work[p] = out.reshape(2, part, 2 * DH)

    @pl.loop(0, rows16.shape[0], unroll=4)
    def _(p):
        for i, at in enumerate((0, 1, 3)):
            rows = whole(acc, p, slice(i * DH, (i + 1) * DH))
            rows16[p, :, at * DH : (at + 1) * DH] = rows.astype(BF16)
        rows16[p, :, 2 * DH : 3 * DH] = (whole(work, p, one) - 1.0).astype(BF16)

    def by_tokens(hh, b, slot_index):
        rows = sorted_rows(work, hh, b, two)
        return nn(hits_by_token(slots[slot_index, hh], pool), rows)

    for j in range(plane - 1):

        @pl.when(relays & (spot == j))
        def _():
            for i in range(2):
                pltpu.make_async_copy(relay.at[i], relay.at[i], relay_sem.at[i]).wait()
                pass_on(i, j).start()

    @pl.when(early)
    def _():
        for hh in range(each):

            @pl.loop(0, near)
            def _(b):
                got(QX, x_in.at[b, :, hh * DH : (hh + 1) * DH], hh * near + b)

            @pl.loop(0, near, unroll=4)
            def _(b):
                view = x_in[b, :, hh * DH : (hh + 1) * DH]
                sort_into(work, hh, b, one, nn(hits_of(slots[near + b, hh], pool), view))

            @pl.loop(0, pairs // group)
            def _(g):
                group_of = [hh * pairs + g * group + i for i in range(group)]
                queries = [whole(work, p, one).astype(BF16) for p in group_of]
                for p, q in zip(group_of, queries):
                    xq16[p] = q
                keys = [rows16[p, :, DH : 3 * DH] for p in group_of]
                values = [rows16[p, :, 3 * DH :] for p in group_of]
                attend(group_of, queries, keys, values, same, probs_x)

            @pl.loop(0, near, unroll=4)
            def _(b):
                back = by_tokens(hh, b, near + b)
                at = hh * near + b
                view = x_out.at[b, :, hh * DH : (hh + 1) * DH]
                view[...] = back[:, :DH].astype(BF16)
                lse_out[at] = back[:, DH:].T[:8]
                dst = x_in.at[b, :, hh * DH : (hh + 1) * DH]
                remote(OX, view, dst, at, at, me + near).start()
                remote(LX, lse_out.at[at], lse_in.at[at], at, at, me + near).start()

    @pl.loop(0, rows16.shape[0] // group)
    def _(g):
        group_of = [g * group + i for i in range(group)]
        queries = [rows16[p, :, :DH] for p in group_of]
        keys = [rows16[p, :, DH : 3 * DH] for p in group_of]
        values = [rows16[p, :, 3 * DH :] for p in group_of]
        attend(group_of, queries, keys, values, same & (col <= row), probs)

    @pl.loop(0, near, unroll=4)
    def _(b):
        for hh in range(each):
            back = by_tokens(hh, b, b)
            attn_own[b, :, hh * DH : (hh + 1) * DH] = back[:, :DH].astype(BF16)
            lse_own[hh * near + b] = back[:, DH:].T[:8]

    for load in loads:
        load.wait()

    pair[0] = jnp.zeros((8, n), F32)

    for j in range(4):

        @pl.when(me > 0)
        def _():
            for i in range(2):
                view = rim.at[i, :, span[j]]
                pltpu.make_async_copy(view, view, rim_recv.at[i, j]).wait()

        @pl.when(me == 0)
        def _():
            rim[:, :, span[j]] = jnp.zeros((2, n, quarter), BF16)

        @pl.loop(j * (heads // 4), (j + 1) * (heads // 4))
        def _(h):
            cols = columns(h, 1)
            keys = jnp.concatenate([rim[0, :, cols], wk_v[:, cols]], axis=0)
            vals = jnp.concatenate([rim[1, :, cols], wv_v[:, cols]], axis=0)
            prob = window_prob(factor, wq_v[:, cols], keys)
            attn = nn(prob.astype(BF16), vals).astype(BF16)
            attn_win[:, cols] = attn
            gained = wg_v[:, cols].astype(F32) * w_gain[:, cols]
            pair[0] += stat_rows(attn.astype(F32), gained)

    which = lax.broadcasted_iota(jnp.int32, (8, n), 0)

    def gained_of(b, hh):
        gain = c_gain[:, columns(t * each + hh, 1)]
        return taken[b, :, of_head(G, hh)].astype(F32) * gain

    def finish(b, merge):
        total = jnp.zeros((8, n), F32)
        for hh in range(each):
            at = hh * near + b
            lanes = slice(hh * DH, (hh + 1) * DH)
            if merge:
                mine = jnp.sum(lse_own[at][0:3], axis=0, keepdims=True)
                other = jnp.sum(lse_in[at][0:3], axis=0, keepdims=True)
                top = jnp.maximum(mine, other)
                mine, other = jnp.exp2(mine - top), jnp.exp2(other - top)
                share = jnp.where(which == 0, mine, other) / (mine + other)
                shares[at] = share
                by_token = share.T
                attn = by_token[:, 0:1] * attn_own[b, :, lanes].astype(F32)
                attn = attn + by_token[:, 1:2] * x_in[b, :, lanes].astype(F32)
                attn_own[b, :, lanes] = attn.astype(BF16)
            else:
                shares[at] = jnp.where(which == 0, 1.0, 0.0)
        for hh in range(each):
            attn = attn_own[b, :, hh * DH : (hh + 1) * DH].astype(F32)
            total = total + stat_rows(attn, gained_of(b, hh))
        part_out[b] = total
        deliver(PART, part_out.at[b], part_in.at[t], b, b, t)
        deliver(ATTN, attn_own.at[b], attn_home.at[:, columns(t * each, each)], b, b, t)

    for this_half, merge in ((early, False), (late, True)):

        @pl.when(this_half)
        def _():
            @pl.loop(0, near)
            def _(b):
                got(G, into(G, b), b)
                if merge:
                    for hh in range(each):
                        at = hh * near + b
                        got(OX, x_in.at[b, :, hh * DH : (hh + 1) * DH], at)
                        got(LX, lse_in.at[at], at)

            @pl.loop(0, near, unroll=2)
            def _(d):
                finish(peer(d + 1), merge)

    @pl.loop(0, near)
    def _(b):
        got(PART, part_in.at[b], b)
        pair[0] += part_in[b]

    swap = pltpu.make_async_remote_copy(
        src_ref=pair.at[0],
        dst_ref=pair.at[1],
        send_sem=pair_sem.at[0],
        recv_sem=pair_sem.at[1],
        device_id=(me, 1 - core),
        device_id_type=MESH,
    )
    swap.start()
    swap.wait()
    totals = pair[0] + pair[1]
    inv = 1.0 / jnp.sqrt(totals[0:1] / feat_width + EPSILON)
    coef = inv * inv * inv * totals[1:2] / feat_width
    stat_own[...] = jnp.where(which == 0, inv, coef)

    @pl.loop(0, near)
    def _(d):
        b = peer(d + 1)
        deliver(STAT, stat_own, stats.at[t], b, b, t)

    def spread(hh, b, is_late):
        lanes = slice(hh * DH, (hh + 1) * DH)
        at = hh * near + b
        by_token = stats[b].T
        attn = attn_own[b, :, lanes].astype(F32)
        dout = by_token[:, 0:1] * gained_of(b, hh) - by_token[:, 1:2] * attn
        dout = dout.astype(BF16).astype(F32)
        terms = dout * attn
        row_dot = jnp.sum(terms, axis=-1, keepdims=True)
        mine = dout
        if is_late:
            share = shares[at].T
            view = d_out.at[b, :, lanes]
            view[...] = (share[:, 1:2] * dout).astype(BF16)
            high = terms.astype(BF16)
            low = (terms - high.astype(F32)).astype(BF16)
            sums = nt(every, high) + nt(every, low)
            first, second = in_parts(sums * shares[at][1:2], 2)
            dot_out[at] = jnp.where(which == 0, first, jnp.where(which == 1, second, 0.0))
            remote(DX, view, d_in.at[b, :, lanes], at, at, me - near).start()
            remote(RX, dot_out.at[at], dot_in.at[at], at, at, me - near).start()
            mine, row_dot = share[:, 0:1] * dout, share[:, 0:1] * row_dot
        dots = at_lanes((n, DH), in_parts(row_dot, 2)).astype(BF16)
        both = jnp.concatenate([mine.astype(BF16), dots], axis=1)
        sort_into(work, hh, b, two, nn(hits_of(slots[b, hh], pool), both))

    every = jnp.ones((8, DH), BF16)

    def spread_all(is_late):
        @pl.loop(0, near)
        def _(b):
            got(STAT, stats.at[b], b)

        for hh in range(each):

            @pl.loop(0, near, unroll=4)
            def _(d):
                spread(hh, peer(d + 1), is_late)

    @pl.when(late)
    def _():
        spread_all(True)

    @pl.loop(0, near)
    def _(b):
        got(ATTN, attn_home.at[:, columns(b * each, each)], b)

    for j in range(plane - 1):

        @pl.when(relays & (spot == j))
        def _():
            for i in range(2):
                pass_on(i, j).wait_send()

    @pl.when(crosses)
    def _():
        for j in range(4):
            for i in range(2):
                rim_first(i, j, j < plane - 1).wait_send()

    @pl.when(straight)
    def _():
        for j in range(4):
            for i in range(2):
                rim_first(i, j, False).wait_send()

    back_crosses = (spot == 0) & (me > 0)
    back_straight = spot != 0
    back_relays = (spot != 0) & (me >= plane)

    def back_copy(j, src, dst, sem, to):
        return pltpu.make_async_remote_copy(
            src_ref=src,
            dst_ref=dst,
            send_sem=rim_send.at[2, j],
            recv_sem=sem,
            device_id=(to, core),
            device_id_type=MESH,
        )

    def back_first(j, by_relay):
        src = rim.at[:, :, span[j]]
        if by_relay:
            return back_copy(j, src, relay_back, relay_sem.at[2], level * plane + j)
        return back_copy(j, src, rim_back.at[:, :, span[j]], rim_recv.at[2, j], me - 1)

    by_token = stat_own[...].T
    inv_col, coef_col = by_token[:, 0:1], by_token[:, 1:2]
    for j in (1, 2, 3, 0):

        @pl.loop(j * (heads // 4), (j + 1) * (heads // 4))
        def _(h):
            cols = columns(h, 1)
            q = wq_v[:, cols]
            keys = jnp.concatenate([rim[0, :, cols], wk_v[:, cols]], axis=0)
            vals = jnp.concatenate([rim[1, :, cols], wv_v[:, cols]], axis=0)
            attn = attn_win[:, cols].astype(F32)
            gained = wg_v[:, cols].astype(F32) * w_gain[:, cols]
            grad = (inv_col * gained - coef_col * attn).astype(BF16)
            prob = window_prob(factor, q, keys)
            row_dot = jnp.sum(grad.astype(F32) * attn, axis=-1, keepdims=True)
            change = (prob * (nt(grad, vals) - row_dot)).astype(BF16)
            wq_v[:, cols] = (nn(change, keys) * factor).astype(BF16)
            dk = tn(change, q)
            dv = tn(prob.astype(BF16), grad)
            rim[0, :, cols] = dk[:WINDOW].astype(BF16)
            rim[1, :, cols] = dv[:WINDOW].astype(BF16)
            wk_v[:, cols] = dk[WINDOW:].astype(BF16)
            wv_v[:, cols] = dv[WINDOW:].astype(BF16)
            attn_win[:, cols] = (attn * inv_col * w_gain[:, cols]).astype(BF16)
            clu = attn_home[:, cols].astype(F32)
            attn_home[:, cols] = (clu * inv_col * c_gain[:, cols]).astype(BF16)

        @pl.when(back_crosses)
        def _():
            back_first(j, 0 < j < plane).start()

        @pl.when(back_straight)
        def _():
            back_first(j, False).start()

    stores = [
        pltpu.make_async_copy(src, dst, local_sem.at[4 + i])
        for i, (src, dst) in enumerate(
            [
                (attn_win, win_normed),
                (attn_home, clu_normed),
                (wq_v, win_dq),
                (wk_v, win_dk),
                (wv_v, win_dv),
            ]
        )
    ]
    for store in stores[:3]:
        store.start()

    @pl.when(early)
    def _():
        spread_all(False)

    minus = jnp.where(lane < 2, -1.0, 0.0).astype(BF16)

    def changes_of(group_of, prob_ref):
        slopes = []
        for p in group_of:
            v = jnp.concatenate([rows16[p, :, 3 * DH :], minus], axis=1)
            slopes.append(nt(whole(work, p, two).astype(BF16), v))
        return [(prob_ref[p].astype(F32) * s).astype(BF16) for p, s in zip(group_of, slopes)]

    def split_rows(x):
        return x.reshape(2, part, DH)

    second, third = slice(DH, 2 * DH), slice(2 * DH, 3 * DH)

    @pl.loop(0, rows16.shape[0] // group)
    def _(g):
        group_of = [g * group + i for i in range(group)]
        for p, change in zip(group_of, changes_of(group_of, probs)):
            grad = whole(work, p, one).astype(BF16)
            acc[p, :, :, one] = split_rows(nn(change, rows16[p, :, DH : 2 * DH]) * factor)
            acc[p, :, :, second] = split_rows(tn(change, rows16[p, :, :DH]))
            acc[p, :, :, third] = split_rows(tn(probs[p], grad))

    @pl.when(late)
    def _():
        @pl.loop(0, near)
        def _(b):
            for hh in range(each):
                sent(QX, taken.at[b, :, of_head(Q, hh)], hh * near + b)

    homes = [(DQ, clu_dq), (DK, clu_dk), (DV, clu_dv)]

    def home_of(i, hh, owner):
        return homes[i][1].at[:, columns(owner * each + hh, 1)]

    def give(i, hh, b):
        at = hh * near + b
        view = taken.at[b, :, of_head(i, hh)]
        deliver(homes[i][0], view, home_of(i, hh, t), b, at, hh * near + t)

    def keys_home(hh, b, hits):
        rows = sorted_rows(acc, hh, b, slice(DH, 3 * DH))
        back = nn(hits, rows)
        taken[b, :, of_head(1, hh)] = (back[:, :DH] * factor).astype(BF16)
        taken[b, :, of_head(2, hh)] = back[:, DH:].astype(BF16)
        give(1, hh, b)
        give(2, hh, b)

    for hh in range(each):

        def own_home(b, is_late):
            hits = hits_by_token(slots[b, hh], pool)
            taken[b, :, of_head(0, hh)] = nn(hits, sorted_rows(acc, hh, b, one)).astype(BF16)
            if is_late:
                keys_home(hh, b, hits)
            else:
                give(0, hh, b)

        for this_half, is_late in ((early, False), (late, True)):

            @pl.when(this_half)
            def _():
                @pl.loop(0, near, unroll=2)
                def _(d):
                    own_home(peer(d + 1), is_late)

    def pass_back(j):
        dst = rim_back.at[:, :, span[j]]
        return pltpu.make_async_remote_copy(
            src_ref=relay_back,
            dst_ref=dst,
            send_sem=relay_sem.at[3],
            recv_sem=rim_recv.at[2, j],
            device_id=(level * plane - 1, core),
            device_id_type=MESH,
        )

    for j in range(1, plane):

        @pl.when(back_relays & (spot == j))
        def _():
            pltpu.make_async_copy(relay_back, relay_back, relay_sem.at[2]).wait()
            pass_back(j).start()

    @pl.when(early)
    def _():
        for hh in range(each):
            lanes = slice(hh * DH, (hh + 1) * DH)

            @pl.loop(0, near)
            def _(b):
                at = hh * near + b
                got(DX, d_in.at[b, :, lanes], at)
                got(RX, dot_in.at[at], at)
                sent(OX, x_out.at[b, :, lanes], at)

            @pl.loop(0, near, unroll=4)
            def _(b):
                at = hh * near + b
                dots = jnp.concatenate(
                    [dot_in[at].T, jnp.zeros((n, DH - 8), F32)], axis=1
                ).astype(BF16)
                both = jnp.concatenate([d_in[b, :, lanes], dots], axis=1)
                sort_into(work, hh, b, two, nn(hits_of(slots[near + b, hh], pool), both))

            @pl.loop(0, pairs // group)
            def _(g):
                group_of = [hh * pairs + g * group + i for i in range(group)]
                for p, change in zip(group_of, changes_of(group_of, probs_x)):
                    grad = whole(work, p, one).astype(BF16)
                    acc[p, :, :, second] += split_rows(tn(change, xq16[p]))
                    acc[p, :, :, third] += split_rows(tn(probs_x[p], grad))
                    dq = nn(change, rows16[p, :, DH : 2 * DH]) * factor
                    work[p, :, :, one] = split_rows(dq)

            @pl.loop(0, near, unroll=2)
            def _(d):
                b = peer(d + 1)
                at = hh * near + b
                hits = hits_by_token(slots[near + b, hh], pool)
                view = x_out.at[b, :, lanes]
                view[...] = nn(hits, sorted_rows(work, hh, b, one)).astype(BF16)
                remote(DQX, view, d_in.at[b, :, lanes], at, at, me + near).start()

            @pl.loop(0, near, unroll=2)
            def _(d):
                b = peer(d + 1)
                keys_home(hh, b, hits_by_token(slots[b, hh], pool))

    @pl.when(late)
    def _():
        for hh in range(each):
            lanes = slice(hh * DH, (hh + 1) * DH)

            @pl.loop(0, near)
            def _(d):
                b = peer(d + 1)
                got(DQX, d_in.at[b, :, lanes], hh * near + b)
                more = d_in[b, :, lanes].astype(F32)
                view = taken.at[b, :, of_head(0, hh)]
                view[...] = (view[...].astype(F32) + more).astype(BF16)
                give(0, hh, b)

    @pl.when(me < n_seq - 1)
    def _():
        for j in range(4):
            view = rim_back.at[:, :, span[j]]
            pltpu.make_async_copy(view, view, rim_recv.at[2, j]).wait()

    @pl.when(me == n_seq - 1)
    def _():
        rim_back[...] = jnp.zeros_like(rim_back)

    @pl.loop(0, heads)
    def _(h):
        cols = columns(h, 1)
        dk = wk_v[:, cols].astype(F32) + rim_back[0, :, cols].astype(F32)
        wk_v[:, cols] = (dk * factor).astype(BF16)
        dv = wv_v[:, cols].astype(F32) + rim_back[1, :, cols].astype(F32)
        wv_v[:, cols] = dv.astype(BF16)

    for store in stores[3:]:
        store.start()

    for j in range(4):

        @pl.when(back_crosses)
        def _():
            back_first(j, 0 < j < plane).wait_send()

        @pl.when(back_straight)
        def _():
            back_first(j, False).wait_send()

    for j in range(1, plane):

        @pl.when(back_relays & (spot == j))
        def _():
            pass_back(j).wait_send()

    @pl.loop(1, near)
    def _(d):
        to = peer(d)
        for kind, src in arrays:
            sent(kind, src.at[:, columns(to * each, each)], to)
        sent(IDS, ids.at[pl.ds(to * each, each)], to)
        sent(PART, part_out.at[to], to)
        sent(ATTN, attn_own.at[to], to)
        sent(STAT, stat_own, to)
        for hh in range(each):
            for i, (kind, home) in enumerate(homes):
                sent(kind, taken.at[to, :, of_head(i, hh)], hh * near + to)

    @pl.loop(0, near)
    def _(b):
        for hh in range(each):
            for i, (kind, home) in enumerate(homes):
                got(kind, home_of(i, hh, b), hh * near + b)

    @pl.when(late)
    def _():
        @pl.loop(0, near)
        def _(b):
            sent(IDSX, ids.at[pl.ds(b * each, each)], b)
            for hh in range(each):
                at = hh * near + b
                sent(DX, d_out.at[b, :, hh * DH : (hh + 1) * DH], at)
                sent(RX, dot_out.at[at], at)

    @pl.when(early)
    def _():
        @pl.loop(0, near)
        def _(b):
            for hh in range(each):
                at = hh * near + b
                sent(LX, lse_out.at[at], at)
                sent(DQX, x_out.at[b, :, hh * DH : (hh + 1) * DH], at)

    for store in stores:
        store.wait()


def copy_kernel(*refs):
    count = len(refs) // 2
    for src, dst in zip(refs[:count], refs[count:]):
        dst[...] = src[...]


def settle(arrays):
    n, wide = arrays[0].shape
    block = pl.BlockSpec((n // 8, wide), lambda i: (i, 0))
    return pl.pallas_call(
        copy_kernel,
        grid=(8,),
        in_specs=[block] * len(arrays),
        out_specs=[block] * len(arrays),
        out_shape=[jax.ShapeDtypeStruct((n, wide), BF16)] * len(arrays),
        compiler_params=pltpu.CompilerParams(vmem_limit_bytes=32 << 20),
    )(*arrays)


def layer(*arrays):
    win_query, cluster_ids = arrays[0], arrays[6]
    n, wide = win_query.shape
    sources = lax.axis_size("seq")
    near = sources // 2
    cap = SLOTS // sources
    clusters = sources * (2 * n // SLOTS)
    part = near * cap
    heads = wide // DH
    each = heads // near
    pairs = each * clusters // 2
    given = list(arrays)
    given[6] = cluster_ids[:, None, :]
    given[7], given[8] = arrays[7][None, :], arrays[8][None, :]
    anywhere = pl.BlockSpec(memory_space=pl.ANY)
    vmem = pl.BlockSpec(memory_space=pltpu.VMEM)
    group = next(g for g in (16, 8, 4, 2, 1) if clusters // 2 % g == 0)
    rows_of = pltpu.VMEM((each * near, 8, n), F32)
    results = pl.pallas_call(
        functools.partial(layer_kernel, DH ** (-0.5), cap, group, 4),
        in_specs=[anywhere] * 6 + [vmem] * 3 + [anywhere] * 2,
        out_specs=[anywhere] * 8,
        out_shape=[jax.ShapeDtypeStruct((n, wide), BF16)] * 8,
        scratch_shapes=[
            pltpu.VMEM((near, n, 4 * each * DH), BF16),
            pltpu.VMEM((sources, each, 1, n), jnp.int32),
            pltpu.VMEM((sources, each, 1, n), jnp.int32),
        ]
        + [pltpu.VMEM((n, wide), BF16)] * 4
        + [pltpu.VMEM((2, n, wide), BF16)] * 2
        + [pltpu.VMEM((2, n, wide // 4), BF16)] * 2
        + [pltpu.VMEM((n, wide), BF16)] * 2
        + [pltpu.VMEM((near, n, each * DH), BF16)] * 5
        + [
            pltpu.VMEM((pairs, 2 * part, 4 * DH), BF16),
            pltpu.VMEM((pairs, 2 * part, DH), BF16),
            pltpu.VMEM((pairs, 2, part, 2 * DH), F32),
            pltpu.VMEM((pairs, 2, part, 3 * DH), F32),
            pltpu.VMEM((pairs, 2 * part, 2 * part), BF16),
            pltpu.VMEM((pairs, 2 * part, 2 * part), BF16),
        ]
        + [rows_of] * 6
        + [
            pltpu.VMEM((near, 8, n), F32),
            pltpu.VMEM((near, 8, n), F32),
            pltpu.VMEM((2, 8, n), F32),
            pltpu.VMEM((8, n), F32),
            pltpu.VMEM((near, 8, n), F32),
            pltpu.SemaphoreType.DMA((18, sources)),
            pltpu.SemaphoreType.DMA((18, sources)),
            pltpu.SemaphoreType.DMA((3, 4)),
            pltpu.SemaphoreType.DMA((3, 4)),
            pltpu.SemaphoreType.DMA((6,)),
            pltpu.SemaphoreType.DMA((2,)),
            pltpu.SemaphoreType.DMA((9,)),
        ],
        cost_estimate=pl.CostEstimate(
            flops=14 * n * 2 * n * wide, bytes_accessed=16 * n * wide * 2, transcendentals=0
        ),
        compiler_params=pltpu.CompilerParams(
            vmem_limit_bytes=60 << 20, collective_id=0, has_side_effects=True
        ),
    )(*given)
    return settle(results)


def solution(mesh):
    sources, split = mesh.shape["seq"], mesh.shape["head"]
    whole_heads = HC // split == sources and SLOTS // sources % 8 == 0 and split == 2 and sources % 4 == 0
    return jax.shard_map(
        layer if whole_heads else body,
        mesh=mesh,
        in_specs=(P("seq", "head"),) * 6
        + (P("head", "seq"), P("head"), P("head"))
        + (P("seq", "head"),) * 2,
        out_specs=(P("seq", "head"),) * 8,
        check_vma=False,
    )
```

```python
import functools

import jax
import jax.numpy as jnp
from jax import lax
from jax.experimental import pallas as pl
from jax.experimental.pallas import tpu as pltpu
from jax.sharding import PartitionSpec as P

HW = 32
HC = 32
DH = 128
WINDOW = 256
SLOTS = 128
CHUNKS = 2

EPSILON = 1e-06
F32 = jnp.float32
BF16 = jnp.bfloat16


def from_behind(block, axis, distance):
    devices = range(lax.axis_size(axis))
    route = [(i - distance, i) for i in devices if i - distance in devices]
    return lax.ppermute(block, axis, route)


def nt(a, b):
    return lax.dot_general(a, b, (((1,), (1,)), ((), ())), preferred_element_type=F32)


def tn(a, b):
    return lax.dot_general(a, b, (((0,), (0,)), ((), ())), preferred_element_type=F32)


def nn(a, b):
    return jnp.dot(a, b, preferred_element_type=F32)


def one_hot(slot_ref, pool):
    n = slot_ref.shape[-1]
    hit = lax.broadcasted_iota(jnp.int32, (pool, n), 0) == slot_ref[0]
    return jnp.where(hit, 1.0, 0.0).astype(BF16)


def normalized(scores, allowed):
    masked = jnp.where(allowed, scores, -jnp.inf)
    grown = jnp.exp(masked - jnp.max(masked, axis=-1, keepdims=True))
    return grown * (1.0 / jnp.sum(grown, axis=-1, keepdims=True))


def call(kernel, grid, in_specs, out_specs, out_shape, flops, size, **more):
    return pl.pallas_call(
        kernel,
        grid=grid,
        in_specs=in_specs,
        out_specs=out_specs,
        out_shape=out_shape,
        cost_estimate=pl.CostEstimate(flops=flops, bytes_accessed=size, transcendentals=0),
        compiler_params=pltpu.CompilerParams(vmem_limit_bytes=48 << 20),
        **more,
    )


def dispatch_kernel(*refs):
    slot_ref, value_refs, out_ref = refs[0], refs[1:-1], refs[-1]
    picked = one_hot(slot_ref, out_ref.shape[0])
    for i, ref in enumerate(value_refs):
        out_ref[:, i * DH : (i + 1) * DH] = nn(picked, ref[...]).astype(BF16)


def dispatch(slot_at, values, first, count, pool):
    n = slot_at.shape[-1]
    wide = len(values) * DH
    return call(
        dispatch_kernel,
        (count,),
        [pl.BlockSpec((1, 1, n), lambda h: (h + first, 0, 0))]
        + [pl.BlockSpec((n, DH), lambda h: (0, h + first)) for _ in values],
        pl.BlockSpec((pool, wide), lambda h: (0, h)),
        jax.ShapeDtypeStruct((pool, count * wide), BF16),
        2 * count * pool * n * wide,
        2 * count * (pool + n) * wide,
    )(slot_at, *values)


def collect_kernel(n_out, *refs):
    slot_ref, rows_ref, out_refs = refs[0], refs[1], refs[-n_out:]
    picked = one_hot(slot_ref, rows_ref.shape[0])
    merged = tn(picked, rows_ref[...]).astype(BF16)
    for i, ref in enumerate(out_refs):
        ref[...] = merged[:, i * DH : (i + 1) * DH]


def collect(slot_at, rows, first, count, n_out, earlier):
    n = slot_at.shape[-1]
    pool = rows.shape[0]
    heads = slot_at.shape[0]
    wide = n_out * DH
    return call(
        functools.partial(collect_kernel, n_out),
        (count,),
        [
            pl.BlockSpec((1, 1, n), lambda h: (h + first, 0, 0)),
            pl.BlockSpec((pool, wide), lambda h: (0, h)),
        ]
        + [pl.BlockSpec(memory_space=pl.ANY) for _ in earlier],
        [pl.BlockSpec((n, DH), lambda h: (0, h + first))] * n_out,
        [jax.ShapeDtypeStruct((n, heads * DH), BF16)] * n_out,
        2 * count * pool * n * wide,
        2 * count * (pool + n) * wide,
        input_output_aliases={2 + i: i for i in range(len(earlier))},
    )(slot_at, rows, *earlier)


class Rows:
    def __init__(self, sources, owned, cap):
        self.sources, self.owned, self.cap = sources, owned, cap
        self.aligned = cap % 8 == 0

    def selector(self, c):
        members = self.sources * self.cap
        layout = (members, members * self.owned)
        member = lax.broadcasted_iota(jnp.int32, layout, 0)
        row = lax.broadcasted_iota(jnp.int32, layout, 1)
        want = member // self.cap * (self.cap * self.owned) + c * self.cap + member % self.cap
        return jnp.where(row == want, 1.0, 0.0).astype(BF16)

    def split(self, rows):
        members = self.sources * self.cap
        if not self.aligned:
            return [nn(self.selector(c), rows).astype(BF16) for c in range(self.owned)]
        wide = rows.shape[1]
        four = rows.astype(F32).reshape(self.sources, self.owned, self.cap, wide)
        return [four[:, c].reshape(members, wide).astype(BF16) for c in range(self.owned)]

    def join(self, parts):
        wide = parts[0].shape[1]
        pool = self.sources * self.cap * self.owned
        if not self.aligned:
            total = jnp.zeros((pool, wide), F32)
            for c, part in enumerate(parts):
                total = total + tn(self.selector(c), part.astype(BF16))
            return total.astype(BF16)
        shaped = [p.reshape(self.sources, 1, self.cap, wide) for p in parts]
        return jnp.concatenate(shaped, axis=1).reshape(pool, wide).astype(BF16)


def cluster_allowed(live_ref, c, members):
    row = lax.broadcasted_iota(jnp.int32, (members, members), 0)
    col = lax.broadcasted_iota(jnp.int32, (members, members), 1)
    live = jnp.broadcast_to(live_ref[0, c : c + 1, :], (members, members)) > 0.5
    return (live & (col <= row)) | (col == row)


def owner_fwd_kernel(rows, factor, live_ref, qkv_ref, out_ref):
    members = rows.sources * rows.cap
    parts = []
    for c, qkv in enumerate(rows.split(qkv_ref[...])):
        q, k, v = qkv[:, :DH], qkv[:, DH : 2 * DH], qkv[:, 2 * DH :]
        prob = normalized(nt(q, k) * factor, cluster_allowed(live_ref, c, members))
        parts.append(nn(prob.astype(BF16), v))
    out_ref[...] = rows.join(parts)


def owner_bwd_kernel(rows, factor, live_ref, qkv_ref, attn_ref, grad_ref, out_ref):
    members = rows.sources * rows.cap
    attn_parts = rows.split(attn_ref[...])
    grad_parts = rows.split(grad_ref[...])
    parts = []
    for c, qkv in enumerate(rows.split(qkv_ref[...])):
        q, k, v = qkv[:, :DH], qkv[:, DH : 2 * DH], qkv[:, 2 * DH :]
        grad = grad_parts[c]
        row_dot = jnp.sum(grad.astype(F32) * attn_parts[c].astype(F32), axis=-1, keepdims=True)
        prob = normalized(nt(q, k) * factor, cluster_allowed(live_ref, c, members))
        change = (prob * (nt(grad, v) - row_dot)).astype(BF16)
        dq = nn(change, k) * factor
        dk = tn(change, q) * factor
        dv = tn(prob.astype(BF16), grad)
        parts.append(jnp.concatenate([dq, dk, dv], axis=1))
    out_ref[...] = rows.join(parts)


def owner_call(kernel, rows, factor, live, first, arrays, n_out):
    pool = arrays[0].shape[0]
    count = arrays[0].shape[1] // (3 * DH)
    members = rows.sources * rows.cap
    wides = [a.shape[1] // count for a in arrays]
    return call(
        functools.partial(kernel, rows, factor),
        (count,),
        [pl.BlockSpec((1, rows.owned, members), lambda h: (h + first, 0, 0))]
        + [pl.BlockSpec((pool, w), lambda h: (0, h)) for w in wides],
        pl.BlockSpec((pool, n_out * DH), lambda h: (0, h)),
        jax.ShapeDtypeStruct((pool, count * n_out * DH), BF16),
        12 * count * pool * members * DH,
        2 * count * pool * (sum(wides) + n_out * DH),
    )(live, *arrays)


def window_prob(factor, q, keys):
    n = q.shape[0]
    row = lax.broadcasted_iota(jnp.int32, (n, n + WINDOW), 0)
    col = lax.broadcasted_iota(jnp.int32, (n, n + WINDOW), 1)
    gap = row + WINDOW - col
    lowest = jnp.where(lax.axis_index("seq") > 0, 0, WINDOW)
    allowed = (gap >= 0) & (gap < WINDOW) & (col >= lowest)
    return normalized(nt(q, keys) * factor, allowed)


def window_fwd_kernel(factor, q_ref, kp_ref, k_ref, vp_ref, v_ref, out_ref):
    keys = jnp.concatenate([kp_ref[0], k_ref[...]], axis=0)
    vals = jnp.concatenate([vp_ref[0], v_ref[...]], axis=0)
    prob = window_prob(factor, q_ref[...], keys)
    out_ref[...] = nn(prob.astype(BF16), vals).astype(BF16)


def window_bwd_kernel(
    factor, q_ref, kp_ref, k_ref, vp_ref, v_ref, attn_ref, grad_ref, dq_ref, dk_ref, dv_ref, rim_ref
):
    q, grad = q_ref[...], grad_ref[...]
    keys = jnp.concatenate([kp_ref[0], k_ref[...]], axis=0)
    vals = jnp.concatenate([vp_ref[0], v_ref[...]], axis=0)
    prob = window_prob(factor, q, keys)
    row_dot = jnp.sum(grad.astype(F32) * attn_ref[...].astype(F32), axis=-1, keepdims=True)
    change = (prob * (nt(grad, vals) - row_dot)).astype(BF16)
    dq_ref[...] = (nn(change, keys) * factor).astype(BF16)
    dk = tn(change, q)
    dv = tn(prob.astype(BF16), grad)
    rim_ref[0] = dk[:WINDOW].astype(BF16)
    rim_ref[1] = dv[:WINDOW].astype(BF16)
    dk_ref[...] = dk[WINDOW:]
    dv_ref[...] = dv[WINDOW:]


def window_specs(n):
    here = pl.BlockSpec((n, DH), lambda h: (0, h))
    key = pl.BlockSpec((1, n, DH), lambda h: (0, 0, h))
    val = pl.BlockSpec((1, n, DH), lambda h: (1, 0, h))
    return here, key, val


def window_fwd(factor, query, key, value, before):
    n, wide = query.shape
    here, rim_key, rim_val = window_specs(n)
    return call(
        functools.partial(window_fwd_kernel, factor),
        (wide // DH,),
        [here, rim_key, here, rim_val, here],
        here,
        jax.ShapeDtypeStruct((n, wide), BF16),
        4 * n * 2 * n * wide,
        12 * n * wide,
    )(query, before, key, before, value)


def window_bwd(factor, query, key, value, before, attn, grad):
    n, wide = query.shape
    here, rim_key, rim_val = window_specs(n)
    return call(
        functools.partial(window_bwd_kernel, factor),
        (wide // DH,),
        [here, rim_key, here, rim_val, here, here, here],
        [here, here, here, pl.BlockSpec((2, n, DH), lambda h: (0, 0, h))],
        [
            jax.ShapeDtypeStruct((n, wide), BF16),
            jax.ShapeDtypeStruct((n, wide), F32),
            jax.ShapeDtypeStruct((n, wide), F32),
            jax.ShapeDtypeStruct((2, n, wide), BF16),
        ],
        10 * n * 2 * n * wide,
        28 * n * wide,
    )(query, before, key, before, value, attn, grad)


def body(
    win_query,
    win_key,
    win_value,
    clu_query,
    clu_key,
    clu_value,
    cluster_ids,
    win_gain,
    clu_gain,
    win_out_grad,
    clu_out_grad,
):
    n_rows = win_query.shape[0]
    factor = DH ** (-0.5)
    feat_width = (HW + HC) * DH
    sources = lax.axis_size("seq")
    n_cap = SLOTS // sources
    owned_count = 2 * n_rows // SLOTS
    pool_size = 2 * n_rows
    clu_heads = clu_query.shape[1] // DH
    rows = Rows(sources, owned_count, n_cap)

    def exchange(values):
        shaped = values.reshape(sources, pool_size // sources, values.shape[1])
        moved = lax.all_to_all(shaped, "seq", split_axis=0, concat_axis=0, tiled=True)
        return moved.reshape(values.shape)

    row_ids = lax.broadcasted_iota(jnp.int32, (n_rows, n_rows), 0)
    col_ids = lax.broadcasted_iota(jnp.int32, (n_rows, n_rows), 1)
    same_cluster = (cluster_ids[:, :, None] == cluster_ids[:, None, :]) & (col_ids < row_ids)
    rank_in = jnp.sum(same_cluster.astype(jnp.int32), axis=-1)
    slot_at = (cluster_ids * n_cap + rank_in)[:, None, :]

    n_clusters = sources * owned_count
    every = lax.broadcasted_iota(jnp.int32, (n_clusters, clu_heads, n_rows), 0)
    counts = jnp.sum((cluster_ids[None] == every).astype(F32), axis=-1)
    counts = counts.reshape(sources, owned_count, clu_heads)
    counts = lax.all_to_all(counts, "seq", split_axis=0, concat_axis=0, tiled=True)
    slot_pos = lax.broadcasted_iota(F32, (clu_heads, owned_count, sources, n_cap), 3)
    live = (slot_pos < counts.transpose(2, 1, 0)[..., None]).astype(F32)
    live = live.reshape(clu_heads, owned_count, sources * n_cap)

    chunks = CHUNKS if clu_heads % CHUNKS == 0 else 1
    per = clu_heads // chunks
    starts = [i * per for i in range(chunks)]

    held = [
        exchange(dispatch(slot_at, [clu_query, clu_key, clu_value], first, per, pool_size))
        for first in starts
    ]
    before = from_behind(jnp.stack([win_key, win_value]), "seq", 1)
    attn_win = window_fwd(factor, win_query, win_key, win_value, before)

    attn_held = [
        owner_call(owner_fwd_kernel, rows, factor, live, first, [qkv], 1)
        for first, qkv in zip(starts, held)
    ]
    attn_back = [exchange(part) for part in attn_held]
    attn_clu = ()
    for first, part in zip(starts, attn_back):
        attn_clu = collect(slot_at, part, first, per, 1, attn_clu)
    attn_clu = attn_clu[0]

    flat_win = attn_win.astype(F32)
    flat_clu = attn_clu.astype(F32)
    grad_win = win_out_grad.astype(F32) * win_gain
    grad_clu = clu_out_grad.astype(F32) * clu_gain
    totals = jnp.stack(
        [
            jnp.sum(flat_win * flat_win, axis=1) + jnp.sum(flat_clu * flat_clu, axis=1),
            jnp.sum(grad_win * flat_win, axis=1) + jnp.sum(grad_clu * flat_clu, axis=1),
        ]
    )
    totals = lax.psum(totals, "head")
    sq_total, dot_total = totals[0], totals[1]
    inv_rms = 1.0 / jnp.sqrt(sq_total / feat_width + EPSILON)
    coef_rows = inv_rms**3 * dot_total / feat_width
    dout_clu = (inv_rms[:, None] * grad_clu - coef_rows[:, None] * flat_clu).astype(BF16)
    dout_win = (inv_rms[:, None] * grad_win - coef_rows[:, None] * flat_win).astype(BF16)
    win_normed = (flat_win * inv_rms[:, None] * win_gain).astype(BF16)
    clu_normed = (flat_clu * inv_rms[:, None] * clu_gain).astype(BF16)

    grad_held = [
        exchange(dispatch(slot_at, [dout_clu], first, per, pool_size)) for first in starts
    ]
    win_dq, key_own, val_own, rim = window_bwd(
        factor, win_query, win_key, win_value, before, attn_win, dout_win
    )
    after_rim = from_behind(rim, "seq", -1)

    clu_grads = ()
    sent = [
        owner_call(owner_bwd_kernel, rows, factor, live, first, [qkv, part, grad], 3)
        for first, qkv, part, grad in zip(starts, held, attn_held, grad_held)
    ]
    home = [exchange(part) for part in sent]
    win_dk = ((key_own + after_rim[0]) * factor).astype(BF16)
    win_dv = (val_own + after_rim[1]).astype(BF16)
    for first, part in zip(starts, home):
        clu_grads = collect(slot_at, part, first, per, 3, clu_grads)
    return (win_normed, clu_normed, win_dq, win_dk, win_dv, *clu_grads)


BIG = 1e30
MESH = pl.DeviceIdType.MESH
LOG2E = 1.4426950408889634


def hits_of(slot, pool):
    n = slot.shape[-1]
    hit = lax.broadcasted_iota(jnp.int32, (pool, n), 0) == slot
    return jnp.where(hit, 1.0, 0.0).astype(BF16)


def hits_by_token(slot, pool):
    n = slot.shape[-1]
    column = jnp.broadcast_to(slot.astype(F32), (8, n)).T[:, :1].astype(jnp.int32)
    hit = lax.broadcasted_iota(jnp.int32, (n, pool), 1) == column
    return jnp.where(hit, 1.0, 0.0).astype(BF16)


def stat_rows(attn, gained):
    wide = attn.shape[1]
    both = jnp.concatenate([attn * attn, gained * attn], axis=1)
    row = lax.broadcasted_iota(jnp.int32, (8, 2 * wide), 0)
    col = lax.broadcasted_iota(jnp.int32, (8, 2 * wide), 1)
    pick = jnp.where(col // wide == row, 1.0, 0.0).astype(BF16)
    high = both.astype(BF16)
    low = (both - high.astype(F32)).astype(BF16)
    return nt(pick, high) + nt(pick, low)


def head_cols(h):
    return pl.ds(pl.multiple_of(h * DH, DH), DH)


def columns(first, count):
    return pl.ds(pl.multiple_of(first * DH, DH), count * DH)


def at_lanes(shape, values):
    lane = lax.broadcasted_iota(jnp.int32, shape, 1)
    total = jnp.zeros(shape, F32)
    for i, value in enumerate(values):
        total = jnp.where(lane == i, value, total)
    return total


def in_parts(x, count):
    parts = []
    for _ in range(count - 1):
        parts.append(x.astype(BF16).astype(F32))
        x = x - parts[-1]
    return parts + [x]


def layer_kernel(
    factor,
    cap,
    group,
    plane,
    wq,
    wk,
    wv,
    cq,
    ck,
    cv,
    ids,
    w_gain,
    c_gain,
    wg,
    cg,
    win_normed,
    clu_normed,
    win_dq,
    win_dk,
    win_dv,
    clu_dq,
    clu_dk,
    clu_dv,
    taken,
    ids_in,
    slots,
    wq_v,
    wk_v,
    wv_v,
    wg_v,
    rim,
    rim_back,
    relay,
    relay_back,
    attn_win,
    attn_home,
    attn_own,
    x_in,
    d_in,
    x_out,
    d_out,
    rows16,
    xq16,
    work,
    acc,
    probs,
    probs_x,
    lse_own,
    lse_out,
    lse_in,
    dot_out,
    dot_in,
    shares,
    part_out,
    part_in,
    pair,
    stat_own,
    stats,
    send_sem,
    recv_sem,
    rim_send,
    rim_recv,
    relay_sem,
    pair_sem,
    local_sem,
):
    me, core = lax.axis_index("seq"), lax.axis_index("head")
    n_seq = lax.axis_size("seq")
    near = n_seq // 2
    half, t = me // near, lax.rem(me, near)
    base = half * near
    early, late = half == 0, half == 1
    n = wq.shape[0]
    heads = wq.shape[1] // DH
    each = heads // near
    pairs = rows16.shape[0] // each
    members = rows16.shape[1]
    part = members // 2
    clusters = 2 * pairs
    pool = clusters * cap
    feat_width = (HW + HC) * DH
    (Q, K, V, G, IDS, IDSX, QX, OX, LX, PART, ATTN, STAT, DX, RX, DQX, DQ, DK, DV) = range(18)

    def peer(d):
        d = lax.rem(d, near)
        return jnp.bitwise_xor(t, d) if near & (near - 1) == 0 else lax.rem(t + d, near)

    def remote(kind, src, dst, mine, theirs, to):
        return pltpu.make_async_remote_copy(
            src_ref=src,
            dst_ref=dst,
            send_sem=send_sem.at[kind, mine],
            recv_sem=recv_sem.at[kind, theirs],
            device_id=(to, core),
            device_id_type=MESH,
        )

    def got(kind, dst, index):
        pltpu.make_async_copy(dst, dst, recv_sem.at[kind, index]).wait()

    def sent(kind, src, index):
        pltpu.make_async_copy(src, src, send_sem.at[kind, index]).wait()

    def deliver(kind, src, dst, b, mine, theirs):
        @pl.when(b != t)
        def _():
            remote(kind, src, dst, mine, theirs, base + b).start()

        @pl.when(b == t)
        def _():
            pltpu.make_async_copy(src, dst, recv_sem.at[kind, theirs]).start()

    loads = [
        pltpu.make_async_copy(src, dst, local_sem.at[i])
        for i, (src, dst) in enumerate([(wq, wq_v), (wk, wk_v), (wv, wv_v), (wg, wg_v)])
    ]

    barrier = pltpu.get_barrier_semaphore()

    @pl.loop(1, n_seq)
    def _(d):
        to = lax.rem(me + d, n_seq)
        pl.semaphore_signal(barrier, inc=1, device_id=(to, core), device_id_type=MESH)

    pl.semaphore_signal(barrier, inc=1, device_id=(me, 1 - core), device_id_type=MESH)
    pl.semaphore_wait(barrier, n_seq)

    @pl.loop(0, near)
    def _(d):
        to = peer(d)
        view = ids.at[pl.ds(to * each, each)]
        deliver(IDS, view, ids_in.at[t], to, to, t)

        @pl.when(late)
        def _():
            remote(IDSX, view, ids_in.at[near + t], to, t, to).start()

    spot, level = lax.rem(me, plane), me // plane
    quarter = heads // 4 * DH
    span = [slice(j * quarter, (j + 1) * quarter) for j in range(4)]
    crosses = (spot == plane - 1) & (me < n_seq - 1)
    straight = (spot != plane - 1) & (me < n_seq - 1)
    relays = (spot != plane - 1) & (me < n_seq - plane)

    def rim_copy(i, j, src, dst, sem, to):
        return pltpu.make_async_remote_copy(
            src_ref=src,
            dst_ref=dst,
            send_sem=rim_send.at[i, j],
            recv_sem=sem,
            device_id=(to, core),
            device_id_type=MESH,
        )

    def rim_first(i, j, by_relay):
        src = (wk, wv)[i].at[:, span[j]]
        if by_relay:
            return rim_copy(i, j, src, relay.at[i], relay_sem.at[i], level * plane + j)
        return rim_copy(i, j, src, rim.at[i, :, span[j]], rim_recv.at[i, j], me + 1)

    arrays = [(Q, cq), (K, ck), (V, cv), (G, cg)]

    def into(kind, source):
        return taken.at[source, :, kind * each * DH : (kind + 1) * each * DH]

    def of_head(kind, hh):
        return slice((kind * each + hh) * DH, (kind * each + hh + 1) * DH)

    def exchange(some):
        @pl.loop(1, near)
        def _(d):
            to = peer(d)
            for kind, src in some:
                view = src.at[:, columns(to * each, each)]
                remote(kind, view, into(kind, t), to, t, base + to).start()

    exchange(arrays[:1])

    @pl.when(crosses)
    def _():
        for j in range(4):
            for i in range(2):
                rim_first(i, j, j < plane - 1).start()

    @pl.when(early)
    def _():
        exchange(arrays[1:3])

    for kind, src in arrays:
        view = src.at[:, columns(t * each, each)]
        pltpu.make_async_copy(view, into(kind, t), recv_sem.at[kind, t]).start()
    for load in loads:
        load.start()

    @pl.when(late)
    def _():
        for hh in range(each):

            @pl.loop(0, near)
            def _(b):
                if hh == 0:
                    got(Q, into(Q, b), b)
                view = taken.at[b, :, of_head(Q, hh)]
                dst = x_in.at[b, :, hh * DH : (hh + 1) * DH]
                remote(QX, view, dst, hh * near + b, hh * near + b, me - near).start()

    @pl.when(late)
    def _():
        exchange(arrays[1:3])

        @pl.when(straight)
        def _():
            for j in range(4):
                for i in range(2):
                    rim_first(i, j, False).start()

    earlier = lax.broadcasted_iota(jnp.int32, (n, n), 0) < lax.broadcasted_iota(
        jnp.int32, (n, n), 1
    )
    earlier = jnp.where(earlier, 1.0, 0.0).astype(BF16)

    def place(b):
        for hh in range(each):
            of_block = ids_in[b, hh]
            member = hits_of(of_block, clusters)
            rank = jnp.sum(member.astype(F32) * nn(member, earlier), axis=0, keepdims=True)
            slots[b, hh] = of_block * cap + rank.astype(jnp.int32)

    @pl.loop(0, near)
    def _(b):
        got(IDS, ids_in.at[b], b)
        place(b)

    @pl.when(early)
    def _():
        @pl.loop(0, near)
        def _(b):
            got(IDSX, ids_in.at[near + b], b)
            place(near + b)

    def pass_on(i, j):
        return pltpu.make_async_remote_copy(
            src_ref=relay.at[i],
            dst_ref=rim.at[i, :, span[j]],
            send_sem=relay_sem.at[4 + i],
            recv_sem=rim_recv.at[i, j],
            device_id=((level + 1) * plane, core),
            device_id_type=MESH,
        )

    def block_rows(b):
        return pl.ds(pl.multiple_of(b * cap, cap), cap)

    def sort_into(ref, hh, b, lanes, rows):
        shaped = rows.reshape(pairs, 2, cap, rows.shape[1])
        ref[hh * pairs : (hh + 1) * pairs, :, block_rows(b), lanes] = shaped

    def sorted_rows(ref, hh, b, lanes):
        rows = ref[hh * pairs : (hh + 1) * pairs, :, block_rows(b), lanes]
        return rows.reshape(pool, rows.shape[3]).astype(BF16)

    def whole(ref, p, lanes):
        return ref[p, :, :, lanes].reshape(members, lanes.stop - lanes.start)

    one, two = slice(0, DH), slice(0, 2 * DH)

    for j in range(plane - 1):

        @pl.when(relays & (spot == j))
        def _():
            for i in range(2):
                pltpu.make_async_copy(relay.at[i], relay.at[i], relay_sem.at[i]).wait()
                pass_on(i, j).start()

    @pl.loop(0, near)
    def _(b):
        for kind in (K, V):
            got(kind, into(kind, b), b)

    @pl.when(early)
    def _():
        @pl.loop(0, near)
        def _(b):
            got(Q, into(Q, b), b)

    @pl.when(straight & early)
    def _():
        for j in range(4):
            for i in range(2):
                rim_first(i, j, False).start()

    @pl.when(late)
    def _():
        exchange(arrays[3:])

    @pl.loop(0, near, unroll=4)
    def _(b):
        for hh in range(each):
            values = jnp.concatenate(
                [taken[b, :, of_head(kind, hh)] for kind in (Q, K, V)]
                + [jnp.ones((n, DH), BF16)],
                axis=1,
            )
            rows = nn(hits_of(slots[b, hh], pool), values)
            sort_into(acc, hh, b, slice(0, 3 * DH), rows[:, : 3 * DH])
            sort_into(work, hh, b, one, rows[:, 3 * DH :])

    row = lax.broadcasted_iota(jnp.int32, (members, members), 0)
    col = lax.broadcasted_iota(jnp.int32, (members, members), 1)
    same = (row // part) == (col // part)
    lane = lax.broadcasted_iota(jnp.int32, (members, DH), 1)
    pick = jnp.where(lane == 0, BIG, 0.0).astype(BF16)
    scale = factor * LOG2E

    def attend(group_of, queries, keys, values, allowed, prob_ref):
        scores = [
            jnp.where(allowed, nt(jnp.concatenate([q, pick], axis=1), k), -jnp.inf)
            for q, k in zip(queries, keys)
        ]
        tops = [jnp.max(s, axis=-1, keepdims=True) for s in scores]
        grown = [jnp.exp2((s - top) * scale) for s, top in zip(scores, tops)]
        sums = [jnp.sum(e, axis=-1, keepdims=True) for e in grown]
        weights = [(e * (1.0 / total)).astype(BF16) for e, total in zip(grown, sums)]
        for p, w, v, top, total in zip(group_of, weights, values, tops, sums):
            prob_ref[p] = w
            lse = top * scale + jnp.log(total) * LOG2E
            out = jnp.concatenate([nn(w, v), at_lanes((members, DH), in_parts(lse, 3))], axis=1)
            work[p] = out.reshape(2, part, 2 * DH)

    @pl.loop(0, rows16.shape[0], unroll=4)
    def _(p):
        for i, at in enumerate((0, 1, 3)):
            rows = whole(acc, p, slice(i * DH, (i + 1) * DH))
            rows16[p, :, at * DH : (at + 1) * DH] = rows.astype(BF16)
        rows16[p, :, 2 * DH : 3 * DH] = (whole(work, p, one) - 1.0).astype(BF16)

    def by_tokens(hh, b, slot_index):
        rows = sorted_rows(work, hh, b, two)
        return nn(hits_by_token(slots[slot_index, hh], pool), rows)

    @pl.when(early)
    def _():
        for hh in range(each):

            @pl.loop(0, near)
            def _(b):
                got(QX, x_in.at[b, :, hh * DH : (hh + 1) * DH], hh * near + b)

            @pl.loop(0, near, unroll=4)
            def _(b):
                view = x_in[b, :, hh * DH : (hh + 1) * DH]
                sort_into(work, hh, b, one, nn(hits_of(slots[near + b, hh], pool), view))

            @pl.loop(0, pairs // group)
            def _(g):
                group_of = [hh * pairs + g * group + i for i in range(group)]
                queries = [whole(work, p, one).astype(BF16) for p in group_of]
                for p, q in zip(group_of, queries):
                    xq16[p] = q
                keys = [rows16[p, :, DH : 3 * DH] for p in group_of]
                values = [rows16[p, :, 3 * DH :] for p in group_of]
                attend(group_of, queries, keys, values, same, probs_x)

            @pl.loop(0, near, unroll=4)
            def _(b):
                back = by_tokens(hh, b, near + b)
                at = hh * near + b
                view = x_out.at[b, :, hh * DH : (hh + 1) * DH]
                view[...] = back[:, :DH].astype(BF16)
                lse_out[at] = back[:, DH:].T[:8]
                dst = x_in.at[b, :, hh * DH : (hh + 1) * DH]
                remote(OX, view, dst, at, at, me + near).start()
                remote(LX, lse_out.at[at], lse_in.at[at], at, at, me + near).start()

    @pl.when(early)
    def _():
        exchange(arrays[3:])

    @pl.loop(0, rows16.shape[0] // group)
    def _(g):
        group_of = [g * group + i for i in range(group)]
        queries = [rows16[p, :, :DH] for p in group_of]
        keys = [rows16[p, :, DH : 3 * DH] for p in group_of]
        values = [rows16[p, :, 3 * DH :] for p in group_of]
        attend(group_of, queries, keys, values, same & (col <= row), probs)

    @pl.loop(0, near, unroll=4)
    def _(b):
        for hh in range(each):
            back = by_tokens(hh, b, b)
            attn_own[b, :, hh * DH : (hh + 1) * DH] = back[:, :DH].astype(BF16)
            lse_own[hh * near + b] = back[:, DH:].T[:8]

    for load in loads:
        load.wait()

    pair[0] = jnp.zeros((8, n), F32)

    for j in range(4):

        @pl.when(me > 0)
        def _():
            for i in range(2):
                view = rim.at[i, :, span[j]]
                pltpu.make_async_copy(view, view, rim_recv.at[i, j]).wait()

        @pl.when(me == 0)
        def _():
            rim[:, :, span[j]] = jnp.zeros((2, n, quarter), BF16)

        @pl.loop(j * (heads // 4), (j + 1) * (heads // 4))
        def _(h):
            cols = columns(h, 1)
            keys = jnp.concatenate([rim[0, :, cols], wk_v[:, cols]], axis=0)
            vals = jnp.concatenate([rim[1, :, cols], wv_v[:, cols]], axis=0)
            prob = window_prob(factor, wq_v[:, cols], keys)
            attn = nn(prob.astype(BF16), vals).astype(BF16)
            attn_win[:, cols] = attn
            gained = wg_v[:, cols].astype(F32) * w_gain[:, cols]
            pair[0] += stat_rows(attn.astype(F32), gained)

    which = lax.broadcasted_iota(jnp.int32, (8, n), 0)

    def gained_of(b, hh):
        gain = c_gain[:, columns(t * each + hh, 1)]
        return taken[b, :, of_head(G, hh)].astype(F32) * gain

    def finish(b, merge):
        total = jnp.zeros((8, n), F32)
        for hh in range(each):
            at = hh * near + b
            lanes = slice(hh * DH, (hh + 1) * DH)
            if merge:
                mine = jnp.sum(lse_own[at][0:3], axis=0, keepdims=True)
                other = jnp.sum(lse_in[at][0:3], axis=0, keepdims=True)
                top = jnp.maximum(mine, other)
                mine, other = jnp.exp2(mine - top), jnp.exp2(other - top)
                share = jnp.where(which == 0, mine, other) / (mine + other)
                shares[at] = share
                by_token = share.T
                attn = by_token[:, 0:1] * attn_own[b, :, lanes].astype(F32)
                attn = attn + by_token[:, 1:2] * x_in[b, :, lanes].astype(F32)
                attn_own[b, :, lanes] = attn.astype(BF16)
            else:
                shares[at] = jnp.where(which == 0, 1.0, 0.0)
        for hh in range(each):
            attn = attn_own[b, :, hh * DH : (hh + 1) * DH].astype(F32)
            total = total + stat_rows(attn, gained_of(b, hh))
        part_out[b] = total
        deliver(PART, part_out.at[b], part_in.at[t], b, b, t)
        deliver(ATTN, attn_own.at[b], attn_home.at[:, columns(t * each, each)], b, b, t)

    for this_half, merge in ((early, False), (late, True)):

        @pl.when(this_half)
        def _():
            @pl.loop(0, near)
            def _(b):
                got(G, into(G, b), b)
                if merge:
                    for hh in range(each):
                        at = hh * near + b
                        got(OX, x_in.at[b, :, hh * DH : (hh + 1) * DH], at)
                        got(LX, lse_in.at[at], at)

            @pl.loop(0, near, unroll=2)
            def _(d):
                finish(peer(d + 1), merge)

    @pl.loop(0, near)
    def _(b):
        got(PART, part_in.at[b], b)
        pair[0] += part_in[b]

    swap = pltpu.make_async_remote_copy(
        src_ref=pair.at[0],
        dst_ref=pair.at[1],
        send_sem=pair_sem.at[0],
        recv_sem=pair_sem.at[1],
        device_id=(me, 1 - core),
        device_id_type=MESH,
    )
    swap.start()
    swap.wait()
    totals = pair[0] + pair[1]
    inv = 1.0 / jnp.sqrt(totals[0:1] / feat_width + EPSILON)
    coef = inv * inv * inv * totals[1:2] / feat_width
    stat_own[...] = jnp.where(which == 0, inv, coef)

    @pl.loop(0, near)
    def _(d):
        b = peer(d + 1)
        deliver(STAT, stat_own, stats.at[t], b, b, t)

    def spread(hh, b, is_late):
        lanes = slice(hh * DH, (hh + 1) * DH)
        at = hh * near + b
        by_token = stats[b].T
        attn = attn_own[b, :, lanes].astype(F32)
        dout = by_token[:, 0:1] * gained_of(b, hh) - by_token[:, 1:2] * attn
        dout = dout.astype(BF16).astype(F32)
        terms = dout * attn
        row_dot = jnp.sum(terms, axis=-1, keepdims=True)
        mine = dout
        if is_late:
            share = shares[at].T
            view = d_out.at[b, :, lanes]
            view[...] = (share[:, 1:2] * dout).astype(BF16)
            high = terms.astype(BF16)
            low = (terms - high.astype(F32)).astype(BF16)
            sums = nt(every, high) + nt(every, low)
            first, second = in_parts(sums * shares[at][1:2], 2)
            dot_out[at] = jnp.where(which == 0, first, jnp.where(which == 1, second, 0.0))
            remote(DX, view, d_in.at[b, :, lanes], at, at, me - near).start()
            remote(RX, dot_out.at[at], dot_in.at[at], at, at, me - near).start()
            mine, row_dot = share[:, 0:1] * dout, share[:, 0:1] * row_dot
        dots = at_lanes((n, DH), in_parts(row_dot, 2)).astype(BF16)
        both = jnp.concatenate([mine.astype(BF16), dots], axis=1)
        sort_into(work, hh, b, two, nn(hits_of(slots[b, hh], pool), both))

    every = jnp.ones((8, DH), BF16)

    def spread_all(is_late):
        @pl.loop(0, near)
        def _(b):
            got(STAT, stats.at[b], b)

        for hh in range(each):

            @pl.loop(0, near, unroll=4)
            def _(d):
                spread(hh, peer(d + 1), is_late)

    @pl.when(late)
    def _():
        spread_all(True)

    @pl.loop(0, near)
    def _(b):
        got(ATTN, attn_home.at[:, columns(b * each, each)], b)

    for j in range(plane - 1):

        @pl.when(relays & (spot == j))
        def _():
            for i in range(2):
                pass_on(i, j).wait_send()

    @pl.when(crosses)
    def _():
        for j in range(4):
            for i in range(2):
                rim_first(i, j, j < plane - 1).wait_send()

    @pl.when(straight)
    def _():
        for j in range(4):
            for i in range(2):
                rim_first(i, j, False).wait_send()

    back_crosses = (spot == 0) & (me > 0)
    back_straight = spot != 0
    back_relays = (spot != 0) & (me >= plane)

    def back_copy(j, src, dst, sem, to):
        return pltpu.make_async_remote_copy(
            src_ref=src,
            dst_ref=dst,
            send_sem=rim_send.at[2, j],
            recv_sem=sem,
            device_id=(to, core),
            device_id_type=MESH,
        )

    def back_first(j, by_relay):
        src = rim.at[:, :, span[j]]
        if by_relay:
            return back_copy(j, src, relay_back, relay_sem.at[2], level * plane + j)
        return back_copy(j, src, rim_back.at[:, :, span[j]], rim_recv.at[2, j], me - 1)

    by_token = stat_own[...].T
    inv_col, coef_col = by_token[:, 0:1], by_token[:, 1:2]
    for j in (1, 2, 3, 0):

        @pl.loop(j * (heads // 4), (j + 1) * (heads // 4))
        def _(h):
            cols = columns(h, 1)
            q = wq_v[:, cols]
            keys = jnp.concatenate([rim[0, :, cols], wk_v[:, cols]], axis=0)
            vals = jnp.concatenate([rim[1, :, cols], wv_v[:, cols]], axis=0)
            attn = attn_win[:, cols].astype(F32)
            gained = wg_v[:, cols].astype(F32) * w_gain[:, cols]
            grad = (inv_col * gained - coef_col * attn).astype(BF16)
            prob = window_prob(factor, q, keys)
            row_dot = jnp.sum(grad.astype(F32) * attn, axis=-1, keepdims=True)
            change = (prob * (nt(grad, vals) - row_dot)).astype(BF16)
            wq_v[:, cols] = (nn(change, keys) * factor).astype(BF16)
            dk = tn(change, q)
            dv = tn(prob.astype(BF16), grad)
            rim[0, :, cols] = dk[:WINDOW].astype(BF16)
            rim[1, :, cols] = dv[:WINDOW].astype(BF16)
            wk_v[:, cols] = dk[WINDOW:].astype(BF16)
            wv_v[:, cols] = dv[WINDOW:].astype(BF16)
            attn_win[:, cols] = (attn * inv_col * w_gain[:, cols]).astype(BF16)
            clu = attn_home[:, cols].astype(F32)
            attn_home[:, cols] = (clu * inv_col * c_gain[:, cols]).astype(BF16)

        @pl.when(back_crosses)
        def _():
            back_first(j, 0 < j < plane).start()

        @pl.when(back_straight)
        def _():
            back_first(j, False).start()

    stores = [
        pltpu.make_async_copy(src, dst, local_sem.at[4 + i])
        for i, (src, dst) in enumerate(
            [
                (attn_win, win_normed),
                (attn_home, clu_normed),
                (wq_v, win_dq),
                (wk_v, win_dk),
                (wv_v, win_dv),
            ]
        )
    ]
    for store in stores[:3]:
        store.start()

    @pl.when(early)
    def _():
        spread_all(False)

    minus = jnp.where(lane < 2, -1.0, 0.0).astype(BF16)

    def changes_of(group_of, prob_ref):
        slopes = []
        for p in group_of:
            v = jnp.concatenate([rows16[p, :, 3 * DH :], minus], axis=1)
            slopes.append(nt(whole(work, p, two).astype(BF16), v))
        return [(prob_ref[p].astype(F32) * s).astype(BF16) for p, s in zip(group_of, slopes)]

    def split_rows(x):
        return x.reshape(2, part, DH)

    second, third = slice(DH, 2 * DH), slice(2 * DH, 3 * DH)

    @pl.loop(0, rows16.shape[0] // group)
    def _(g):
        group_of = [g * group + i for i in range(group)]
        for p, change in zip(group_of, changes_of(group_of, probs)):
            grad = whole(work, p, one).astype(BF16)
            acc[p, :, :, one] = split_rows(nn(change, rows16[p, :, DH : 2 * DH]) * factor)
            acc[p, :, :, second] = split_rows(tn(change, rows16[p, :, :DH]))
            acc[p, :, :, third] = split_rows(tn(probs[p], grad))

    @pl.when(late)
    def _():
        @pl.loop(0, near)
        def _(b):
            for hh in range(each):
                sent(QX, taken.at[b, :, of_head(Q, hh)], hh * near + b)

    homes = [(DQ, clu_dq), (DK, clu_dk), (DV, clu_dv)]

    def home_of(i, hh, owner):
        return homes[i][1].at[:, columns(owner * each + hh, 1)]

    def give(i, hh, b):
        at = hh * near + b
        view = taken.at[b, :, of_head(i, hh)]
        deliver(homes[i][0], view, home_of(i, hh, t), b, at, hh * near + t)

    def keys_home(hh, b, hits):
        rows = sorted_rows(acc, hh, b, slice(DH, 3 * DH))
        back = nn(hits, rows)
        taken[b, :, of_head(1, hh)] = (back[:, :DH] * factor).astype(BF16)
        taken[b, :, of_head(2, hh)] = back[:, DH:].astype(BF16)
        give(1, hh, b)
        give(2, hh, b)

    for hh in range(each):

        def own_home(b, is_late):
            hits = hits_by_token(slots[b, hh], pool)
            taken[b, :, of_head(0, hh)] = nn(hits, sorted_rows(acc, hh, b, one)).astype(BF16)
            if is_late:
                keys_home(hh, b, hits)
            else:
                give(0, hh, b)

        for this_half, is_late in ((early, False), (late, True)):

            @pl.when(this_half)
            def _():
                @pl.loop(0, near, unroll=2)
                def _(d):
                    own_home(peer(d + 1), is_late)

    def pass_back(j):
        dst = rim_back.at[:, :, span[j]]
        return pltpu.make_async_remote_copy(
            src_ref=relay_back,
            dst_ref=dst,
            send_sem=relay_sem.at[3],
            recv_sem=rim_recv.at[2, j],
            device_id=(level * plane - 1, core),
            device_id_type=MESH,
        )

    for j in range(1, plane):

        @pl.when(back_relays & (spot == j))
        def _():
            pltpu.make_async_copy(relay_back, relay_back, relay_sem.at[2]).wait()
            pass_back(j).start()

    @pl.when(early)
    def _():
        for hh in range(each):
            lanes = slice(hh * DH, (hh + 1) * DH)

            @pl.loop(0, near)
            def _(b):
                at = hh * near + b
                got(DX, d_in.at[b, :, lanes], at)
                got(RX, dot_in.at[at], at)
                sent(OX, x_out.at[b, :, lanes], at)

            @pl.loop(0, near, unroll=4)
            def _(b):
                at = hh * near + b
                dots = jnp.concatenate(
                    [dot_in[at].T, jnp.zeros((n, DH - 8), F32)], axis=1
                ).astype(BF16)
                both = jnp.concatenate([d_in[b, :, lanes], dots], axis=1)
                sort_into(work, hh, b, two, nn(hits_of(slots[near + b, hh], pool), both))

            @pl.loop(0, pairs // group)
            def _(g):
                group_of = [hh * pairs + g * group + i for i in range(group)]
                for p, change in zip(group_of, changes_of(group_of, probs_x)):
                    grad = whole(work, p, one).astype(BF16)
                    acc[p, :, :, second] += split_rows(tn(change, xq16[p]))
                    acc[p, :, :, third] += split_rows(tn(probs_x[p], grad))
                    dq = nn(change, rows16[p, :, DH : 2 * DH]) * factor
                    work[p, :, :, one] = split_rows(dq)

            @pl.loop(0, near, unroll=2)
            def _(d):
                b = peer(d + 1)
                at = hh * near + b
                hits = hits_by_token(slots[near + b, hh], pool)
                view = x_out.at[b, :, lanes]
                view[...] = nn(hits, sorted_rows(work, hh, b, one)).astype(BF16)
                remote(DQX, view, d_in.at[b, :, lanes], at, at, me + near).start()

            @pl.loop(0, near, unroll=2)
            def _(d):
                b = peer(d + 1)
                keys_home(hh, b, hits_by_token(slots[b, hh], pool))

    @pl.when(late)
    def _():
        for hh in range(each):
            lanes = slice(hh * DH, (hh + 1) * DH)

            @pl.loop(0, near)
            def _(d):
                b = peer(d + 1)
                got(DQX, d_in.at[b, :, lanes], hh * near + b)
                more = d_in[b, :, lanes].astype(F32)
                view = taken.at[b, :, of_head(0, hh)]
                view[...] = (view[...].astype(F32) + more).astype(BF16)
                give(0, hh, b)

    @pl.when(me < n_seq - 1)
    def _():
        for j in range(4):
            view = rim_back.at[:, :, span[j]]
            pltpu.make_async_copy(view, view, rim_recv.at[2, j]).wait()

    @pl.when(me == n_seq - 1)
    def _():
        rim_back[...] = jnp.zeros_like(rim_back)

    @pl.loop(0, heads)
    def _(h):
        cols = columns(h, 1)
        dk = wk_v[:, cols].astype(F32) + rim_back[0, :, cols].astype(F32)
        wk_v[:, cols] = (dk * factor).astype(BF16)
        dv = wv_v[:, cols].astype(F32) + rim_back[1, :, cols].astype(F32)
        wv_v[:, cols] = dv.astype(BF16)

    for store in stores[3:]:
        store.start()

    for j in range(4):

        @pl.when(back_crosses)
        def _():
            back_first(j, 0 < j < plane).wait_send()

        @pl.when(back_straight)
        def _():
            back_first(j, False).wait_send()

    for j in range(1, plane):

        @pl.when(back_relays & (spot == j))
        def _():
            pass_back(j).wait_send()

    @pl.loop(1, near)
    def _(d):
        to = peer(d)
        for kind, src in arrays:
            sent(kind, src.at[:, columns(to * each, each)], to)
        sent(IDS, ids.at[pl.ds(to * each, each)], to)
        sent(PART, part_out.at[to], to)
        sent(ATTN, attn_own.at[to], to)
        sent(STAT, stat_own, to)
        for hh in range(each):
            for i, (kind, home) in enumerate(homes):
                sent(kind, taken.at[to, :, of_head(i, hh)], hh * near + to)

    @pl.loop(0, near)
    def _(b):
        for hh in range(each):
            for i, (kind, home) in enumerate(homes):
                got(kind, home_of(i, hh, b), hh * near + b)

    @pl.when(late)
    def _():
        @pl.loop(0, near)
        def _(b):
            sent(IDSX, ids.at[pl.ds(b * each, each)], b)
            for hh in range(each):
                at = hh * near + b
                sent(DX, d_out.at[b, :, hh * DH : (hh + 1) * DH], at)
                sent(RX, dot_out.at[at], at)

    @pl.when(early)
    def _():
        @pl.loop(0, near)
        def _(b):
            for hh in range(each):
                at = hh * near + b
                sent(LX, lse_out.at[at], at)
                sent(DQX, x_out.at[b, :, hh * DH : (hh + 1) * DH], at)

    for store in stores:
        store.wait()


def copy_kernel(*refs):
    count = len(refs) // 2
    for src, dst in zip(refs[:count], refs[count:]):
        dst[...] = src[...]


def settle(arrays):
    n, wide = arrays[0].shape
    block = pl.BlockSpec((n // 8, wide), lambda i: (i, 0))
    return pl.pallas_call(
        copy_kernel,
        grid=(8,),
        in_specs=[block] * len(arrays),
        out_specs=[block] * len(arrays),
        out_shape=[jax.ShapeDtypeStruct((n, wide), BF16)] * len(arrays),
        compiler_params=pltpu.CompilerParams(vmem_limit_bytes=32 << 20),
    )(*arrays)


def layer(*arrays):
    win_query, cluster_ids = arrays[0], arrays[6]
    n, wide = win_query.shape
    sources = lax.axis_size("seq")
    near = sources // 2
    cap = SLOTS // sources
    clusters = sources * (2 * n // SLOTS)
    part = near * cap
    heads = wide // DH
    each = heads // near
    pairs = each * clusters // 2
    given = list(arrays)
    given[6] = cluster_ids[:, None, :]
    given[7], given[8] = arrays[7][None, :], arrays[8][None, :]
    anywhere = pl.BlockSpec(memory_space=pl.ANY)
    vmem = pl.BlockSpec(memory_space=pltpu.VMEM)
    group = next(g for g in (16, 8, 4, 2, 1) if clusters // 2 % g == 0)
    rows_of = pltpu.VMEM((each * near, 8, n), F32)
    results = pl.pallas_call(
        functools.partial(layer_kernel, DH ** (-0.5), cap, group, 4),
        in_specs=[anywhere] * 6 + [vmem] * 3 + [anywhere] * 2,
        out_specs=[anywhere] * 8,
        out_shape=[jax.ShapeDtypeStruct((n, wide), BF16)] * 8,
        scratch_shapes=[
            pltpu.VMEM((near, n, 4 * each * DH), BF16),
            pltpu.VMEM((sources, each, 1, n), jnp.int32),
            pltpu.VMEM((sources, each, 1, n), jnp.int32),
        ]
        + [pltpu.VMEM((n, wide), BF16)] * 4
        + [pltpu.VMEM((2, n, wide), BF16)] * 2
        + [pltpu.VMEM((2, n, wide // 4), BF16)] * 2
        + [pltpu.VMEM((n, wide), BF16)] * 2
        + [pltpu.VMEM((near, n, each * DH), BF16)] * 5
        + [
            pltpu.VMEM((pairs, 2 * part, 4 * DH), BF16),
            pltpu.VMEM((pairs, 2 * part, DH), BF16),
            pltpu.VMEM((pairs, 2, part, 2 * DH), F32),
            pltpu.VMEM((pairs, 2, part, 3 * DH), F32),
            pltpu.VMEM((pairs, 2 * part, 2 * part), BF16),
            pltpu.VMEM((pairs, 2 * part, 2 * part), BF16),
        ]
        + [rows_of] * 6
        + [
            pltpu.VMEM((near, 8, n), F32),
            pltpu.VMEM((near, 8, n), F32),
            pltpu.VMEM((2, 8, n), F32),
            pltpu.VMEM((8, n), F32),
            pltpu.VMEM((near, 8, n), F32),
            pltpu.SemaphoreType.DMA((18, sources)),
            pltpu.SemaphoreType.DMA((18, sources)),
            pltpu.SemaphoreType.DMA((3, 4)),
            pltpu.SemaphoreType.DMA((3, 4)),
            pltpu.SemaphoreType.DMA((6,)),
            pltpu.SemaphoreType.DMA((2,)),
            pltpu.SemaphoreType.DMA((9,)),
        ],
        cost_estimate=pl.CostEstimate(
            flops=14 * n * 2 * n * wide, bytes_accessed=16 * n * wide * 2, transcendentals=0
        ),
        compiler_params=pltpu.CompilerParams(
            vmem_limit_bytes=60 << 20, collective_id=0, has_side_effects=True
        ),
    )(*given)
    return settle(results)


def solution(mesh):
    sources, split = mesh.shape["seq"], mesh.shape["head"]
    whole_heads = HC // split == sources and SLOTS // sources % 8 == 0 and split == 2 and sources % 4 == 0
    return jax.shard_map(
        layer if whole_heads else body,
        mesh=mesh,
        in_specs=(P("seq", "head"),) * 6
        + (P("head", "seq"), P("head"), P("head"))
        + (P("seq", "head"),) * 2,
        out_specs=(P("seq", "head"),) * 8,
        check_vma=False,
    )
```

```python
import functools

import jax
import jax.numpy as jnp
from jax import lax
from jax.experimental import pallas as pl
from jax.experimental.pallas import tpu as pltpu
from jax.sharding import PartitionSpec as P

HW = 32
HC = 32
DH = 128
WINDOW = 256
SLOTS = 128
CHUNKS = 2

EPSILON = 1e-06
F32 = jnp.float32
BF16 = jnp.bfloat16


def from_behind(block, axis, distance):
    devices = range(lax.axis_size(axis))
    route = [(i - distance, i) for i in devices if i - distance in devices]
    return lax.ppermute(block, axis, route)


def nt(a, b):
    return lax.dot_general(a, b, (((1,), (1,)), ((), ())), preferred_element_type=F32)


def tn(a, b):
    return lax.dot_general(a, b, (((0,), (0,)), ((), ())), preferred_element_type=F32)


def nn(a, b):
    return jnp.dot(a, b, preferred_element_type=F32)


def one_hot(slot_ref, pool):
    n = slot_ref.shape[-1]
    hit = lax.broadcasted_iota(jnp.int32, (pool, n), 0) == slot_ref[0]
    return jnp.where(hit, 1.0, 0.0).astype(BF16)


def normalized(scores, allowed):
    masked = jnp.where(allowed, scores, -jnp.inf)
    grown = jnp.exp(masked - jnp.max(masked, axis=-1, keepdims=True))
    return grown * (1.0 / jnp.sum(grown, axis=-1, keepdims=True))


def call(kernel, grid, in_specs, out_specs, out_shape, flops, size, **more):
    return pl.pallas_call(
        kernel,
        grid=grid,
        in_specs=in_specs,
        out_specs=out_specs,
        out_shape=out_shape,
        cost_estimate=pl.CostEstimate(flops=flops, bytes_accessed=size, transcendentals=0),
        compiler_params=pltpu.CompilerParams(vmem_limit_bytes=48 << 20),
        **more,
    )


def dispatch_kernel(*refs):
    slot_ref, value_refs, out_ref = refs[0], refs[1:-1], refs[-1]
    picked = one_hot(slot_ref, out_ref.shape[0])
    for i, ref in enumerate(value_refs):
        out_ref[:, i * DH : (i + 1) * DH] = nn(picked, ref[...]).astype(BF16)


def dispatch(slot_at, values, first, count, pool):
    n = slot_at.shape[-1]
    wide = len(values) * DH
    return call(
        dispatch_kernel,
        (count,),
        [pl.BlockSpec((1, 1, n), lambda h: (h + first, 0, 0))]
        + [pl.BlockSpec((n, DH), lambda h: (0, h + first)) for _ in values],
        pl.BlockSpec((pool, wide), lambda h: (0, h)),
        jax.ShapeDtypeStruct((pool, count * wide), BF16),
        2 * count * pool * n * wide,
        2 * count * (pool + n) * wide,
    )(slot_at, *values)


def collect_kernel(n_out, *refs):
    slot_ref, rows_ref, out_refs = refs[0], refs[1], refs[-n_out:]
    picked = one_hot(slot_ref, rows_ref.shape[0])
    merged = tn(picked, rows_ref[...]).astype(BF16)
    for i, ref in enumerate(out_refs):
        ref[...] = merged[:, i * DH : (i + 1) * DH]


def collect(slot_at, rows, first, count, n_out, earlier):
    n = slot_at.shape[-1]
    pool = rows.shape[0]
    heads = slot_at.shape[0]
    wide = n_out * DH
    return call(
        functools.partial(collect_kernel, n_out),
        (count,),
        [
            pl.BlockSpec((1, 1, n), lambda h: (h + first, 0, 0)),
            pl.BlockSpec((pool, wide), lambda h: (0, h)),
        ]
        + [pl.BlockSpec(memory_space=pl.ANY) for _ in earlier],
        [pl.BlockSpec((n, DH), lambda h: (0, h + first))] * n_out,
        [jax.ShapeDtypeStruct((n, heads * DH), BF16)] * n_out,
        2 * count * pool * n * wide,
        2 * count * (pool + n) * wide,
        input_output_aliases={2 + i: i for i in range(len(earlier))},
    )(slot_at, rows, *earlier)


class Rows:
    def __init__(self, sources, owned, cap):
        self.sources, self.owned, self.cap = sources, owned, cap
        self.aligned = cap % 8 == 0

    def selector(self, c):
        members = self.sources * self.cap
        layout = (members, members * self.owned)
        member = lax.broadcasted_iota(jnp.int32, layout, 0)
        row = lax.broadcasted_iota(jnp.int32, layout, 1)
        want = member // self.cap * (self.cap * self.owned) + c * self.cap + member % self.cap
        return jnp.where(row == want, 1.0, 0.0).astype(BF16)

    def split(self, rows):
        members = self.sources * self.cap
        if not self.aligned:
            return [nn(self.selector(c), rows).astype(BF16) for c in range(self.owned)]
        wide = rows.shape[1]
        four = rows.astype(F32).reshape(self.sources, self.owned, self.cap, wide)
        return [four[:, c].reshape(members, wide).astype(BF16) for c in range(self.owned)]

    def join(self, parts):
        wide = parts[0].shape[1]
        pool = self.sources * self.cap * self.owned
        if not self.aligned:
            total = jnp.zeros((pool, wide), F32)
            for c, part in enumerate(parts):
                total = total + tn(self.selector(c), part.astype(BF16))
            return total.astype(BF16)
        shaped = [p.reshape(self.sources, 1, self.cap, wide) for p in parts]
        return jnp.concatenate(shaped, axis=1).reshape(pool, wide).astype(BF16)


def cluster_allowed(live_ref, c, members):
    row = lax.broadcasted_iota(jnp.int32, (members, members), 0)
    col = lax.broadcasted_iota(jnp.int32, (members, members), 1)
    live = jnp.broadcast_to(live_ref[0, c : c + 1, :], (members, members)) > 0.5
    return (live & (col <= row)) | (col == row)


def owner_fwd_kernel(rows, factor, live_ref, qkv_ref, out_ref):
    members = rows.sources * rows.cap
    parts = []
    for c, qkv in enumerate(rows.split(qkv_ref[...])):
        q, k, v = qkv[:, :DH], qkv[:, DH : 2 * DH], qkv[:, 2 * DH :]
        prob = normalized(nt(q, k) * factor, cluster_allowed(live_ref, c, members))
        parts.append(nn(prob.astype(BF16), v))
    out_ref[...] = rows.join(parts)


def owner_bwd_kernel(rows, factor, live_ref, qkv_ref, attn_ref, grad_ref, out_ref):
    members = rows.sources * rows.cap
    attn_parts = rows.split(attn_ref[...])
    grad_parts = rows.split(grad_ref[...])
    parts = []
    for c, qkv in enumerate(rows.split(qkv_ref[...])):
        q, k, v = qkv[:, :DH], qkv[:, DH : 2 * DH], qkv[:, 2 * DH :]
        grad = grad_parts[c]
        row_dot = jnp.sum(grad.astype(F32) * attn_parts[c].astype(F32), axis=-1, keepdims=True)
        prob = normalized(nt(q, k) * factor, cluster_allowed(live_ref, c, members))
        change = (prob * (nt(grad, v) - row_dot)).astype(BF16)
        dq = nn(change, k) * factor
        dk = tn(change, q) * factor
        dv = tn(prob.astype(BF16), grad)
        parts.append(jnp.concatenate([dq, dk, dv], axis=1))
    out_ref[...] = rows.join(parts)


def owner_call(kernel, rows, factor, live, first, arrays, n_out):
    pool = arrays[0].shape[0]
    count = arrays[0].shape[1] // (3 * DH)
    members = rows.sources * rows.cap
    wides = [a.shape[1] // count for a in arrays]
    return call(
        functools.partial(kernel, rows, factor),
        (count,),
        [pl.BlockSpec((1, rows.owned, members), lambda h: (h + first, 0, 0))]
        + [pl.BlockSpec((pool, w), lambda h: (0, h)) for w in wides],
        pl.BlockSpec((pool, n_out * DH), lambda h: (0, h)),
        jax.ShapeDtypeStruct((pool, count * n_out * DH), BF16),
        12 * count * pool * members * DH,
        2 * count * pool * (sum(wides) + n_out * DH),
    )(live, *arrays)


def window_prob(factor, q, keys):
    n = q.shape[0]
    row = lax.broadcasted_iota(jnp.int32, (n, n + WINDOW), 0)
    col = lax.broadcasted_iota(jnp.int32, (n, n + WINDOW), 1)
    gap = row + WINDOW - col
    lowest = jnp.where(lax.axis_index("seq") > 0, 0, WINDOW)
    allowed = (gap >= 0) & (gap < WINDOW) & (col >= lowest)
    return normalized(nt(q, keys) * factor, allowed)


def window_fwd_kernel(factor, q_ref, kp_ref, k_ref, vp_ref, v_ref, out_ref):
    keys = jnp.concatenate([kp_ref[0], k_ref[...]], axis=0)
    vals = jnp.concatenate([vp_ref[0], v_ref[...]], axis=0)
    prob = window_prob(factor, q_ref[...], keys)
    out_ref[...] = nn(prob.astype(BF16), vals).astype(BF16)


def window_bwd_kernel(
    factor, q_ref, kp_ref, k_ref, vp_ref, v_ref, attn_ref, grad_ref, dq_ref, dk_ref, dv_ref, rim_ref
):
    q, grad = q_ref[...], grad_ref[...]
    keys = jnp.concatenate([kp_ref[0], k_ref[...]], axis=0)
    vals = jnp.concatenate([vp_ref[0], v_ref[...]], axis=0)
    prob = window_prob(factor, q, keys)
    row_dot = jnp.sum(grad.astype(F32) * attn_ref[...].astype(F32), axis=-1, keepdims=True)
    change = (prob * (nt(grad, vals) - row_dot)).astype(BF16)
    dq_ref[...] = (nn(change, keys) * factor).astype(BF16)
    dk = tn(change, q)
    dv = tn(prob.astype(BF16), grad)
    rim_ref[0] = dk[:WINDOW].astype(BF16)
    rim_ref[1] = dv[:WINDOW].astype(BF16)
    dk_ref[...] = dk[WINDOW:]
    dv_ref[...] = dv[WINDOW:]


def window_specs(n):
    here = pl.BlockSpec((n, DH), lambda h: (0, h))
    key = pl.BlockSpec((1, n, DH), lambda h: (0, 0, h))
    val = pl.BlockSpec((1, n, DH), lambda h: (1, 0, h))
    return here, key, val


def window_fwd(factor, query, key, value, before):
    n, wide = query.shape
    here, rim_key, rim_val = window_specs(n)
    return call(
        functools.partial(window_fwd_kernel, factor),
        (wide // DH,),
        [here, rim_key, here, rim_val, here],
        here,
        jax.ShapeDtypeStruct((n, wide), BF16),
        4 * n * 2 * n * wide,
        12 * n * wide,
    )(query, before, key, before, value)


def window_bwd(factor, query, key, value, before, attn, grad):
    n, wide = query.shape
    here, rim_key, rim_val = window_specs(n)
    return call(
        functools.partial(window_bwd_kernel, factor),
        (wide // DH,),
        [here, rim_key, here, rim_val, here, here, here],
        [here, here, here, pl.BlockSpec((2, n, DH), lambda h: (0, 0, h))],
        [
            jax.ShapeDtypeStruct((n, wide), BF16),
            jax.ShapeDtypeStruct((n, wide), F32),
            jax.ShapeDtypeStruct((n, wide), F32),
            jax.ShapeDtypeStruct((2, n, wide), BF16),
        ],
        10 * n * 2 * n * wide,
        28 * n * wide,
    )(query, before, key, before, value, attn, grad)


def body(
    win_query,
    win_key,
    win_value,
    clu_query,
    clu_key,
    clu_value,
    cluster_ids,
    win_gain,
    clu_gain,
    win_out_grad,
    clu_out_grad,
):
    n_rows = win_query.shape[0]
    factor = DH ** (-0.5)
    feat_width = (HW + HC) * DH
    sources = lax.axis_size("seq")
    n_cap = SLOTS // sources
    owned_count = 2 * n_rows // SLOTS
    pool_size = 2 * n_rows
    clu_heads = clu_query.shape[1] // DH
    rows = Rows(sources, owned_count, n_cap)

    def exchange(values):
        shaped = values.reshape(sources, pool_size // sources, values.shape[1])
        moved = lax.all_to_all(shaped, "seq", split_axis=0, concat_axis=0, tiled=True)
        return moved.reshape(values.shape)

    row_ids = lax.broadcasted_iota(jnp.int32, (n_rows, n_rows), 0)
    col_ids = lax.broadcasted_iota(jnp.int32, (n_rows, n_rows), 1)
    same_cluster = (cluster_ids[:, :, None] == cluster_ids[:, None, :]) & (col_ids < row_ids)
    rank_in = jnp.sum(same_cluster.astype(jnp.int32), axis=-1)
    slot_at = (cluster_ids * n_cap + rank_in)[:, None, :]

    n_clusters = sources * owned_count
    every = lax.broadcasted_iota(jnp.int32, (n_clusters, clu_heads, n_rows), 0)
    counts = jnp.sum((cluster_ids[None] == every).astype(F32), axis=-1)
    counts = counts.reshape(sources, owned_count, clu_heads)
    counts = lax.all_to_all(counts, "seq", split_axis=0, concat_axis=0, tiled=True)
    slot_pos = lax.broadcasted_iota(F32, (clu_heads, owned_count, sources, n_cap), 3)
    live = (slot_pos < counts.transpose(2, 1, 0)[..., None]).astype(F32)
    live = live.reshape(clu_heads, owned_count, sources * n_cap)

    chunks = CHUNKS if clu_heads % CHUNKS == 0 else 1
    per = clu_heads // chunks
    starts = [i * per for i in range(chunks)]

    held = [
        exchange(dispatch(slot_at, [clu_query, clu_key, clu_value], first, per, pool_size))
        for first in starts
    ]
    before = from_behind(jnp.stack([win_key, win_value]), "seq", 1)
    attn_win = window_fwd(factor, win_query, win_key, win_value, before)

    attn_held = [
        owner_call(owner_fwd_kernel, rows, factor, live, first, [qkv], 1)
        for first, qkv in zip(starts, held)
    ]
    attn_back = [exchange(part) for part in attn_held]
    attn_clu = ()
    for first, part in zip(starts, attn_back):
        attn_clu = collect(slot_at, part, first, per, 1, attn_clu)
    attn_clu = attn_clu[0]

    flat_win = attn_win.astype(F32)
    flat_clu = attn_clu.astype(F32)
    grad_win = win_out_grad.astype(F32) * win_gain
    grad_clu = clu_out_grad.astype(F32) * clu_gain
    totals = jnp.stack(
        [
            jnp.sum(flat_win * flat_win, axis=1) + jnp.sum(flat_clu * flat_clu, axis=1),
            jnp.sum(grad_win * flat_win, axis=1) + jnp.sum(grad_clu * flat_clu, axis=1),
        ]
    )
    totals = lax.psum(totals, "head")
    sq_total, dot_total = totals[0], totals[1]
    inv_rms = 1.0 / jnp.sqrt(sq_total / feat_width + EPSILON)
    coef_rows = inv_rms**3 * dot_total / feat_width
    dout_clu = (inv_rms[:, None] * grad_clu - coef_rows[:, None] * flat_clu).astype(BF16)
    dout_win = (inv_rms[:, None] * grad_win - coef_rows[:, None] * flat_win).astype(BF16)
    win_normed = (flat_win * inv_rms[:, None] * win_gain).astype(BF16)
    clu_normed = (flat_clu * inv_rms[:, None] * clu_gain).astype(BF16)

    grad_held = [
        exchange(dispatch(slot_at, [dout_clu], first, per, pool_size)) for first in starts
    ]
    win_dq, key_own, val_own, rim = window_bwd(
        factor, win_query, win_key, win_value, before, attn_win, dout_win
    )
    after_rim = from_behind(rim, "seq", -1)

    clu_grads = ()
    sent = [
        owner_call(owner_bwd_kernel, rows, factor, live, first, [qkv, part, grad], 3)
        for first, qkv, part, grad in zip(starts, held, attn_held, grad_held)
    ]
    home = [exchange(part) for part in sent]
    win_dk = ((key_own + after_rim[0]) * factor).astype(BF16)
    win_dv = (val_own + after_rim[1]).astype(BF16)
    for first, part in zip(starts, home):
        clu_grads = collect(slot_at, part, first, per, 3, clu_grads)
    return (win_normed, clu_normed, win_dq, win_dk, win_dv, *clu_grads)


BIG = 1e30
MESH = pl.DeviceIdType.MESH
LOG2E = 1.4426950408889634


def hits_of(slot, pool):
    n = slot.shape[-1]
    hit = lax.broadcasted_iota(jnp.int32, (pool, n), 0) == slot
    return jnp.where(hit, 1.0, 0.0).astype(BF16)


def hits_by_token(slot, pool):
    n = slot.shape[-1]
    column = jnp.broadcast_to(slot.astype(F32), (8, n)).T[:, :1].astype(jnp.int32)
    hit = lax.broadcasted_iota(jnp.int32, (n, pool), 1) == column
    return jnp.where(hit, 1.0, 0.0).astype(BF16)


def stat_rows(attn, gained):
    wide = attn.shape[1]
    both = jnp.concatenate([attn * attn, gained * attn], axis=1)
    row = lax.broadcasted_iota(jnp.int32, (8, 2 * wide), 0)
    col = lax.broadcasted_iota(jnp.int32, (8, 2 * wide), 1)
    pick = jnp.where(col // wide == row, 1.0, 0.0).astype(BF16)
    high = both.astype(BF16)
    low = (both - high.astype(F32)).astype(BF16)
    return nt(pick, high) + nt(pick, low)


def head_cols(h):
    return pl.ds(pl.multiple_of(h * DH, DH), DH)


def columns(first, count):
    return pl.ds(pl.multiple_of(first * DH, DH), count * DH)


def at_lanes(shape, values):
    lane = lax.broadcasted_iota(jnp.int32, shape, 1)
    total = jnp.zeros(shape, F32)
    for i, value in enumerate(values):
        total = jnp.where(lane == i, value, total)
    return total


def in_parts(x, count):
    parts = []
    for _ in range(count - 1):
        parts.append(x.astype(BF16).astype(F32))
        x = x - parts[-1]
    return parts + [x]


def layer_kernel(
    factor,
    cap,
    group,
    plane,
    wq,
    wk,
    wv,
    cq,
    ck,
    cv,
    ids,
    w_gain,
    c_gain,
    wg,
    cg,
    win_normed,
    clu_normed,
    win_dq,
    win_dk,
    win_dv,
    clu_dq,
    clu_dk,
    clu_dv,
    taken,
    ids_in,
    slots,
    wq_v,
    wk_v,
    wv_v,
    wg_v,
    rim,
    rim_back,
    relay,
    relay_back,
    attn_win,
    attn_home,
    attn_own,
    x_in,
    d_in,
    x_out,
    d_out,
    rows16,
    xq16,
    work,
    acc,
    probs,
    probs_x,
    lse_own,
    lse_out,
    lse_in,
    dot_out,
    dot_in,
    shares,
    part_out,
    part_in,
    pair,
    stat_own,
    stats,
    send_sem,
    recv_sem,
    rim_send,
    rim_recv,
    relay_sem,
    pair_sem,
    local_sem,
):
    me, core = lax.axis_index("seq"), lax.axis_index("head")
    n_seq = lax.axis_size("seq")
    near = n_seq // 2
    half, t = me // near, lax.rem(me, near)
    base = half * near
    early, late = half == 0, half == 1
    n = wq.shape[0]
    heads = wq.shape[1] // DH
    each = heads // near
    pairs = rows16.shape[0] // each
    members = rows16.shape[1]
    part = members // 2
    clusters = 2 * pairs
    pool = clusters * cap
    feat_width = (HW + HC) * DH
    (Q, K, V, G, IDS, IDSX, QX, OX, LX, PART, ATTN, STAT, DX, RX, DQX, DQ, DK, DV) = range(18)

    def peer(d):
        d = lax.rem(d, near)
        return jnp.bitwise_xor(t, d) if near & (near - 1) == 0 else lax.rem(t + d, near)

    def remote(kind, src, dst, mine, theirs, to):
        return pltpu.make_async_remote_copy(
            src_ref=src,
            dst_ref=dst,
            send_sem=send_sem.at[kind, mine],
            recv_sem=recv_sem.at[kind, theirs],
            device_id=(to, core),
            device_id_type=MESH,
        )

    def got(kind, dst, index):
        pltpu.make_async_copy(dst, dst, recv_sem.at[kind, index]).wait()

    def sent(kind, src, index):
        pltpu.make_async_copy(src, src, send_sem.at[kind, index]).wait()

    def deliver(kind, src, dst, b, mine, theirs):
        @pl.when(b != t)
        def _():
            remote(kind, src, dst, mine, theirs, base + b).start()

        @pl.when(b == t)
        def _():
            pltpu.make_async_copy(src, dst, recv_sem.at[kind, theirs]).start()

    loads = [
        pltpu.make_async_copy(src, dst, local_sem.at[i])
        for i, (src, dst) in enumerate([(wq, wq_v), (wk, wk_v), (wv, wv_v), (wg, wg_v)])
    ]

    barrier = pltpu.get_barrier_semaphore()

    @pl.loop(1, n_seq)
    def _(d):
        to = lax.rem(me + d, n_seq)
        pl.semaphore_signal(barrier, inc=1, device_id=(to, core), device_id_type=MESH)

    pl.semaphore_signal(barrier, inc=1, device_id=(me, 1 - core), device_id_type=MESH)
    pl.semaphore_wait(barrier, n_seq)

    @pl.loop(0, near)
    def _(d):
        to = peer(d)
        view = ids.at[pl.ds(to * each, each)]
        deliver(IDS, view, ids_in.at[t], to, to, t)

        @pl.when(late)
        def _():
            remote(IDSX, view, ids_in.at[near + t], to, t, to).start()

    spot, level = lax.rem(me, plane), me // plane
    quarter = heads // 4 * DH
    span = [slice(j * quarter, (j + 1) * quarter) for j in range(4)]
    crosses = (spot == plane - 1) & (me < n_seq - 1)
    straight = (spot != plane - 1) & (me < n_seq - 1)
    relays = (spot != plane - 1) & (me < n_seq - plane)

    def rim_copy(i, j, src, dst, sem, to):
        return pltpu.make_async_remote_copy(
            src_ref=src,
            dst_ref=dst,
            send_sem=rim_send.at[i, j],
            recv_sem=sem,
            device_id=(to, core),
            device_id_type=MESH,
        )

    def rim_first(i, j, by_relay):
        src = (wk, wv)[i].at[:, span[j]]
        if by_relay:
            return rim_copy(i, j, src, relay.at[i], relay_sem.at[i], level * plane + j)
        return rim_copy(i, j, src, rim.at[i, :, span[j]], rim_recv.at[i, j], me + 1)

    arrays = [(Q, cq), (K, ck), (V, cv), (G, cg)]

    def into(kind, source):
        return taken.at[source, :, kind * each * DH : (kind + 1) * each * DH]

    def of_head(kind, hh):
        return slice((kind * each + hh) * DH, (kind * each + hh + 1) * DH)

    def exchange(some):
        @pl.loop(1, near)
        def _(d):
            to = peer(d)
            for kind, src in some:
                view = src.at[:, columns(to * each, each)]
                remote(kind, view, into(kind, t), to, t, base + to).start()

    @pl.when(late)
    def _():
        exchange(arrays[:1])

    @pl.when(crosses & (me == near - 1))
    def _():
        for j in range(4):
            for i in range(2):
                rim_first(i, j, j < plane - 1).start()

    @pl.when(early)
    def _():
        exchange(arrays[1:3])
        exchange(arrays[:1])

    for kind, src in arrays:
        view = src.at[:, columns(t * each, each)]
        pltpu.make_async_copy(view, into(kind, t), recv_sem.at[kind, t]).start()
    for load in loads:
        load.start()

    @pl.when(late)
    def _():
        for hh in range(each):

            @pl.loop(0, near)
            def _(b):
                if hh == 0:
                    got(Q, into(Q, b), b)
                view = taken.at[b, :, of_head(Q, hh)]
                dst = x_in.at[b, :, hh * DH : (hh + 1) * DH]
                remote(QX, view, dst, hh * near + b, hh * near + b, me - near).start()

    @pl.when(late)
    def _():
        @pl.when(crosses)
        def _():
            for j in range(4):
                for i in range(2):
                    rim_first(i, j, j < plane - 1).start()

        exchange(arrays[1:3])

        @pl.when(straight)
        def _():
            for j in range(4):
                for i in range(2):
                    rim_first(i, j, False).start()

    earlier = lax.broadcasted_iota(jnp.int32, (n, n), 0) < lax.broadcasted_iota(
        jnp.int32, (n, n), 1
    )
    earlier = jnp.where(earlier, 1.0, 0.0).astype(BF16)

    def place(b):
        for hh in range(each):
            of_block = ids_in[b, hh]
            member = hits_of(of_block, clusters)
            rank = jnp.sum(member.astype(F32) * nn(member, earlier), axis=0, keepdims=True)
            slots[b, hh] = of_block * cap + rank.astype(jnp.int32)

    @pl.loop(0, near)
    def _(b):
        got(IDS, ids_in.at[b], b)
        place(b)

    @pl.when(early)
    def _():
        @pl.loop(0, near)
        def _(b):
            got(IDSX, ids_in.at[near + b], b)
            place(near + b)

    def pass_on(i, j):
        return pltpu.make_async_remote_copy(
            src_ref=relay.at[i],
            dst_ref=rim.at[i, :, span[j]],
            send_sem=relay_sem.at[4 + i],
            recv_sem=rim_recv.at[i, j],
            device_id=((level + 1) * plane, core),
            device_id_type=MESH,
        )

    def block_rows(b):
        return pl.ds(pl.multiple_of(b * cap, cap), cap)

    def sort_into(ref, hh, b, lanes, rows):
        shaped = rows.reshape(pairs, 2, cap, rows.shape[1])
        ref[hh * pairs : (hh + 1) * pairs, :, block_rows(b), lanes] = shaped

    def sorted_rows(ref, hh, b, lanes):
        rows = ref[hh * pairs : (hh + 1) * pairs, :, block_rows(b), lanes]
        return rows.reshape(pool, rows.shape[3]).astype(BF16)

    def whole(ref, p, lanes):
        return ref[p, :, :, lanes].reshape(members, lanes.stop - lanes.start)

    one, two = slice(0, DH), slice(0, 2 * DH)

    middle = level >= near // plane - 1

    for j in range(plane - 1):

        @pl.when(relays & middle & (spot == j))
        def _():
            for i in range(2):
                pltpu.make_async_copy(relay.at[i], relay.at[i], relay_sem.at[i]).wait()
                pass_on(i, j).start()

    @pl.loop(0, near)
    def _(b):
        for kind in (K, V):
            got(kind, into(kind, b), b)

    @pl.when(early)
    def _():
        exchange(arrays[3:])

    @pl.when(crosses & (me < near - 1))
    def _():
        for j in range(4):
            for i in range(2):
                rim_first(i, j, j < plane - 1).start()

    @pl.when(straight & early)
    def _():
        for j in range(4):
            for i in range(2):
                rim_first(i, j, False).start()

    @pl.when(late)
    def _():
        exchange(arrays[3:])

    @pl.loop(0, near, unroll=4)
    def _(b):
        for hh in range(each):
            values = jnp.concatenate(
                [taken[b, :, of_head(kind, hh)] for kind in (K, V)]
                + [jnp.ones((n, DH), BF16)],
                axis=1,
            )
            rows = nn(hits_of(slots[b, hh], pool), values)
            sort_into(acc, hh, b, slice(DH, 3 * DH), rows[:, : 2 * DH])
            sort_into(work, hh, b, one, rows[:, 2 * DH :])

    row = lax.broadcasted_iota(jnp.int32, (members, members), 0)
    col = lax.broadcasted_iota(jnp.int32, (members, members), 1)
    same = (row // part) == (col // part)
    lane = lax.broadcasted_iota(jnp.int32, (members, DH), 1)
    pick = jnp.where(lane == 0, BIG, 0.0).astype(BF16)
    scale = factor * LOG2E

    def attend(group_of, queries, keys, values, allowed, prob_ref):
        scores = [
            jnp.where(allowed, nt(jnp.concatenate([q, pick], axis=1), k), -jnp.inf)
            for q, k in zip(queries, keys)
        ]
        tops = [jnp.max(s, axis=-1, keepdims=True) for s in scores]
        grown = [jnp.exp2((s - top) * scale) for s, top in zip(scores, tops)]
        sums = [jnp.sum(e, axis=-1, keepdims=True) for e in grown]
        weights = [(e * (1.0 / total)).astype(BF16) for e, total in zip(grown, sums)]
        for p, w, v, top, total in zip(group_of, weights, values, tops, sums):
            prob_ref[p] = w
            lse = top * scale + jnp.log(total) * LOG2E
            out = jnp.concatenate([nn(w, v), at_lanes((members, DH), in_parts(lse, 3))], axis=1)
            work[p] = out.reshape(2, part, 2 * DH)

    @pl.loop(0, rows16.shape[0], unroll=4)
    def _(p):
        for i, at in ((1, 1), (2, 3)):
            rows = whole(acc, p, slice(i * DH, (i + 1) * DH))
            rows16[p, :, at * DH : (at + 1) * DH] = rows.astype(BF16)
        rows16[p, :, 2 * DH : 3 * DH] = (whole(work, p, one) - 1.0).astype(BF16)

    def by_tokens(hh, b, slot_index):
        rows = sorted_rows(work, hh, b, two)
        return nn(hits_by_token(slots[slot_index, hh], pool), rows)

    @pl.when(early)
    def _():
        for hh in range(each):

            @pl.loop(0, near)
            def _(b):
                got(QX, x_in.at[b, :, hh * DH : (hh + 1) * DH], hh * near + b)

            @pl.loop(0, near, unroll=4)
            def _(b):
                view = x_in[b, :, hh * DH : (hh + 1) * DH]
                sort_into(work, hh, b, one, nn(hits_of(slots[near + b, hh], pool), view))

            @pl.loop(0, pairs // group)
            def _(g):
                group_of = [hh * pairs + g * group + i for i in range(group)]
                queries = [whole(work, p, one).astype(BF16) for p in group_of]
                for p, q in zip(group_of, queries):
                    xq16[p] = q
                keys = [rows16[p, :, DH : 3 * DH] for p in group_of]
                values = [rows16[p, :, 3 * DH :] for p in group_of]
                attend(group_of, queries, keys, values, same, probs_x)

            @pl.loop(0, near, unroll=4)
            def _(b):
                back = by_tokens(hh, b, near + b)
                at = hh * near + b
                view = x_out.at[b, :, hh * DH : (hh + 1) * DH]
                view[...] = back[:, :DH].astype(BF16)
                lse_out[at] = back[:, DH:].T[:8]
                dst = x_in.at[b, :, hh * DH : (hh + 1) * DH]
                remote(OX, view, dst, at, at, me + near).start()
                remote(LX, lse_out.at[at], lse_in.at[at], at, at, me + near).start()

    @pl.when(early)
    def _():
        @pl.loop(0, near)
        def _(b):
            got(Q, into(Q, b), b)

    @pl.loop(0, near, unroll=4)
    def _(b):
        for hh in range(each):
            view = taken[b, :, of_head(Q, hh)]
            sort_into(acc, hh, b, one, nn(hits_of(slots[b, hh], pool), view))

    @pl.loop(0, rows16.shape[0] // group)
    def _(g):
        group_of = [g * group + i for i in range(group)]
        queries = [whole(acc, p, one).astype(BF16) for p in group_of]
        for p, q in zip(group_of, queries):
            rows16[p, :, :DH] = q
        keys = [rows16[p, :, DH : 3 * DH] for p in group_of]
        values = [rows16[p, :, 3 * DH :] for p in group_of]
        attend(group_of, queries, keys, values, same & (col <= row), probs)

    for j in range(plane - 1):

        @pl.when(relays & ~middle & (spot == j))
        def _():
            for i in range(2):
                pltpu.make_async_copy(relay.at[i], relay.at[i], relay_sem.at[i]).wait()
                pass_on(i, j).start()

    @pl.loop(0, near, unroll=4)
    def _(b):
        for hh in range(each):
            back = by_tokens(hh, b, b)
            attn_own[b, :, hh * DH : (hh + 1) * DH] = back[:, :DH].astype(BF16)
            lse_own[hh * near + b] = back[:, DH:].T[:8]

    for load in loads:
        load.wait()

    pair[0] = jnp.zeros((8, n), F32)

    for j in range(4):

        @pl.when(me > 0)
        def _():
            for i in range(2):
                view = rim.at[i, :, span[j]]
                pltpu.make_async_copy(view, view, rim_recv.at[i, j]).wait()

        @pl.when(me == 0)
        def _():
            rim[:, :, span[j]] = jnp.zeros((2, n, quarter), BF16)

        @pl.loop(j * (heads // 4), (j + 1) * (heads // 4))
        def _(h):
            cols = columns(h, 1)
            keys = jnp.concatenate([rim[0, :, cols], wk_v[:, cols]], axis=0)
            vals = jnp.concatenate([rim[1, :, cols], wv_v[:, cols]], axis=0)
            prob = window_prob(factor, wq_v[:, cols], keys)
            attn = nn(prob.astype(BF16), vals).astype(BF16)
            attn_win[:, cols] = attn
            gained = wg_v[:, cols].astype(F32) * w_gain[:, cols]
            pair[0] += stat_rows(attn.astype(F32), gained)

    which = lax.broadcasted_iota(jnp.int32, (8, n), 0)

    def gained_of(b, hh):
        gain = c_gain[:, columns(t * each + hh, 1)]
        return taken[b, :, of_head(G, hh)].astype(F32) * gain

    def finish(b, merge):
        total = jnp.zeros((8, n), F32)
        for hh in range(each):
            at = hh * near + b
            lanes = slice(hh * DH, (hh + 1) * DH)
            if merge:
                mine = jnp.sum(lse_own[at][0:3], axis=0, keepdims=True)
                other = jnp.sum(lse_in[at][0:3], axis=0, keepdims=True)
                top = jnp.maximum(mine, other)
                mine, other = jnp.exp2(mine - top), jnp.exp2(other - top)
                share = jnp.where(which == 0, mine, other) / (mine + other)
                shares[at] = share
                by_token = share.T
                attn = by_token[:, 0:1] * attn_own[b, :, lanes].astype(F32)
                attn = attn + by_token[:, 1:2] * x_in[b, :, lanes].astype(F32)
                attn_own[b, :, lanes] = attn.astype(BF16)
            else:
                shares[at] = jnp.where(which == 0, 1.0, 0.0)
        for hh in range(each):
            attn = attn_own[b, :, hh * DH : (hh + 1) * DH].astype(F32)
            total = total + stat_rows(attn, gained_of(b, hh))
        part_out[b] = total
        deliver(PART, part_out.at[b], part_in.at[t], b, b, t)
        deliver(ATTN, attn_own.at[b], attn_home.at[:, columns(t * each, each)], b, b, t)

    for this_half, merge in ((early, False), (late, True)):

        @pl.when(this_half)
        def _():
            @pl.loop(0, near)
            def _(b):
                got(G, into(G, b), b)
                if merge:
                    for hh in range(each):
                        at = hh * near + b
                        got(OX, x_in.at[b, :, hh * DH : (hh + 1) * DH], at)
                        got(LX, lse_in.at[at], at)

            @pl.loop(0, near, unroll=2)
            def _(d):
                finish(peer(d + 1), merge)

    @pl.loop(0, near)
    def _(b):
        got(PART, part_in.at[b], b)
        pair[0] += part_in[b]

    swap = pltpu.make_async_remote_copy(
        src_ref=pair.at[0],
        dst_ref=pair.at[1],
        send_sem=pair_sem.at[0],
        recv_sem=pair_sem.at[1],
        device_id=(me, 1 - core),
        device_id_type=MESH,
    )
    swap.start()
    swap.wait()
    totals = pair[0] + pair[1]
    inv = 1.0 / jnp.sqrt(totals[0:1] / feat_width + EPSILON)
    coef = inv * inv * inv * totals[1:2] / feat_width
    stat_own[...] = jnp.where(which == 0, inv, coef)

    @pl.loop(0, near)
    def _(d):
        b = peer(d + 1)
        deliver(STAT, stat_own, stats.at[t], b, b, t)

    def dout_of(hh, b):
        by_token = stats[b].T
        attn = attn_own[b, :, hh * DH : (hh + 1) * DH].astype(F32)
        dout = by_token[:, 0:1] * gained_of(b, hh) - by_token[:, 1:2] * attn
        return dout.astype(BF16).astype(F32), attn

    def visit(hh, b):
        lanes = slice(hh * DH, (hh + 1) * DH)
        at = hh * near + b
        dout, attn = dout_of(hh, b)
        terms = dout * attn
        share = shares[at]
        view = d_out.at[b, :, lanes]
        view[...] = (share.T[:, 1:2] * dout).astype(BF16)
        high = terms.astype(BF16)
        low = (terms - high.astype(F32)).astype(BF16)
        sums = nt(every, high) + nt(every, low)
        first, second = in_parts(sums * share[1:2], 2)
        dot_out[at] = jnp.where(which == 0, first, jnp.where(which == 1, second, 0.0))
        remote(DX, view, d_in.at[b, :, lanes], at, at, me - near).start()
        remote(RX, dot_out.at[at], dot_in.at[at], at, at, me - near).start()

    def spread(hh, b, is_late):
        dout, attn = dout_of(hh, b)
        row_dot = jnp.sum(dout * attn, axis=-1, keepdims=True)
        if is_late:
            share = shares[hh * near + b].T
            dout, row_dot = share[:, 0:1] * dout, share[:, 0:1] * row_dot
        dots = at_lanes((n, DH), in_parts(row_dot, 2)).astype(BF16)
        both = jnp.concatenate([dout.astype(BF16), dots], axis=1)
        sort_into(work, hh, b, two, nn(hits_of(slots[b, hh], pool), both))

    every = jnp.ones((8, DH), BF16)

    def spread_all(is_late):
        @pl.loop(0, near)
        def _(b):
            got(STAT, stats.at[b], b)

        if is_late:
            for hh in range(each):

                @pl.loop(0, near, unroll=4)
                def _(d):
                    visit(hh, peer(d + 1))

        for hh in range(each):

            @pl.loop(0, near, unroll=4)
            def _(d):
                spread(hh, peer(d + 1), is_late)

    @pl.when(late)
    def _():
        spread_all(True)

    @pl.loop(0, near)
    def _(b):
        got(ATTN, attn_home.at[:, columns(b * each, each)], b)

    for j in range(plane - 1):

        @pl.when(relays & (spot == j))
        def _():
            for i in range(2):
                pass_on(i, j).wait_send()

    @pl.when(crosses)
    def _():
        for j in range(4):
            for i in range(2):
                rim_first(i, j, j < plane - 1).wait_send()

    @pl.when(straight)
    def _():
        for j in range(4):
            for i in range(2):
                rim_first(i, j, False).wait_send()

    back_crosses = (spot == 0) & (me > 0)
    back_straight = spot != 0
    back_relays = (spot != 0) & (me >= plane)

    def back_copy(j, src, dst, sem, to):
        return pltpu.make_async_remote_copy(
            src_ref=src,
            dst_ref=dst,
            send_sem=rim_send.at[2, j],
            recv_sem=sem,
            device_id=(to, core),
            device_id_type=MESH,
        )

    def back_first(j, by_relay):
        src = rim.at[:, :, span[j]]
        if by_relay:
            return back_copy(j, src, relay_back, relay_sem.at[2], level * plane + j)
        return back_copy(j, src, rim_back.at[:, :, span[j]], rim_recv.at[2, j], me - 1)

    by_token = stat_own[...].T
    inv_col, coef_col = by_token[:, 0:1], by_token[:, 1:2]
    for j in (1, 2, 3, 0):

        @pl.loop(j * (heads // 4), (j + 1) * (heads // 4))
        def _(h):
            cols = columns(h, 1)
            q = wq_v[:, cols]
            keys = jnp.concatenate([rim[0, :, cols], wk_v[:, cols]], axis=0)
            vals = jnp.concatenate([rim[1, :, cols], wv_v[:, cols]], axis=0)
            attn = attn_win[:, cols].astype(F32)
            gained = wg_v[:, cols].astype(F32) * w_gain[:, cols]
            grad = (inv_col * gained - coef_col * attn).astype(BF16)
            prob = window_prob(factor, q, keys)
            row_dot = jnp.sum(grad.astype(F32) * attn, axis=-1, keepdims=True)
            change = (prob * (nt(grad, vals) - row_dot)).astype(BF16)
            wq_v[:, cols] = (nn(change, keys) * factor).astype(BF16)
            dk = tn(change, q)
            dv = tn(prob.astype(BF16), grad)
            rim[0, :, cols] = dk[:WINDOW].astype(BF16)
            rim[1, :, cols] = dv[:WINDOW].astype(BF16)
            wk_v[:, cols] = dk[WINDOW:].astype(BF16)
            wv_v[:, cols] = dv[WINDOW:].astype(BF16)
            attn_win[:, cols] = (attn * inv_col * w_gain[:, cols]).astype(BF16)
            clu = attn_home[:, cols].astype(F32)
            attn_home[:, cols] = (clu * inv_col * c_gain[:, cols]).astype(BF16)

        @pl.when(back_crosses)
        def _():
            back_first(j, 0 < j < plane).start()

        @pl.when(back_straight)
        def _():
            back_first(j, False).start()

    stores = [
        pltpu.make_async_copy(src, dst, local_sem.at[4 + i])
        for i, (src, dst) in enumerate(
            [
                (attn_win, win_normed),
                (attn_home, clu_normed),
                (wq_v, win_dq),
                (wk_v, win_dk),
                (wv_v, win_dv),
            ]
        )
    ]
    for store in stores[:3]:
        store.start()

    @pl.when(early)
    def _():
        spread_all(False)

    minus = jnp.where(lane < 2, -1.0, 0.0).astype(BF16)

    def changes_of(group_of, prob_ref):
        slopes = []
        for p in group_of:
            v = jnp.concatenate([rows16[p, :, 3 * DH :], minus], axis=1)
            slopes.append(nt(whole(work, p, two).astype(BF16), v))
        return [(prob_ref[p].astype(F32) * s).astype(BF16) for p, s in zip(group_of, slopes)]

    def split_rows(x):
        return x.reshape(2, part, DH)

    second, third = slice(DH, 2 * DH), slice(2 * DH, 3 * DH)

    @pl.loop(0, rows16.shape[0] // group)
    def _(g):
        group_of = [g * group + i for i in range(group)]
        for p, change in zip(group_of, changes_of(group_of, probs)):
            grad = whole(work, p, one).astype(BF16)
            acc[p, :, :, one] = split_rows(nn(change, rows16[p, :, DH : 2 * DH]) * factor)
            acc[p, :, :, second] = split_rows(tn(change, rows16[p, :, :DH]))
            acc[p, :, :, third] = split_rows(tn(probs[p], grad))

    @pl.when(late)
    def _():
        @pl.loop(0, near)
        def _(b):
            for hh in range(each):
                sent(QX, taken.at[b, :, of_head(Q, hh)], hh * near + b)

    homes = [(DQ, clu_dq), (DK, clu_dk), (DV, clu_dv)]

    def home_of(i, hh, owner):
        return homes[i][1].at[:, columns(owner * each + hh, 1)]

    def give(i, hh, b):
        at = hh * near + b
        view = taken.at[b, :, of_head(i, hh)]
        deliver(homes[i][0], view, home_of(i, hh, t), b, at, hh * near + t)

    def keys_home(hh, b, hits):
        rows = sorted_rows(acc, hh, b, slice(DH, 3 * DH))
        back = nn(hits, rows)
        taken[b, :, of_head(1, hh)] = (back[:, :DH] * factor).astype(BF16)
        taken[b, :, of_head(2, hh)] = back[:, DH:].astype(BF16)
        give(1, hh, b)
        give(2, hh, b)

    for hh in range(each):

        def own_home(b, is_late):
            hits = hits_by_token(slots[b, hh], pool)
            taken[b, :, of_head(0, hh)] = nn(hits, sorted_rows(acc, hh, b, one)).astype(BF16)
            if is_late:
                keys_home(hh, b, hits)
            else:
                give(0, hh, b)

        for this_half, is_late in ((early, False), (late, True)):

            @pl.when(this_half)
            def _():
                @pl.loop(0, near, unroll=2)
                def _(d):
                    own_home(peer(d + 1), is_late)

    def pass_back(j):
        dst = rim_back.at[:, :, span[j]]
        return pltpu.make_async_remote_copy(
            src_ref=relay_back,
            dst_ref=dst,
            send_sem=relay_sem.at[3],
            recv_sem=rim_recv.at[2, j],
            device_id=(level * plane - 1, core),
            device_id_type=MESH,
        )

    for j in range(1, plane):

        @pl.when(back_relays & (spot == j))
        def _():
            pltpu.make_async_copy(relay_back, relay_back, relay_sem.at[2]).wait()
            pass_back(j).start()

    @pl.when(early)
    def _():
        for hh in range(each):
            lanes = slice(hh * DH, (hh + 1) * DH)

            @pl.loop(0, near)
            def _(b):
                at = hh * near + b
                got(DX, d_in.at[b, :, lanes], at)
                got(RX, dot_in.at[at], at)
                sent(OX, x_out.at[b, :, lanes], at)

            @pl.loop(0, near, unroll=4)
            def _(b):
                at = hh * near + b
                dots = jnp.concatenate(
                    [dot_in[at].T, jnp.zeros((n, DH - 8), F32)], axis=1
                ).astype(BF16)
                both = jnp.concatenate([d_in[b, :, lanes], dots], axis=1)
                sort_into(work, hh, b, two, nn(hits_of(slots[near + b, hh], pool), both))

            @pl.loop(0, pairs // group)
            def _(g):
                group_of = [hh * pairs + g * group + i for i in range(group)]
                for p, change in zip(group_of, changes_of(group_of, probs_x)):
                    grad = whole(work, p, one).astype(BF16)
                    acc[p, :, :, second] += split_rows(tn(change, xq16[p]))
                    acc[p, :, :, third] += split_rows(tn(probs_x[p], grad))
                    dq = nn(change, rows16[p, :, DH : 2 * DH]) * factor
                    work[p, :, :, one] = split_rows(dq)

            @pl.loop(0, near, unroll=2)
            def _(d):
                b = peer(d + 1)
                at = hh * near + b
                hits = hits_by_token(slots[near + b, hh], pool)
                view = x_out.at[b, :, lanes]
                view[...] = nn(hits, sorted_rows(work, hh, b, one)).astype(BF16)
                remote(DQX, view, d_in.at[b, :, lanes], at, at, me + near).start()

            @pl.loop(0, near, unroll=2)
            def _(d):
                b = peer(d + 1)
                keys_home(hh, b, hits_by_token(slots[b, hh], pool))

    @pl.when(late)
    def _():
        for hh in range(each):
            lanes = slice(hh * DH, (hh + 1) * DH)

            @pl.loop(0, near)
            def _(d):
                b = peer(d + 1)
                got(DQX, d_in.at[b, :, lanes], hh * near + b)
                more = d_in[b, :, lanes].astype(F32)
                view = taken.at[b, :, of_head(0, hh)]
                view[...] = (view[...].astype(F32) + more).astype(BF16)
                give(0, hh, b)

    @pl.when(me < n_seq - 1)
    def _():
        for j in range(4):
            view = rim_back.at[:, :, span[j]]
            pltpu.make_async_copy(view, view, rim_recv.at[2, j]).wait()

    @pl.when(me == n_seq - 1)
    def _():
        rim_back[...] = jnp.zeros_like(rim_back)

    @pl.loop(0, heads)
    def _(h):
        cols = columns(h, 1)
        dk = wk_v[:, cols].astype(F32) + rim_back[0, :, cols].astype(F32)
        wk_v[:, cols] = (dk * factor).astype(BF16)
        dv = wv_v[:, cols].astype(F32) + rim_back[1, :, cols].astype(F32)
        wv_v[:, cols] = dv.astype(BF16)

    for store in stores[3:]:
        store.start()

    for j in range(4):

        @pl.when(back_crosses)
        def _():
            back_first(j, 0 < j < plane).wait_send()

        @pl.when(back_straight)
        def _():
            back_first(j, False).wait_send()

    for j in range(1, plane):

        @pl.when(back_relays & (spot == j))
        def _():
            pass_back(j).wait_send()

    @pl.loop(1, near)
    def _(d):
        to = peer(d)
        for kind, src in arrays:
            sent(kind, src.at[:, columns(to * each, each)], to)
        sent(IDS, ids.at[pl.ds(to * each, each)], to)
        sent(PART, part_out.at[to], to)
        sent(ATTN, attn_own.at[to], to)
        sent(STAT, stat_own, to)
        for hh in range(each):
            for i, (kind, home) in enumerate(homes):
                sent(kind, taken.at[to, :, of_head(i, hh)], hh * near + to)

    @pl.loop(0, near)
    def _(b):
        for hh in range(each):
            for i, (kind, home) in enumerate(homes):
                got(kind, home_of(i, hh, b), hh * near + b)

    @pl.when(late)
    def _():
        @pl.loop(0, near)
        def _(b):
            sent(IDSX, ids.at[pl.ds(b * each, each)], b)
            for hh in range(each):
                at = hh * near + b
                sent(DX, d_out.at[b, :, hh * DH : (hh + 1) * DH], at)
                sent(RX, dot_out.at[at], at)

    @pl.when(early)
    def _():
        @pl.loop(0, near)
        def _(b):
            for hh in range(each):
                at = hh * near + b
                sent(LX, lse_out.at[at], at)
                sent(DQX, x_out.at[b, :, hh * DH : (hh + 1) * DH], at)

    for store in stores:
        store.wait()


def copy_kernel(*refs):
    count = len(refs) // 2
    for src, dst in zip(refs[:count], refs[count:]):
        dst[...] = src[...]


def settle(arrays):
    n, wide = arrays[0].shape
    block = pl.BlockSpec((n // 8, wide), lambda i: (i, 0))
    return pl.pallas_call(
        copy_kernel,
        grid=(8,),
        in_specs=[block] * len(arrays),
        out_specs=[block] * len(arrays),
        out_shape=[jax.ShapeDtypeStruct((n, wide), BF16)] * len(arrays),
        compiler_params=pltpu.CompilerParams(vmem_limit_bytes=32 << 20),
    )(*arrays)


def layer(*arrays):
    win_query, cluster_ids = arrays[0], arrays[6]
    n, wide = win_query.shape
    sources = lax.axis_size("seq")
    near = sources // 2
    cap = SLOTS // sources
    clusters = sources * (2 * n // SLOTS)
    part = near * cap
    heads = wide // DH
    each = heads // near
    pairs = each * clusters // 2
    given = list(arrays)
    given[6] = cluster_ids[:, None, :]
    given[7], given[8] = arrays[7][None, :], arrays[8][None, :]
    anywhere = pl.BlockSpec(memory_space=pl.ANY)
    vmem = pl.BlockSpec(memory_space=pltpu.VMEM)
    group = next(g for g in (16, 8, 4, 2, 1) if clusters // 2 % g == 0)
    rows_of = pltpu.VMEM((each * near, 8, n), F32)
    results = pl.pallas_call(
        functools.partial(layer_kernel, DH ** (-0.5), cap, group, 4),
        in_specs=[anywhere] * 6 + [vmem] * 3 + [anywhere] * 2,
        out_specs=[anywhere] * 8,
        out_shape=[jax.ShapeDtypeStruct((n, wide), BF16)] * 8,
        scratch_shapes=[
            pltpu.VMEM((near, n, 4 * each * DH), BF16),
            pltpu.VMEM((sources, each, 1, n), jnp.int32),
            pltpu.VMEM((sources, each, 1, n), jnp.int32),
        ]
        + [pltpu.VMEM((n, wide), BF16)] * 4
        + [pltpu.VMEM((2, n, wide), BF16)] * 2
        + [pltpu.VMEM((2, n, wide // 4), BF16)] * 2
        + [pltpu.VMEM((n, wide), BF16)] * 2
        + [pltpu.VMEM((near, n, each * DH), BF16)] * 5
        + [
            pltpu.VMEM((pairs, 2 * part, 4 * DH), BF16),
            pltpu.VMEM((pairs, 2 * part, DH), BF16),
            pltpu.VMEM((pairs, 2, part, 2 * DH), F32),
            pltpu.VMEM((pairs, 2, part, 3 * DH), F32),
            pltpu.VMEM((pairs, 2 * part, 2 * part), BF16),
            pltpu.VMEM((pairs, 2 * part, 2 * part), BF16),
        ]
        + [rows_of] * 6
        + [
            pltpu.VMEM((near, 8, n), F32),
            pltpu.VMEM((near, 8, n), F32),
            pltpu.VMEM((2, 8, n), F32),
            pltpu.VMEM((8, n), F32),
            pltpu.VMEM((near, 8, n), F32),
            pltpu.SemaphoreType.DMA((18, sources)),
            pltpu.SemaphoreType.DMA((18, sources)),
            pltpu.SemaphoreType.DMA((3, 4)),
            pltpu.SemaphoreType.DMA((3, 4)),
            pltpu.SemaphoreType.DMA((6,)),
            pltpu.SemaphoreType.DMA((2,)),
            pltpu.SemaphoreType.DMA((9,)),
        ],
        cost_estimate=pl.CostEstimate(
            flops=14 * n * 2 * n * wide, bytes_accessed=16 * n * wide * 2, transcendentals=0
        ),
        compiler_params=pltpu.CompilerParams(
            vmem_limit_bytes=60 << 20, collective_id=0, has_side_effects=True
        ),
    )(*given)
    return settle(results)


def solution(mesh):
    sources, split = mesh.shape["seq"], mesh.shape["head"]
    whole_heads = HC // split == sources and SLOTS // sources % 8 == 0 and split == 2 and sources % 4 == 0
    return jax.shard_map(
        layer if whole_heads else body,
        mesh=mesh,
        in_specs=(P("seq", "head"),) * 6
        + (P("head", "seq"), P("head"), P("head"))
        + (P("seq", "head"),) * 2,
        out_specs=(P("seq", "head"),) * 8,
        check_vma=False,
    )
```

```python
import functools

import jax
import jax.numpy as jnp
from jax import lax
from jax.experimental import pallas as pl
from jax.experimental.pallas import tpu as pltpu
from jax.sharding import PartitionSpec as P

HW = 32
HC = 32
DH = 128
WINDOW = 256
SLOTS = 128
CHUNKS = 2

EPSILON = 1e-06
F32 = jnp.float32
BF16 = jnp.bfloat16


def from_behind(block, axis, distance):
    devices = range(lax.axis_size(axis))
    route = [(i - distance, i) for i in devices if i - distance in devices]
    return lax.ppermute(block, axis, route)


def nt(a, b):
    return lax.dot_general(a, b, (((1,), (1,)), ((), ())), preferred_element_type=F32)


def tn(a, b):
    return lax.dot_general(a, b, (((0,), (0,)), ((), ())), preferred_element_type=F32)


def nn(a, b):
    return jnp.dot(a, b, preferred_element_type=F32)


def one_hot(slot_ref, pool):
    n = slot_ref.shape[-1]
    hit = lax.broadcasted_iota(jnp.int32, (pool, n), 0) == slot_ref[0]
    return jnp.where(hit, 1.0, 0.0).astype(BF16)


def normalized(scores, allowed):
    masked = jnp.where(allowed, scores, -jnp.inf)
    grown = jnp.exp(masked - jnp.max(masked, axis=-1, keepdims=True))
    return grown * (1.0 / jnp.sum(grown, axis=-1, keepdims=True))


def call(kernel, grid, in_specs, out_specs, out_shape, flops, size, **more):
    return pl.pallas_call(
        kernel,
        grid=grid,
        in_specs=in_specs,
        out_specs=out_specs,
        out_shape=out_shape,
        cost_estimate=pl.CostEstimate(flops=flops, bytes_accessed=size, transcendentals=0),
        compiler_params=pltpu.CompilerParams(vmem_limit_bytes=48 << 20),
        **more,
    )


def dispatch_kernel(*refs):
    slot_ref, value_refs, out_ref = refs[0], refs[1:-1], refs[-1]
    picked = one_hot(slot_ref, out_ref.shape[0])
    for i, ref in enumerate(value_refs):
        out_ref[:, i * DH : (i + 1) * DH] = nn(picked, ref[...]).astype(BF16)


def dispatch(slot_at, values, first, count, pool):
    n = slot_at.shape[-1]
    wide = len(values) * DH
    return call(
        dispatch_kernel,
        (count,),
        [pl.BlockSpec((1, 1, n), lambda h: (h + first, 0, 0))]
        + [pl.BlockSpec((n, DH), lambda h: (0, h + first)) for _ in values],
        pl.BlockSpec((pool, wide), lambda h: (0, h)),
        jax.ShapeDtypeStruct((pool, count * wide), BF16),
        2 * count * pool * n * wide,
        2 * count * (pool + n) * wide,
    )(slot_at, *values)


def collect_kernel(n_out, *refs):
    slot_ref, rows_ref, out_refs = refs[0], refs[1], refs[-n_out:]
    picked = one_hot(slot_ref, rows_ref.shape[0])
    merged = tn(picked, rows_ref[...]).astype(BF16)
    for i, ref in enumerate(out_refs):
        ref[...] = merged[:, i * DH : (i + 1) * DH]


def collect(slot_at, rows, first, count, n_out, earlier):
    n = slot_at.shape[-1]
    pool = rows.shape[0]
    heads = slot_at.shape[0]
    wide = n_out * DH
    return call(
        functools.partial(collect_kernel, n_out),
        (count,),
        [
            pl.BlockSpec((1, 1, n), lambda h: (h + first, 0, 0)),
            pl.BlockSpec((pool, wide), lambda h: (0, h)),
        ]
        + [pl.BlockSpec(memory_space=pl.ANY) for _ in earlier],
        [pl.BlockSpec((n, DH), lambda h: (0, h + first))] * n_out,
        [jax.ShapeDtypeStruct((n, heads * DH), BF16)] * n_out,
        2 * count * pool * n * wide,
        2 * count * (pool + n) * wide,
        input_output_aliases={2 + i: i for i in range(len(earlier))},
    )(slot_at, rows, *earlier)


class Rows:
    def __init__(self, sources, owned, cap):
        self.sources, self.owned, self.cap = sources, owned, cap
        self.aligned = cap % 8 == 0

    def selector(self, c):
        members = self.sources * self.cap
        layout = (members, members * self.owned)
        member = lax.broadcasted_iota(jnp.int32, layout, 0)
        row = lax.broadcasted_iota(jnp.int32, layout, 1)
        want = member // self.cap * (self.cap * self.owned) + c * self.cap + member % self.cap
        return jnp.where(row == want, 1.0, 0.0).astype(BF16)

    def split(self, rows):
        members = self.sources * self.cap
        if not self.aligned:
            return [nn(self.selector(c), rows).astype(BF16) for c in range(self.owned)]
        wide = rows.shape[1]
        four = rows.astype(F32).reshape(self.sources, self.owned, self.cap, wide)
        return [four[:, c].reshape(members, wide).astype(BF16) for c in range(self.owned)]

    def join(self, parts):
        wide = parts[0].shape[1]
        pool = self.sources * self.cap * self.owned
        if not self.aligned:
            total = jnp.zeros((pool, wide), F32)
            for c, part in enumerate(parts):
                total = total + tn(self.selector(c), part.astype(BF16))
            return total.astype(BF16)
        shaped = [p.reshape(self.sources, 1, self.cap, wide) for p in parts]
        return jnp.concatenate(shaped, axis=1).reshape(pool, wide).astype(BF16)


def cluster_allowed(live_ref, c, members):
    row = lax.broadcasted_iota(jnp.int32, (members, members), 0)
    col = lax.broadcasted_iota(jnp.int32, (members, members), 1)
    live = jnp.broadcast_to(live_ref[0, c : c + 1, :], (members, members)) > 0.5
    return (live & (col <= row)) | (col == row)


def owner_fwd_kernel(rows, factor, live_ref, qkv_ref, out_ref):
    members = rows.sources * rows.cap
    parts = []
    for c, qkv in enumerate(rows.split(qkv_ref[...])):
        q, k, v = qkv[:, :DH], qkv[:, DH : 2 * DH], qkv[:, 2 * DH :]
        prob = normalized(nt(q, k) * factor, cluster_allowed(live_ref, c, members))
        parts.append(nn(prob.astype(BF16), v))
    out_ref[...] = rows.join(parts)


def owner_bwd_kernel(rows, factor, live_ref, qkv_ref, attn_ref, grad_ref, out_ref):
    members = rows.sources * rows.cap
    attn_parts = rows.split(attn_ref[...])
    grad_parts = rows.split(grad_ref[...])
    parts = []
    for c, qkv in enumerate(rows.split(qkv_ref[...])):
        q, k, v = qkv[:, :DH], qkv[:, DH : 2 * DH], qkv[:, 2 * DH :]
        grad = grad_parts[c]
        row_dot = jnp.sum(grad.astype(F32) * attn_parts[c].astype(F32), axis=-1, keepdims=True)
        prob = normalized(nt(q, k) * factor, cluster_allowed(live_ref, c, members))
        change = (prob * (nt(grad, v) - row_dot)).astype(BF16)
        dq = nn(change, k) * factor
        dk = tn(change, q) * factor
        dv = tn(prob.astype(BF16), grad)
        parts.append(jnp.concatenate([dq, dk, dv], axis=1))
    out_ref[...] = rows.join(parts)


def owner_call(kernel, rows, factor, live, first, arrays, n_out):
    pool = arrays[0].shape[0]
    count = arrays[0].shape[1] // (3 * DH)
    members = rows.sources * rows.cap
    wides = [a.shape[1] // count for a in arrays]
    return call(
        functools.partial(kernel, rows, factor),
        (count,),
        [pl.BlockSpec((1, rows.owned, members), lambda h: (h + first, 0, 0))]
        + [pl.BlockSpec((pool, w), lambda h: (0, h)) for w in wides],
        pl.BlockSpec((pool, n_out * DH), lambda h: (0, h)),
        jax.ShapeDtypeStruct((pool, count * n_out * DH), BF16),
        12 * count * pool * members * DH,
        2 * count * pool * (sum(wides) + n_out * DH),
    )(live, *arrays)


def window_prob(factor, q, keys):
    n = q.shape[0]
    row = lax.broadcasted_iota(jnp.int32, (n, n + WINDOW), 0)
    col = lax.broadcasted_iota(jnp.int32, (n, n + WINDOW), 1)
    gap = row + WINDOW - col
    lowest = jnp.where(lax.axis_index("seq") > 0, 0, WINDOW)
    allowed = (gap >= 0) & (gap < WINDOW) & (col >= lowest)
    return normalized(nt(q, keys) * factor, allowed)


def window_fwd_kernel(factor, q_ref, kp_ref, k_ref, vp_ref, v_ref, out_ref):
    keys = jnp.concatenate([kp_ref[0], k_ref[...]], axis=0)
    vals = jnp.concatenate([vp_ref[0], v_ref[...]], axis=0)
    prob = window_prob(factor, q_ref[...], keys)
    out_ref[...] = nn(prob.astype(BF16), vals).astype(BF16)


def window_bwd_kernel(
    factor, q_ref, kp_ref, k_ref, vp_ref, v_ref, attn_ref, grad_ref, dq_ref, dk_ref, dv_ref, rim_ref
):
    q, grad = q_ref[...], grad_ref[...]
    keys = jnp.concatenate([kp_ref[0], k_ref[...]], axis=0)
    vals = jnp.concatenate([vp_ref[0], v_ref[...]], axis=0)
    prob = window_prob(factor, q, keys)
    row_dot = jnp.sum(grad.astype(F32) * attn_ref[...].astype(F32), axis=-1, keepdims=True)
    change = (prob * (nt(grad, vals) - row_dot)).astype(BF16)
    dq_ref[...] = (nn(change, keys) * factor).astype(BF16)
    dk = tn(change, q)
    dv = tn(prob.astype(BF16), grad)
    rim_ref[0] = dk[:WINDOW].astype(BF16)
    rim_ref[1] = dv[:WINDOW].astype(BF16)
    dk_ref[...] = dk[WINDOW:]
    dv_ref[...] = dv[WINDOW:]


def window_specs(n):
    here = pl.BlockSpec((n, DH), lambda h: (0, h))
    key = pl.BlockSpec((1, n, DH), lambda h: (0, 0, h))
    val = pl.BlockSpec((1, n, DH), lambda h: (1, 0, h))
    return here, key, val


def window_fwd(factor, query, key, value, before):
    n, wide = query.shape
    here, rim_key, rim_val = window_specs(n)
    return call(
        functools.partial(window_fwd_kernel, factor),
        (wide // DH,),
        [here, rim_key, here, rim_val, here],
        here,
        jax.ShapeDtypeStruct((n, wide), BF16),
        4 * n * 2 * n * wide,
        12 * n * wide,
    )(query, before, key, before, value)


def window_bwd(factor, query, key, value, before, attn, grad):
    n, wide = query.shape
    here, rim_key, rim_val = window_specs(n)
    return call(
        functools.partial(window_bwd_kernel, factor),
        (wide // DH,),
        [here, rim_key, here, rim_val, here, here, here],
        [here, here, here, pl.BlockSpec((2, n, DH), lambda h: (0, 0, h))],
        [
            jax.ShapeDtypeStruct((n, wide), BF16),
            jax.ShapeDtypeStruct((n, wide), F32),
            jax.ShapeDtypeStruct((n, wide), F32),
            jax.ShapeDtypeStruct((2, n, wide), BF16),
        ],
        10 * n * 2 * n * wide,
        28 * n * wide,
    )(query, before, key, before, value, attn, grad)


def body(
    win_query,
    win_key,
    win_value,
    clu_query,
    clu_key,
    clu_value,
    cluster_ids,
    win_gain,
    clu_gain,
    win_out_grad,
    clu_out_grad,
):
    n_rows = win_query.shape[0]
    factor = DH ** (-0.5)
    feat_width = (HW + HC) * DH
    sources = lax.axis_size("seq")
    n_cap = SLOTS // sources
    owned_count = 2 * n_rows // SLOTS
    pool_size = 2 * n_rows
    clu_heads = clu_query.shape[1] // DH
    rows = Rows(sources, owned_count, n_cap)

    def exchange(values):
        shaped = values.reshape(sources, pool_size // sources, values.shape[1])
        moved = lax.all_to_all(shaped, "seq", split_axis=0, concat_axis=0, tiled=True)
        return moved.reshape(values.shape)

    row_ids = lax.broadcasted_iota(jnp.int32, (n_rows, n_rows), 0)
    col_ids = lax.broadcasted_iota(jnp.int32, (n_rows, n_rows), 1)
    same_cluster = (cluster_ids[:, :, None] == cluster_ids[:, None, :]) & (col_ids < row_ids)
    rank_in = jnp.sum(same_cluster.astype(jnp.int32), axis=-1)
    slot_at = (cluster_ids * n_cap + rank_in)[:, None, :]

    n_clusters = sources * owned_count
    every = lax.broadcasted_iota(jnp.int32, (n_clusters, clu_heads, n_rows), 0)
    counts = jnp.sum((cluster_ids[None] == every).astype(F32), axis=-1)
    counts = counts.reshape(sources, owned_count, clu_heads)
    counts = lax.all_to_all(counts, "seq", split_axis=0, concat_axis=0, tiled=True)
    slot_pos = lax.broadcasted_iota(F32, (clu_heads, owned_count, sources, n_cap), 3)
    live = (slot_pos < counts.transpose(2, 1, 0)[..., None]).astype(F32)
    live = live.reshape(clu_heads, owned_count, sources * n_cap)

    chunks = CHUNKS if clu_heads % CHUNKS == 0 else 1
    per = clu_heads // chunks
    starts = [i * per for i in range(chunks)]

    held = [
        exchange(dispatch(slot_at, [clu_query, clu_key, clu_value], first, per, pool_size))
        for first in starts
    ]
    before = from_behind(jnp.stack([win_key, win_value]), "seq", 1)
    attn_win = window_fwd(factor, win_query, win_key, win_value, before)

    attn_held = [
        owner_call(owner_fwd_kernel, rows, factor, live, first, [qkv], 1)
        for first, qkv in zip(starts, held)
    ]
    attn_back = [exchange(part) for part in attn_held]
    attn_clu = ()
    for first, part in zip(starts, attn_back):
        attn_clu = collect(slot_at, part, first, per, 1, attn_clu)
    attn_clu = attn_clu[0]

    flat_win = attn_win.astype(F32)
    flat_clu = attn_clu.astype(F32)
    grad_win = win_out_grad.astype(F32) * win_gain
    grad_clu = clu_out_grad.astype(F32) * clu_gain
    totals = jnp.stack(
        [
            jnp.sum(flat_win * flat_win, axis=1) + jnp.sum(flat_clu * flat_clu, axis=1),
            jnp.sum(grad_win * flat_win, axis=1) + jnp.sum(grad_clu * flat_clu, axis=1),
        ]
    )
    totals = lax.psum(totals, "head")
    sq_total, dot_total = totals[0], totals[1]
    inv_rms = 1.0 / jnp.sqrt(sq_total / feat_width + EPSILON)
    coef_rows = inv_rms**3 * dot_total / feat_width
    dout_clu = (inv_rms[:, None] * grad_clu - coef_rows[:, None] * flat_clu).astype(BF16)
    dout_win = (inv_rms[:, None] * grad_win - coef_rows[:, None] * flat_win).astype(BF16)
    win_normed = (flat_win * inv_rms[:, None] * win_gain).astype(BF16)
    clu_normed = (flat_clu * inv_rms[:, None] * clu_gain).astype(BF16)

    grad_held = [
        exchange(dispatch(slot_at, [dout_clu], first, per, pool_size)) for first in starts
    ]
    win_dq, key_own, val_own, rim = window_bwd(
        factor, win_query, win_key, win_value, before, attn_win, dout_win
    )
    after_rim = from_behind(rim, "seq", -1)

    clu_grads = ()
    sent = [
        owner_call(owner_bwd_kernel, rows, factor, live, first, [qkv, part, grad], 3)
        for first, qkv, part, grad in zip(starts, held, attn_held, grad_held)
    ]
    home = [exchange(part) for part in sent]
    win_dk = ((key_own + after_rim[0]) * factor).astype(BF16)
    win_dv = (val_own + after_rim[1]).astype(BF16)
    for first, part in zip(starts, home):
        clu_grads = collect(slot_at, part, first, per, 3, clu_grads)
    return (win_normed, clu_normed, win_dq, win_dk, win_dv, *clu_grads)


BIG = 1e30
MESH = pl.DeviceIdType.MESH
LOG2E = 1.4426950408889634


def hits_of(slot, pool):
    n = slot.shape[-1]
    hit = lax.broadcasted_iota(jnp.int32, (pool, n), 0) == slot
    return jnp.where(hit, 1.0, 0.0).astype(BF16)


def hits_by_token(slot, pool):
    n = slot.shape[-1]
    column = jnp.broadcast_to(slot.astype(F32), (8, n)).T[:, :1].astype(jnp.int32)
    hit = lax.broadcasted_iota(jnp.int32, (n, pool), 1) == column
    return jnp.where(hit, 1.0, 0.0).astype(BF16)


def stat_rows(attn, gained):
    wide = attn.shape[1]
    both = jnp.concatenate([attn * attn, gained * attn], axis=1)
    row = lax.broadcasted_iota(jnp.int32, (8, 2 * wide), 0)
    col = lax.broadcasted_iota(jnp.int32, (8, 2 * wide), 1)
    pick = jnp.where(col // wide == row, 1.0, 0.0).astype(BF16)
    high = both.astype(BF16)
    low = (both - high.astype(F32)).astype(BF16)
    return nt(pick, high) + nt(pick, low)


def head_cols(h):
    return pl.ds(pl.multiple_of(h * DH, DH), DH)


def columns(first, count):
    return pl.ds(pl.multiple_of(first * DH, DH), count * DH)


def at_lanes(shape, values):
    lane = lax.broadcasted_iota(jnp.int32, shape, 1)
    total = jnp.zeros(shape, F32)
    for i, value in enumerate(values):
        total = jnp.where(lane == i, value, total)
    return total


def in_parts(x, count):
    parts = []
    for _ in range(count - 1):
        parts.append(x.astype(BF16).astype(F32))
        x = x - parts[-1]
    return parts + [x]


def layer_kernel(
    factor,
    cap,
    group,
    plane,
    wq,
    wk,
    wv,
    cq,
    ck,
    cv,
    ids,
    w_gain,
    c_gain,
    wg,
    cg,
    win_normed,
    clu_normed,
    win_dq,
    win_dk,
    win_dv,
    clu_dq,
    clu_dk,
    clu_dv,
    taken,
    ids_in,
    slots,
    wq_v,
    wk_v,
    wv_v,
    wg_v,
    rim,
    rim_back,
    relay,
    relay_back,
    attn_win,
    attn_home,
    attn_own,
    x_in,
    d_in,
    x_out,
    d_out,
    rows16,
    xq16,
    work,
    acc,
    probs,
    probs_x,
    lse_own,
    lse_out,
    lse_in,
    dot_out,
    dot_in,
    shares,
    part_out,
    part_in,
    pair,
    stat_own,
    stats,
    send_sem,
    recv_sem,
    rim_send,
    rim_recv,
    relay_sem,
    pair_sem,
    local_sem,
):
    me, core = lax.axis_index("seq"), lax.axis_index("head")
    n_seq = lax.axis_size("seq")
    near = n_seq // 2
    half, t = me // near, lax.rem(me, near)
    base = half * near
    early, late = half == 0, half == 1
    n = wq.shape[0]
    heads = wq.shape[1] // DH
    each = heads // near
    pairs = rows16.shape[0] // each
    members = rows16.shape[1]
    part = members // 2
    clusters = 2 * pairs
    pool = clusters * cap
    feat_width = (HW + HC) * DH
    (Q, K, V, G, IDS, IDSX, QX, OX, LX, PART, ATTN, STAT, DX, RX, DQX, DQ, DK, DV) = range(18)

    def peer(d):
        d = lax.rem(d, near)
        return jnp.bitwise_xor(t, d) if near & (near - 1) == 0 else lax.rem(t + d, near)

    def remote(kind, src, dst, mine, theirs, to):
        return pltpu.make_async_remote_copy(
            src_ref=src,
            dst_ref=dst,
            send_sem=send_sem.at[kind, mine],
            recv_sem=recv_sem.at[kind, theirs],
            device_id=(to, core),
            device_id_type=MESH,
        )

    def got(kind, dst, index):
        pltpu.make_async_copy(dst, dst, recv_sem.at[kind, index]).wait()

    def sent(kind, src, index):
        pltpu.make_async_copy(src, src, send_sem.at[kind, index]).wait()

    def deliver(kind, src, dst, b, mine, theirs):
        @pl.when(b != t)
        def _():
            remote(kind, src, dst, mine, theirs, base + b).start()

        @pl.when(b == t)
        def _():
            pltpu.make_async_copy(src, dst, recv_sem.at[kind, theirs]).start()

    loads = [
        pltpu.make_async_copy(src, dst, local_sem.at[i])
        for i, (src, dst) in enumerate([(wq, wq_v), (wk, wk_v), (wv, wv_v), (wg, wg_v)])
    ]

    barrier = pltpu.get_barrier_semaphore()

    @pl.loop(1, n_seq)
    def _(d):
        to = lax.rem(me + d, n_seq)
        pl.semaphore_signal(barrier, inc=1, device_id=(to, core), device_id_type=MESH)

    pl.semaphore_signal(barrier, inc=1, device_id=(me, 1 - core), device_id_type=MESH)
    pl.semaphore_wait(barrier, n_seq)

    @pl.loop(0, near)
    def _(d):
        to = peer(d)
        view = ids.at[pl.ds(to * each, each)]
        deliver(IDS, view, ids_in.at[t], to, to, t)

        @pl.when(late)
        def _():
            remote(IDSX, view, ids_in.at[near + t], to, t, to).start()

    spot, level = lax.rem(me, plane), me // plane
    quarter = heads // 4 * DH
    span = [slice(j * quarter, (j + 1) * quarter) for j in range(4)]
    crosses = (spot == plane - 1) & (me < n_seq - 1)
    straight = (spot != plane - 1) & (me < n_seq - 1)
    relays = (spot != plane - 1) & (me < n_seq - plane)

    def rim_copy(i, j, src, dst, sem, to):
        return pltpu.make_async_remote_copy(
            src_ref=src,
            dst_ref=dst,
            send_sem=rim_send.at[i, j],
            recv_sem=sem,
            device_id=(to, core),
            device_id_type=MESH,
        )

    def rim_first(i, j, by_relay):
        src = (wk, wv)[i].at[:, span[j]]
        if by_relay:
            return rim_copy(i, j, src, relay.at[i], relay_sem.at[i], level * plane + j)
        return rim_copy(i, j, src, rim.at[i, :, span[j]], rim_recv.at[i, j], me + 1)

    arrays = [(Q, cq), (K, ck), (V, cv), (G, cg)]

    def into(kind, source):
        return taken.at[source, :, kind * each * DH : (kind + 1) * each * DH]

    def of_head(kind, hh):
        return slice((kind * each + hh) * DH, (kind * each + hh + 1) * DH)

    def exchange(some):
        @pl.loop(1, near)
        def _(d):
            to = peer(d)
            for kind, src in some:
                view = src.at[:, columns(to * each, each)]
                remote(kind, view, into(kind, t), to, t, base + to).start()

    @pl.when(late)
    def _():
        exchange(arrays[:1])

    @pl.when(crosses & (me == near - 1))
    def _():
        for j in range(4):
            for i in range(2):
                rim_first(i, j, j < plane - 1).start()

    @pl.when(early)
    def _():
        exchange(arrays[1:3])
        exchange(arrays[:1])

    for kind, src in arrays:
        view = src.at[:, columns(t * each, each)]
        pltpu.make_async_copy(view, into(kind, t), recv_sem.at[kind, t]).start()
    for load in loads:
        load.start()

    @pl.when(late)
    def _():
        for hh in range(each):

            @pl.loop(0, near)
            def _(b):
                if hh == 0:
                    got(Q, into(Q, b), b)
                view = taken.at[b, :, of_head(Q, hh)]
                dst = x_in.at[b, :, hh * DH : (hh + 1) * DH]
                remote(QX, view, dst, hh * near + b, hh * near + b, me - near).start()

    @pl.when(late)
    def _():
        @pl.when(crosses)
        def _():
            for j in range(4):
                for i in range(2):
                    rim_first(i, j, j < plane - 1).start()

        exchange(arrays[1:3])

        @pl.when(straight)
        def _():
            for j in range(4):
                for i in range(2):
                    rim_first(i, j, False).start()

    earlier = lax.broadcasted_iota(jnp.int32, (n, n), 0) < lax.broadcasted_iota(
        jnp.int32, (n, n), 1
    )
    earlier = jnp.where(earlier, 1.0, 0.0).astype(BF16)

    def place(b):
        for hh in range(each):
            of_block = ids_in[b, hh]
            member = hits_of(of_block, clusters)
            rank = jnp.sum(member.astype(F32) * nn(member, earlier), axis=0, keepdims=True)
            slots[b, hh] = of_block * cap + rank.astype(jnp.int32)

    @pl.loop(0, near)
    def _(b):
        got(IDS, ids_in.at[b], b)
        place(b)

    @pl.when(early)
    def _():
        @pl.loop(0, near)
        def _(b):
            got(IDSX, ids_in.at[near + b], b)
            place(near + b)

    def pass_on(i, j):
        return pltpu.make_async_remote_copy(
            src_ref=relay.at[i],
            dst_ref=rim.at[i, :, span[j]],
            send_sem=relay_sem.at[4 + i],
            recv_sem=rim_recv.at[i, j],
            device_id=((level + 1) * plane, core),
            device_id_type=MESH,
        )

    def block_rows(b):
        return pl.ds(pl.multiple_of(b * cap, cap), cap)

    def sort_into(ref, hh, b, lanes, rows):
        shaped = rows.reshape(pairs, 2, cap, rows.shape[1])
        ref[hh * pairs : (hh + 1) * pairs, :, block_rows(b), lanes] = shaped

    def sorted_rows(ref, hh, b, lanes):
        rows = ref[hh * pairs : (hh + 1) * pairs, :, block_rows(b), lanes]
        return rows.reshape(pool, rows.shape[3]).astype(BF16)

    def whole(ref, p, lanes):
        return ref[p, :, :, lanes].reshape(members, lanes.stop - lanes.start)

    one, two = slice(0, DH), slice(0, 2 * DH)

    middle = level >= near // plane - 1

    for j in range(plane - 1):

        @pl.when(relays & middle & (spot == j))
        def _():
            for i in range(2):
                pltpu.make_async_copy(relay.at[i], relay.at[i], relay_sem.at[i]).wait()
                pass_on(i, j).start()

    @pl.loop(0, near)
    def _(b):
        for kind in (K, V):
            got(kind, into(kind, b), b)

    @pl.when(crosses & (me < near - 1))
    def _():
        for j in range(4):
            for i in range(2):
                rim_first(i, j, j < plane - 1).start()

    @pl.when(straight & early)
    def _():
        for j in range(2):
            for i in range(2):
                rim_first(i, j, False).start()

    @pl.when(early)
    def _():
        exchange(arrays[3:])

    @pl.when(straight & early)
    def _():
        for j in range(2, 4):
            for i in range(2):
                rim_first(i, j, False).start()

    @pl.when(late)
    def _():
        exchange(arrays[3:])

    @pl.loop(0, near, unroll=4)
    def _(b):
        for hh in range(each):
            values = jnp.concatenate(
                [taken[b, :, of_head(kind, hh)] for kind in (K, V)]
                + [jnp.ones((n, DH), BF16)],
                axis=1,
            )
            rows = nn(hits_of(slots[b, hh], pool), values)
            sort_into(acc, hh, b, slice(DH, 3 * DH), rows[:, : 2 * DH])
            sort_into(work, hh, b, one, rows[:, 2 * DH :])

    row = lax.broadcasted_iota(jnp.int32, (members, members), 0)
    col = lax.broadcasted_iota(jnp.int32, (members, members), 1)
    same = (row // part) == (col // part)
    lane = lax.broadcasted_iota(jnp.int32, (members, DH), 1)
    pick = jnp.where(lane == 0, BIG, 0.0).astype(BF16)
    scale = factor * LOG2E

    def attend(group_of, queries, keys, values, allowed, prob_ref):
        scores = [
            jnp.where(allowed, nt(jnp.concatenate([q, pick], axis=1), k), -jnp.inf)
            for q, k in zip(queries, keys)
        ]
        tops = [jnp.max(s, axis=-1, keepdims=True) for s in scores]
        grown = [jnp.exp2((s - top) * scale) for s, top in zip(scores, tops)]
        sums = [jnp.sum(e, axis=-1, keepdims=True) for e in grown]
        weights = [(e * (1.0 / total)).astype(BF16) for e, total in zip(grown, sums)]
        for p, w, v, top, total in zip(group_of, weights, values, tops, sums):
            prob_ref[p] = w
            lse = top * scale + jnp.log(total) * LOG2E
            out = jnp.concatenate([nn(w, v), at_lanes((members, DH), in_parts(lse, 3))], axis=1)
            work[p] = out.reshape(2, part, 2 * DH)

    @pl.loop(0, rows16.shape[0], unroll=4)
    def _(p):
        for i, at in ((1, 1), (2, 3)):
            rows = whole(acc, p, slice(i * DH, (i + 1) * DH))
            rows16[p, :, at * DH : (at + 1) * DH] = rows.astype(BF16)
        rows16[p, :, 2 * DH : 3 * DH] = (whole(work, p, one) - 1.0).astype(BF16)

    def by_tokens(hh, b, slot_index):
        rows = sorted_rows(work, hh, b, two)
        return nn(hits_by_token(slots[slot_index, hh], pool), rows)

    @pl.when(early)
    def _():
        for hh in range(each):

            @pl.loop(0, near)
            def _(b):
                got(QX, x_in.at[b, :, hh * DH : (hh + 1) * DH], hh * near + b)

            @pl.loop(0, near, unroll=4)
            def _(b):
                view = x_in[b, :, hh * DH : (hh + 1) * DH]
                sort_into(work, hh, b, one, nn(hits_of(slots[near + b, hh], pool), view))

            @pl.loop(0, pairs // group)
            def _(g):
                group_of = [hh * pairs + g * group + i for i in range(group)]
                queries = [whole(work, p, one).astype(BF16) for p in group_of]
                for p, q in zip(group_of, queries):
                    xq16[p] = q
                keys = [rows16[p, :, DH : 3 * DH] for p in group_of]
                values = [rows16[p, :, 3 * DH :] for p in group_of]
                attend(group_of, queries, keys, values, same, probs_x)

            @pl.loop(0, near, unroll=4)
            def _(b):
                back = by_tokens(hh, b, near + b)
                at = hh * near + b
                view = x_out.at[b, :, hh * DH : (hh + 1) * DH]
                view[...] = back[:, :DH].astype(BF16)
                lse_out[at] = back[:, DH:].T[:8]
                dst = x_in.at[b, :, hh * DH : (hh + 1) * DH]
                remote(OX, view, dst, at, at, me + near).start()
                remote(LX, lse_out.at[at], lse_in.at[at], at, at, me + near).start()

    @pl.when(early)
    def _():
        @pl.loop(0, near)
        def _(b):
            got(Q, into(Q, b), b)

    @pl.loop(0, near, unroll=4)
    def _(b):
        for hh in range(each):
            view = taken[b, :, of_head(Q, hh)]
            sort_into(acc, hh, b, one, nn(hits_of(slots[b, hh], pool), view))

    @pl.loop(0, rows16.shape[0] // group)
    def _(g):
        group_of = [g * group + i for i in range(group)]
        queries = [whole(acc, p, one).astype(BF16) for p in group_of]
        for p, q in zip(group_of, queries):
            rows16[p, :, :DH] = q
        keys = [rows16[p, :, DH : 3 * DH] for p in group_of]
        values = [rows16[p, :, 3 * DH :] for p in group_of]
        attend(group_of, queries, keys, values, same & (col <= row), probs)

    for j in range(plane - 1):

        @pl.when(relays & ~middle & (spot == j))
        def _():
            for i in range(2):
                pltpu.make_async_copy(relay.at[i], relay.at[i], relay_sem.at[i]).wait()
                pass_on(i, j).start()

    @pl.loop(0, near, unroll=4)
    def _(b):
        for hh in range(each):
            back = by_tokens(hh, b, b)
            attn_own[b, :, hh * DH : (hh + 1) * DH] = back[:, :DH].astype(BF16)
            lse_own[hh * near + b] = back[:, DH:].T[:8]

    for load in loads:
        load.wait()

    pair[0] = jnp.zeros((8, n), F32)

    for j in range(4):

        @pl.when(me > 0)
        def _():
            for i in range(2):
                view = rim.at[i, :, span[j]]
                pltpu.make_async_copy(view, view, rim_recv.at[i, j]).wait()

        @pl.when(me == 0)
        def _():
            rim[:, :, span[j]] = jnp.zeros((2, n, quarter), BF16)

        @pl.loop(j * (heads // 4), (j + 1) * (heads // 4))
        def _(h):
            cols = columns(h, 1)
            keys = jnp.concatenate([rim[0, :, cols], wk_v[:, cols]], axis=0)
            vals = jnp.concatenate([rim[1, :, cols], wv_v[:, cols]], axis=0)
            prob = window_prob(factor, wq_v[:, cols], keys)
            attn = nn(prob.astype(BF16), vals).astype(BF16)
            attn_win[:, cols] = attn
            gained = wg_v[:, cols].astype(F32) * w_gain[:, cols]
            pair[0] += stat_rows(attn.astype(F32), gained)

    which = lax.broadcasted_iota(jnp.int32, (8, n), 0)

    def gained_of(b, hh):
        gain = c_gain[:, columns(t * each + hh, 1)]
        return taken[b, :, of_head(G, hh)].astype(F32) * gain

    def finish(b, merge):
        total = jnp.zeros((8, n), F32)
        for hh in range(each):
            at = hh * near + b
            lanes = slice(hh * DH, (hh + 1) * DH)
            if merge:
                mine = jnp.sum(lse_own[at][0:3], axis=0, keepdims=True)
                other = jnp.sum(lse_in[at][0:3], axis=0, keepdims=True)
                top = jnp.maximum(mine, other)
                mine, other = jnp.exp2(mine - top), jnp.exp2(other - top)
                share = jnp.where(which == 0, mine, other) / (mine + other)
                shares[at] = share
                by_token = share.T
                attn = by_token[:, 0:1] * attn_own[b, :, lanes].astype(F32)
                attn = attn + by_token[:, 1:2] * x_in[b, :, lanes].astype(F32)
                attn_own[b, :, lanes] = attn.astype(BF16)
            else:
                shares[at] = jnp.where(which == 0, 1.0, 0.0)
        for hh in range(each):
            attn = attn_own[b, :, hh * DH : (hh + 1) * DH].astype(F32)
            total = total + stat_rows(attn, gained_of(b, hh))
        part_out[b] = total
        deliver(PART, part_out.at[b], part_in.at[t], b, b, t)
        deliver(ATTN, attn_own.at[b], attn_home.at[:, columns(t * each, each)], b, b, t)

    for this_half, merge in ((early, False), (late, True)):

        @pl.when(this_half)
        def _():
            @pl.loop(0, near)
            def _(b):
                got(G, into(G, b), b)
                if merge:
                    for hh in range(each):
                        at = hh * near + b
                        got(OX, x_in.at[b, :, hh * DH : (hh + 1) * DH], at)
                        got(LX, lse_in.at[at], at)

            @pl.loop(0, near, unroll=2)
            def _(d):
                finish(peer(d + 1), merge)

    @pl.loop(0, near)
    def _(b):
        got(PART, part_in.at[b], b)
        pair[0] += part_in[b]

    swap = pltpu.make_async_remote_copy(
        src_ref=pair.at[0],
        dst_ref=pair.at[1],
        send_sem=pair_sem.at[0],
        recv_sem=pair_sem.at[1],
        device_id=(me, 1 - core),
        device_id_type=MESH,
    )
    swap.start()
    swap.wait()
    totals = pair[0] + pair[1]
    inv = 1.0 / jnp.sqrt(totals[0:1] / feat_width + EPSILON)
    coef = inv * inv * inv * totals[1:2] / feat_width
    stat_own[...] = jnp.where(which == 0, inv, coef)

    @pl.loop(0, near)
    def _(d):
        b = peer(d + 1)
        deliver(STAT, stat_own, stats.at[t], b, b, t)

    def dout_of(hh, b):
        by_token = stats[b].T
        attn = attn_own[b, :, hh * DH : (hh + 1) * DH].astype(F32)
        dout = by_token[:, 0:1] * gained_of(b, hh) - by_token[:, 1:2] * attn
        return dout.astype(BF16).astype(F32), attn

    def visit(hh, b):
        lanes = slice(hh * DH, (hh + 1) * DH)
        at = hh * near + b
        dout, attn = dout_of(hh, b)
        terms = dout * attn
        share = shares[at]
        view = d_out.at[b, :, lanes]
        view[...] = (share.T[:, 1:2] * dout).astype(BF16)
        high = terms.astype(BF16)
        low = (terms - high.astype(F32)).astype(BF16)
        sums = nt(every, high) + nt(every, low)
        first, second = in_parts(sums * share[1:2], 2)
        dot_out[at] = jnp.where(which == 0, first, jnp.where(which == 1, second, 0.0))
        remote(DX, view, d_in.at[b, :, lanes], at, at, me - near).start()
        remote(RX, dot_out.at[at], dot_in.at[at], at, at, me - near).start()

    def spread(hh, b, is_late):
        dout, attn = dout_of(hh, b)
        row_dot = jnp.sum(dout * attn, axis=-1, keepdims=True)
        if is_late:
            share = shares[hh * near + b].T
            dout, row_dot = share[:, 0:1] * dout, share[:, 0:1] * row_dot
        dots = at_lanes((n, DH), in_parts(row_dot, 2)).astype(BF16)
        both = jnp.concatenate([dout.astype(BF16), dots], axis=1)
        sort_into(work, hh, b, two, nn(hits_of(slots[b, hh], pool), both))

    every = jnp.ones((8, DH), BF16)

    def spread_all(is_late):
        @pl.loop(0, near)
        def _(b):
            got(STAT, stats.at[b], b)

        if is_late:
            for hh in range(each):

                @pl.loop(0, near, unroll=4)
                def _(d):
                    visit(hh, peer(d + 1))

        for hh in range(each):

            @pl.loop(0, near, unroll=4)
            def _(d):
                spread(hh, peer(d + 1), is_late)

    @pl.when(late)
    def _():
        spread_all(True)

    @pl.loop(0, near)
    def _(b):
        got(ATTN, attn_home.at[:, columns(b * each, each)], b)

    for j in range(plane - 1):

        @pl.when(relays & (spot == j))
        def _():
            for i in range(2):
                pass_on(i, j).wait_send()

    @pl.when(crosses)
    def _():
        for j in range(4):
            for i in range(2):
                rim_first(i, j, j < plane - 1).wait_send()

    @pl.when(straight)
    def _():
        for j in range(4):
            for i in range(2):
                rim_first(i, j, False).wait_send()

    back_crosses = (spot == 0) & (me > 0)
    back_straight = spot != 0
    back_relays = (spot != 0) & (me >= plane)

    def back_copy(j, src, dst, sem, to):
        return pltpu.make_async_remote_copy(
            src_ref=src,
            dst_ref=dst,
            send_sem=rim_send.at[2, j],
            recv_sem=sem,
            device_id=(to, core),
            device_id_type=MESH,
        )

    def back_first(j, by_relay):
        src = rim.at[:, :, span[j]]
        if by_relay:
            return back_copy(j, src, relay_back, relay_sem.at[2], level * plane + j)
        return back_copy(j, src, rim_back.at[:, :, span[j]], rim_recv.at[2, j], me - 1)

    by_token = stat_own[...].T
    inv_col, coef_col = by_token[:, 0:1], by_token[:, 1:2]
    for j in (1, 2, 3, 0):

        @pl.loop(j * (heads // 4), (j + 1) * (heads // 4))
        def _(h):
            cols = columns(h, 1)
            q = wq_v[:, cols]
            keys = jnp.concatenate([rim[0, :, cols], wk_v[:, cols]], axis=0)
            vals = jnp.concatenate([rim[1, :, cols], wv_v[:, cols]], axis=0)
            attn = attn_win[:, cols].astype(F32)
            gained = wg_v[:, cols].astype(F32) * w_gain[:, cols]
            grad = (inv_col * gained - coef_col * attn).astype(BF16)
            prob = window_prob(factor, q, keys)
            row_dot = jnp.sum(grad.astype(F32) * attn, axis=-1, keepdims=True)
            change = (prob * (nt(grad, vals) - row_dot)).astype(BF16)
            wq_v[:, cols] = (nn(change, keys) * factor).astype(BF16)
            dk = tn(change, q)
            dv = tn(prob.astype(BF16), grad)
            rim[0, :, cols] = dk[:WINDOW].astype(BF16)
            rim[1, :, cols] = dv[:WINDOW].astype(BF16)
            wk_v[:, cols] = dk[WINDOW:].astype(BF16)
            wv_v[:, cols] = dv[WINDOW:].astype(BF16)
            attn_win[:, cols] = (attn * inv_col * w_gain[:, cols]).astype(BF16)
            clu = attn_home[:, cols].astype(F32)
            attn_home[:, cols] = (clu * inv_col * c_gain[:, cols]).astype(BF16)

        @pl.when(back_crosses)
        def _():
            back_first(j, 0 < j < plane).start()

        @pl.when(back_straight)
        def _():
            back_first(j, False).start()

    stores = [
        pltpu.make_async_copy(src, dst, local_sem.at[4 + i])
        for i, (src, dst) in enumerate(
            [
                (attn_win, win_normed),
                (attn_home, clu_normed),
                (wq_v, win_dq),
                (wk_v, win_dk),
                (wv_v, win_dv),
            ]
        )
    ]
    for store in stores[:3]:
        store.start()

    @pl.when(early)
    def _():
        spread_all(False)

    minus = jnp.where(lane < 2, -1.0, 0.0).astype(BF16)

    def changes_of(group_of, prob_ref):
        slopes = []
        for p in group_of:
            v = jnp.concatenate([rows16[p, :, 3 * DH :], minus], axis=1)
            slopes.append(nt(whole(work, p, two).astype(BF16), v))
        return [(prob_ref[p].astype(F32) * s).astype(BF16) for p, s in zip(group_of, slopes)]

    def split_rows(x):
        return x.reshape(2, part, DH)

    second, third = slice(DH, 2 * DH), slice(2 * DH, 3 * DH)

    @pl.loop(0, rows16.shape[0] // group)
    def _(g):
        group_of = [g * group + i for i in range(group)]
        for p, change in zip(group_of, changes_of(group_of, probs)):
            grad = whole(work, p, one).astype(BF16)
            acc[p, :, :, one] = split_rows(nn(change, rows16[p, :, DH : 2 * DH]) * factor)
            acc[p, :, :, second] = split_rows(tn(change, rows16[p, :, :DH]))
            acc[p, :, :, third] = split_rows(tn(probs[p], grad))

    @pl.when(late)
    def _():
        @pl.loop(0, near)
        def _(b):
            for hh in range(each):
                sent(QX, taken.at[b, :, of_head(Q, hh)], hh * near + b)

    homes = [(DQ, clu_dq), (DK, clu_dk), (DV, clu_dv)]

    def home_of(i, hh, owner):
        return homes[i][1].at[:, columns(owner * each + hh, 1)]

    def give(i, hh, b):
        at = hh * near + b
        view = taken.at[b, :, of_head(i, hh)]
        deliver(homes[i][0], view, home_of(i, hh, t), b, at, hh * near + t)

    def keys_home(hh, b, hits):
        rows = sorted_rows(acc, hh, b, slice(DH, 3 * DH))
        back = nn(hits, rows)
        taken[b, :, of_head(1, hh)] = (back[:, :DH] * factor).astype(BF16)
        taken[b, :, of_head(2, hh)] = back[:, DH:].astype(BF16)
        give(1, hh, b)
        give(2, hh, b)

    def own_home(hh, b, is_late):
        hits = hits_by_token(slots[b, hh], pool)
        taken[b, :, of_head(0, hh)] = nn(hits, sorted_rows(acc, hh, b, one)).astype(BF16)
        keys_home(hh, b, hits)
        if not is_late:
            give(0, hh, b)

    @pl.when(late)
    def _():
        for hh in range(each):

            @pl.loop(0, near, unroll=2)
            def _(d):
                own_home(hh, peer(d + 1), True)

    def pass_back(j):
        dst = rim_back.at[:, :, span[j]]
        return pltpu.make_async_remote_copy(
            src_ref=relay_back,
            dst_ref=dst,
            send_sem=relay_sem.at[3],
            recv_sem=rim_recv.at[2, j],
            device_id=(level * plane - 1, core),
            device_id_type=MESH,
        )

    for j in range(1, plane):

        @pl.when(back_relays & (spot == j))
        def _():
            pltpu.make_async_copy(relay_back, relay_back, relay_sem.at[2]).wait()
            pass_back(j).start()

    @pl.when(early)
    def _():
        for hh in range(each):
            lanes = slice(hh * DH, (hh + 1) * DH)

            @pl.loop(0, near)
            def _(b):
                at = hh * near + b
                got(DX, d_in.at[b, :, lanes], at)
                got(RX, dot_in.at[at], at)
                sent(OX, x_out.at[b, :, lanes], at)

            @pl.loop(0, near, unroll=4)
            def _(b):
                at = hh * near + b
                dots = jnp.concatenate(
                    [dot_in[at].T, jnp.zeros((n, DH - 8), F32)], axis=1
                ).astype(BF16)
                both = jnp.concatenate([d_in[b, :, lanes], dots], axis=1)
                sort_into(work, hh, b, two, nn(hits_of(slots[near + b, hh], pool), both))

            @pl.loop(0, pairs // group)
            def _(g):
                group_of = [hh * pairs + g * group + i for i in range(group)]
                for p, change in zip(group_of, changes_of(group_of, probs_x)):
                    grad = whole(work, p, one).astype(BF16)
                    acc[p, :, :, second] += split_rows(tn(change, xq16[p]))
                    acc[p, :, :, third] += split_rows(tn(probs_x[p], grad))
                    dq = nn(change, rows16[p, :, DH : 2 * DH]) * factor
                    work[p, :, :, one] = split_rows(dq)

            @pl.loop(0, near, unroll=2)
            def _(d):
                b = peer(d + 1)
                at = hh * near + b
                hits = hits_by_token(slots[near + b, hh], pool)
                view = x_out.at[b, :, lanes]
                view[...] = nn(hits, sorted_rows(work, hh, b, one)).astype(BF16)
                remote(DQX, view, d_in.at[b, :, lanes], at, at, me + near).start()

        for hh in range(each):

            @pl.loop(0, near, unroll=2)
            def _(d):
                own_home(hh, peer(d + 1), False)

    @pl.when(late)
    def _():
        for hh in range(each):
            lanes = slice(hh * DH, (hh + 1) * DH)

            @pl.loop(0, near)
            def _(d):
                b = peer(d + 1)
                got(DQX, d_in.at[b, :, lanes], hh * near + b)
                more = d_in[b, :, lanes].astype(F32)
                view = taken.at[b, :, of_head(0, hh)]
                view[...] = (view[...].astype(F32) + more).astype(BF16)
                give(0, hh, b)

    @pl.when(me < n_seq - 1)
    def _():
        for j in range(4):
            view = rim_back.at[:, :, span[j]]
            pltpu.make_async_copy(view, view, rim_recv.at[2, j]).wait()

    @pl.when(me == n_seq - 1)
    def _():
        rim_back[...] = jnp.zeros_like(rim_back)

    @pl.loop(0, heads)
    def _(h):
        cols = columns(h, 1)
        dk = wk_v[:, cols].astype(F32) + rim_back[0, :, cols].astype(F32)
        wk_v[:, cols] = (dk * factor).astype(BF16)
        dv = wv_v[:, cols].astype(F32) + rim_back[1, :, cols].astype(F32)
        wv_v[:, cols] = dv.astype(BF16)

    for store in stores[3:]:
        store.start()

    for j in range(4):

        @pl.when(back_crosses)
        def _():
            back_first(j, 0 < j < plane).wait_send()

        @pl.when(back_straight)
        def _():
            back_first(j, False).wait_send()

    for j in range(1, plane):

        @pl.when(back_relays & (spot == j))
        def _():
            pass_back(j).wait_send()

    @pl.loop(1, near)
    def _(d):
        to = peer(d)
        for kind, src in arrays:
            sent(kind, src.at[:, columns(to * each, each)], to)
        sent(IDS, ids.at[pl.ds(to * each, each)], to)
        sent(PART, part_out.at[to], to)
        sent(ATTN, attn_own.at[to], to)
        sent(STAT, stat_own, to)
        for hh in range(each):
            for i, (kind, home) in enumerate(homes):
                sent(kind, taken.at[to, :, of_head(i, hh)], hh * near + to)

    @pl.loop(0, near)
    def _(b):
        for hh in range(each):
            for i, (kind, home) in enumerate(homes):
                got(kind, home_of(i, hh, b), hh * near + b)

    @pl.when(late)
    def _():
        @pl.loop(0, near)
        def _(b):
            sent(IDSX, ids.at[pl.ds(b * each, each)], b)
            for hh in range(each):
                at = hh * near + b
                sent(DX, d_out.at[b, :, hh * DH : (hh + 1) * DH], at)
                sent(RX, dot_out.at[at], at)

    @pl.when(early)
    def _():
        @pl.loop(0, near)
        def _(b):
            for hh in range(each):
                at = hh * near + b
                sent(LX, lse_out.at[at], at)
                sent(DQX, x_out.at[b, :, hh * DH : (hh + 1) * DH], at)

    for store in stores:
        store.wait()


def copy_kernel(*refs):
    count = len(refs) // 2
    for src, dst in zip(refs[:count], refs[count:]):
        dst[...] = src[...]


def settle(arrays):
    n, wide = arrays[0].shape
    block = pl.BlockSpec((n // 8, wide), lambda i: (i, 0))
    return pl.pallas_call(
        copy_kernel,
        grid=(8,),
        in_specs=[block] * len(arrays),
        out_specs=[block] * len(arrays),
        out_shape=[jax.ShapeDtypeStruct((n, wide), BF16)] * len(arrays),
        compiler_params=pltpu.CompilerParams(vmem_limit_bytes=32 << 20),
    )(*arrays)


def layer(*arrays):
    win_query, cluster_ids = arrays[0], arrays[6]
    n, wide = win_query.shape
    sources = lax.axis_size("seq")
    near = sources // 2
    cap = SLOTS // sources
    clusters = sources * (2 * n // SLOTS)
    part = near * cap
    heads = wide // DH
    each = heads // near
    pairs = each * clusters // 2
    given = list(arrays)
    given[6] = cluster_ids[:, None, :]
    given[7], given[8] = arrays[7][None, :], arrays[8][None, :]
    anywhere = pl.BlockSpec(memory_space=pl.ANY)
    vmem = pl.BlockSpec(memory_space=pltpu.VMEM)
    group = next(g for g in (16, 8, 4, 2, 1) if clusters // 2 % g == 0)
    rows_of = pltpu.VMEM((each * near, 8, n), F32)
    results = pl.pallas_call(
        functools.partial(layer_kernel, DH ** (-0.5), cap, group, 4),
        in_specs=[anywhere] * 6 + [vmem] * 3 + [anywhere] * 2,
        out_specs=[anywhere] * 8,
        out_shape=[jax.ShapeDtypeStruct((n, wide), BF16)] * 8,
        scratch_shapes=[
            pltpu.VMEM((near, n, 4 * each * DH), BF16),
            pltpu.VMEM((sources, each, 1, n), jnp.int32),
            pltpu.VMEM((sources, each, 1, n), jnp.int32),
        ]
        + [pltpu.VMEM((n, wide), BF16)] * 4
        + [pltpu.VMEM((2, n, wide), BF16)] * 2
        + [pltpu.VMEM((2, n, wide // 4), BF16)] * 2
        + [pltpu.VMEM((n, wide), BF16)] * 2
        + [pltpu.VMEM((near, n, each * DH), BF16)] * 5
        + [
            pltpu.VMEM((pairs, 2 * part, 4 * DH), BF16),
            pltpu.VMEM((pairs, 2 * part, DH), BF16),
            pltpu.VMEM((pairs, 2, part, 2 * DH), F32),
            pltpu.VMEM((pairs, 2, part, 3 * DH), F32),
            pltpu.VMEM((pairs, 2 * part, 2 * part), BF16),
            pltpu.VMEM((pairs, 2 * part, 2 * part), BF16),
        ]
        + [rows_of] * 6
        + [
            pltpu.VMEM((near, 8, n), F32),
            pltpu.VMEM((near, 8, n), F32),
            pltpu.VMEM((2, 8, n), F32),
            pltpu.VMEM((8, n), F32),
            pltpu.VMEM((near, 8, n), F32),
            pltpu.SemaphoreType.DMA((18, sources)),
            pltpu.SemaphoreType.DMA((18, sources)),
            pltpu.SemaphoreType.DMA((3, 4)),
            pltpu.SemaphoreType.DMA((3, 4)),
            pltpu.SemaphoreType.DMA((6,)),
            pltpu.SemaphoreType.DMA((2,)),
            pltpu.SemaphoreType.DMA((9,)),
        ],
        cost_estimate=pl.CostEstimate(
            flops=14 * n * 2 * n * wide, bytes_accessed=16 * n * wide * 2, transcendentals=0
        ),
        compiler_params=pltpu.CompilerParams(
            vmem_limit_bytes=60 << 20, collective_id=0, has_side_effects=True
        ),
    )(*given)
    return settle(results)


def solution(mesh):
    sources, split = mesh.shape["seq"], mesh.shape["head"]
    whole_heads = HC // split == sources and SLOTS // sources % 8 == 0 and split == 2 and sources % 4 == 0
    return jax.shard_map(
        layer if whole_heads else body,
        mesh=mesh,
        in_specs=(P("seq", "head"),) * 6
        + (P("head", "seq"), P("head"), P("head"))
        + (P("seq", "head"),) * 2,
        out_specs=(P("seq", "head"),) * 8,
        check_vma=False,
    )
```
